32 devices in a mesh: parts: 2 (over y), sub: 4 (over z), row: 2 (over x), col: 2 (over core).
Axes of the slice: x: 2, y: 2, z: 4, core: 2. Of those that a mesh axis runs over, the one named last changes fastest.
Arguments:
- loads: float32 [8, 32, 1024], P(('parts', 'sub'), 'col'), parts along dimension 0, may hold values from -6 to 6
- weights: float32 [8, 1024], P(('parts', 'sub')), parts along dimension 0, may hold values from 0.25 to 4
- dual_ops: bfloat16 [8, 2048, 2048], P(('parts', 'sub'), 'row'), parts along dimension 0, as said below
- corner_maps: bfloat16 [8, 24, 2048], P(('parts', 'sub'), None, 'row'), parts along dimension 0, may hold values from -0.25 to 0.25
- coarse_inverse: float32 [96, 48], P('parts'), parts along dimension 0, as said below
- corner_ids: int32 [8, 24], P('parts'), parts along dimension 0, may hold values from 0 to 47, as said below
- iface_sizes: int32 [8], P('parts'), parts along dimension 0, may hold values from 512 to 1024, as said below
- left_partner: int32 [8, 1024], P(('parts', 'sub')), parts along dimension 0, may hold values from 0 to 1023, as said below
- right_partner: int32 [8, 1024], P(('parts', 'sub')), parts along dimension 0, may hold values from 0 to 1023, as said below
Outputs:
- solution: float32 [8, 32, 1024], P(('parts', 'sub'), 'col'), parts along dimension 0
- residual: float32 [8, 32, 1024], P(('parts', 'sub'), 'col'), parts along dimension 0
The draws below stay inside these ranges and needn't reach their ends.
There are 2 independent parts, one for each index of `parts`. The reference program is written for one: setup_inputs(seed, part) draws one part's arguments, and reference() takes and returns one part's arrays. A program takes and returns all parts, laid end to end along the dimension named above; each array names one. Nothing has to cross between parts.
Inputs may be any that keep to these rules, and one draw needn't show every extreme that they name: Global indices 24/2 * s to 24/2 * s + 24/2 - 1 are the corners of the interface between s and s+1; the first half of subdomain s's corner_ids is a permutation of those of interface s-1, the second half a permutation of those of interface s. `left_partner`: each row s is a permutation that maps the slots below iface_sizes[s-1] onto slots below it. `right_partner`: each row s is a permutation that maps the slots below iface_sizes[s] onto slots below it, and is the inverse of left_partner[s+1]. `dual_ops`: symmetric positive definite. `coarse_inverse`: symmetric positive definite. For each s < 2, one of iface_sizes[s] and iface_sizes[s + 2] is 896 or more and the other 640 or less.
All inputs are finite; a program needn't handle non-finite values.
Results may differ from the reference program's by a relative error of at most 0.015.
Values may be sent and summed in bfloat16 or wider, within the bound.
No kernel may reach another device: no remote copies, remote signals or barrier semaphores. Data moves between devices by JAX's collectives and lax.ppermute only.
A program may use at most 64 MiB of HBM per device.

```python
import math
import jax
import jax.numpy as jnp
from jax import lax

ORDER = 2048
COLS = 32
C_LOC = 24
ITERS = 2
S = 4
HALF = 1024
NC = 48


def draw_dual_ops(key, part):

    def one_matrix(sub_key):
        first, second = jax.random.split(sub_key)
        noise = jax.random.normal(first, (ORDER, ORDER), jnp.float32)
        spread = 0.35
        diagonal = jax.random.uniform(second, (ORDER,), jnp.float32, 1.0, 3.0)
        symmetric = (noise + noise.T) * (spread / (2.0 * ORDER) ** 0.5)
        return (symmetric + jnp.diag(diagonal)).astype(jnp.bfloat16)
    return lax.map(one_matrix, jax.random.split(key, S))


def draw_coarse_inverse(key, part):
    first, second = jax.random.split(jax.random.fold_in(key, 3))
    noise = jax.random.normal(first, (NC, NC), jnp.float32)
    spread = 0.5
    diagonal = jax.random.uniform(second, (NC,), jnp.float32, 1.5, 3.0)
    symmetric = (noise + noise.T) * (spread / (2.0 * NC) ** 0.5)
    return symmetric + jnp.diag(diagonal)


def draw_corner_ids(key, part):
    width = C_LOC // 2
    keys = jax.random.split(jax.random.fold_in(key, 5), 2 * S)
    orders = jax.vmap(lambda one_key: jax.random.permutation(one_key, width))(keys).astype(jnp.int32)
    subdomains = jnp.arange(S, dtype=jnp.int32)
    before = width * ((subdomains + S - 1) % S)[:, None] + orders[:S]
    after = width * subdomains[:, None] + orders[S:]
    return jnp.concatenate([before, after], axis=1).astype(jnp.int32)


def interface_sizes(key):
    first, second, third = jax.random.split(jax.random.fold_in(key, 11), 3)
    pairs = S // 2
    light = jax.random.randint(first, (pairs,), HALF // 2, 5 * HALF // 8 + 1, dtype=jnp.int32)
    heavy = jax.random.randint(second, (pairs,), 7 * HALF // 8, HALF + 1, dtype=jnp.int32)
    flip = jax.random.randint(third, (pairs,), 0, 2, dtype=jnp.int32)
    lower = jnp.where(flip == 1, heavy, light)
    upper = jnp.where(flip == 1, light, heavy)
    return jnp.concatenate([lower, upper]).astype(jnp.int32)


def draw_iface_sizes(key, part):
    return interface_sizes(key)


def interface_orders(key):
    sizes = interface_sizes(key)
    keys = jax.random.split(jax.random.fold_in(key, 7), S)
    slots = jnp.arange(HALF, dtype=jnp.int32)

    def one_order(one_key, count):
        ranks = jax.random.permutation(one_key, HALF).astype(jnp.int32)
        scores = ranks + HALF * (slots >= count).astype(jnp.int32)
        return jnp.argsort(scores, stable=True).astype(jnp.int32)
    return jax.vmap(one_order)(keys, sizes).astype(jnp.int32)


def draw_left_partner(key, part):
    return jnp.roll(interface_orders(key), 1, axis=0).astype(jnp.int32)


def draw_right_partner(key, part):
    return jnp.argsort(interface_orders(key), axis=1, stable=True).astype(jnp.int32)


def block_scale(key, extent, shards, least, largest):
    level, own = 1.0, jax.random.fold_in(key, 6)
    for dim, blocks in shards:
        steps = jnp.exp(jax.random.uniform(jax.random.fold_in(own, dim), (blocks,), jnp.float32, least / len(shards), largest / len(shards)))
        level = level * jnp.repeat(steps, extent[dim] // blocks).reshape([-1 if axis == dim else 1 for axis in range(len(extent))])
    return level


def centred(stream_key, dims, scale, reach, cuts=(), kind=jnp.bfloat16):
    level = block_scale(stream_key, dims, cuts, -0.22, 0.18) if cuts else 1.0
    entries = jax.random.normal(stream_key, dims, jnp.float32) * scale * level
    return jnp.minimum(jnp.maximum(entries, -reach), reach).astype(kind)


def setup_inputs(seed: int = 0, part: int = 0) -> dict:
    key_of = jax.random.split(jax.random.key(seed), 10)
    part_keys = jax.random.split(jax.random.fold_in(key_of[9], part), 10)
    return {
        "loads": centred(part_keys[0], (S, COLS, HALF), 1.0, 6.0, ((0, 4), (1, 2)), jnp.float32),
        "weights": jnp.clip(jnp.exp(math.log(4.0) - 2.7725887 * jax.random.uniform(part_keys[1], (S, HALF), jnp.float32) ** block_scale(part_keys[1], (S, HALF), ((0, 4),), -0.2, 0.2)), 0.25, 4.0),
        "dual_ops": draw_dual_ops(jax.random.fold_in(jax.random.fold_in(key_of[9], part), 71), part),
        "corner_maps": centred(part_keys[3], (S, C_LOC, ORDER), (ORDER // 4) ** -0.5, 0.25, ((0, 4), (2, 2))),
        "coarse_inverse": draw_coarse_inverse(jax.random.fold_in(jax.random.fold_in(key_of[9], part), 71), part),
        "corner_ids": draw_corner_ids(jax.random.fold_in(jax.random.fold_in(key_of[9], part), 71), part),
        "iface_sizes": draw_iface_sizes(jax.random.fold_in(jax.random.fold_in(key_of[9], part), 71), part),
        "left_partner": draw_left_partner(jax.random.fold_in(jax.random.fold_in(key_of[9], part), 71), part),
        "right_partner": draw_right_partner(jax.random.fold_in(jax.random.fold_in(key_of[9], part), 71), part),
    }


def apply_operator(vec, dual_ops, corner_maps, coarse_inverse, corner_ids, left_partner, right_partner, live):
    ahead = jnp.roll(vec, -1, axis=0)
    right_index = jnp.broadcast_to(right_partner[:, None, :], vec.shape)
    right_side = jnp.take_along_axis(ahead, right_index, axis=2)
    full = jnp.concatenate([vec, right_side], axis=2).astype(jnp.bfloat16)

    def one_local(items):
        piece, matrix, coupling = items
        local = jnp.dot(piece, matrix, preferred_element_type=jnp.float32)
        corner = jnp.dot(piece, coupling.T, preferred_element_type=jnp.float32)
        return local, corner

    local, corner = lax.map(one_local, (full, dual_ops, corner_maps))
    columns = jnp.arange(NC, dtype=jnp.int32)
    onehot = (corner_ids[:, :, None] == columns[None, None, :]).astype(jnp.float32)
    coarse = jnp.einsum("scj,sjn->cn", corner, onehot, precision=lax.Precision.HIGHEST)
    solved = jnp.dot(coarse, coarse_inverse, precision=lax.Precision.HIGHEST)
    back = jnp.einsum("cn,sjn->scj", solved, onehot, precision=lax.Precision.HIGHEST).astype(jnp.bfloat16)

    def one_back(items):
        piece, coupling = items
        return jnp.dot(piece, coupling, preferred_element_type=jnp.float32)

    united = local + lax.map(one_back, (back, corner_maps))
    upper = jnp.roll(united[:, :, HALF:], 1, axis=0)
    left_index = jnp.broadcast_to(left_partner[:, None, :], vec.shape)
    return (united[:, :, :HALF] + jnp.take_along_axis(upper, left_index, axis=2)) * live[:, None, :]


def reference(loads, weights, dual_ops, corner_maps, coarse_inverse, corner_ids, iface_sizes, left_partner, right_partner):
    slots = jnp.arange(HALF, dtype=jnp.int32)
    live = (slots[None, :] < jnp.roll(iface_sizes, 1)[:, None]).astype(jnp.float32)
    scaling = weights[:, None, :]
    residual = loads * live[:, None, :]
    solution = jnp.zeros_like(residual)
    precond = scaling * residual
    direction = precond
    rz_value = jnp.sum(residual * precond, axis=(0, 2))
    for step in range(ITERS):
        image = apply_operator(direction, dual_ops, corner_maps, coarse_inverse, corner_ids, left_partner, right_partner, live)
        alpha = rz_value / jnp.sum(direction * image, axis=(0, 2))
        solution = solution + alpha[None, :, None] * direction
        residual = residual - alpha[None, :, None] * image
        precond = scaling * residual
        new_value = jnp.sum(residual * precond, axis=(0, 2))
        direction = precond + (new_value / rz_value)[None, :, None] * direction
        rz_value = new_value
    return solution, residual
```

```python
import jax
import jax.numpy as jnp
from jax import lax
from jax.experimental import pallas as pl
from jax.experimental.pallas import tpu as pltpu
from jax.sharding import PartitionSpec as P

TILE = 128
LANES = 128
ITERS = 2
F32 = jnp.float32
BF16 = jnp.bfloat16
HIGH = lax.Precision.HIGHEST
VMEM = pl.BlockSpec(memory_space=pltpu.VMEM)
SMEM = pl.BlockSpec(memory_space=pltpu.SMEM)


def shifted(value, axis, steps):
    count = lax.axis_size(axis)
    pairs = [(source, (source + steps) % count) for source in range(count)]
    return lax.ppermute(value, axis, pairs)


def inner(first, second, half):
    return jnp.sum(first[:, :half] * second[:, :half], axis=1)


def paired_totals(residual, precond, image, half):
    return lax.psum((inner(residual, precond, half), inner(precond, image, half)), "sub")


def tile_products(vector, rows_op, first_tile, last_tile, output):

    def one_tile(tile_at, acc):
        piece = lax.dynamic_slice_in_dim(rows_op, tile_at * TILE, TILE, 0)
        product = lax.dot_general(
            vector, piece, (((1,), (1,)), ((), ())), preferred_element_type=jnp.float32
        )
        return lax.dynamic_update_slice_in_dim(acc, product, tile_at * TILE, 1)

    return lax.fori_loop(first_tile, last_tile, one_tile, output)


def live_tiles(size_before, size_after, block_start, block, half):
    left_live = jnp.clip(size_before - block_start, 0, block)
    right_live = jnp.clip(size_after - (block_start - half), 0, block)
    live_cols = jnp.where(block_start < half, left_live, right_live)
    return (live_cols + TILE - 1) // TILE


def general(
    loads,
    weights,
    dual_ops,
    corner_maps,
    coarse_inverse,
    corner_ids,
    iface_sizes,
    left_partner,
    right_partner,
):
    half = loads.shape[2]
    block = dual_ops.shape[1]
    width = coarse_inverse.shape[0]
    subdomain = lax.axis_index("sub")
    count = lax.axis_size("sub")
    row_index = lax.axis_index("row")
    left_map = left_partner[0]
    right_map = right_partner[0]
    slots = jnp.arange(half, dtype=jnp.int32)
    size_before = iface_sizes[(subdomain + count - 1) % count]
    size_after = iface_sizes[subdomain]
    live_left = (slots < size_before).astype(jnp.float32)
    live_right = (right_map < size_after).astype(jnp.float32)
    columns = jnp.arange(width, dtype=jnp.int32)
    own_hot = (corner_ids[subdomain][:, None] == columns[None, :]).astype(jnp.float32)
    operator = dual_ops[0]
    coupling = corner_maps[0]
    block_start = row_index * block
    own_tiles = live_tiles(size_before, size_after, block_start, block, half)

    def apply_operator(vec):
        halfway = vec.astype(jnp.bfloat16)
        empty = jnp.zeros((halfway.shape[0], block), jnp.float32)
        local = tile_products(halfway, operator, jnp.int32(0), own_tiles, empty)
        own_slots = lax.dynamic_slice_in_dim(halfway, row_index * block, block, 1)
        corner = lax.dot_general(
            own_slots, coupling, (((1,), (1,)), ((), ())), preferred_element_type=jnp.float32
        )
        scattered = jnp.dot(corner, own_hot, precision=lax.Precision.HIGHEST)
        coarse = lax.psum(scattered, ("sub", "row"))
        solved = jnp.dot(coarse, coarse_inverse, precision=lax.Precision.HIGHEST)
        back = lax.dot_general(
            solved, own_hot, (((1,), (1,)), ((), ())), precision=lax.Precision.HIGHEST
        ).astype(jnp.bfloat16)
        united = local + jnp.dot(back, coupling, preferred_element_type=jnp.float32)
        whole = lax.all_gather(united.astype(jnp.bfloat16), "row", axis=1, tiled=True).astype(
            united.dtype
        )
        lower = whole[:, :half]
        upper = whole[:, half:]
        arrived_left = shifted(upper.astype(jnp.bfloat16), "sub", 1).astype(upper.dtype)
        arrived_right = shifted(lower.astype(jnp.bfloat16), "sub", -1).astype(lower.dtype)
        result_left = (lower + jnp.take(arrived_left, left_map, axis=1)) * live_left
        result_right = (upper + jnp.take(arrived_right, right_map, axis=1)) * live_right
        return jnp.concatenate([result_left, result_right], axis=1)

    received = (
        shifted(loads[0].astype(jnp.bfloat16), "sub", -1).astype(jnp.float32),
        shifted(weights.astype(jnp.bfloat16), "sub", -1).astype(weights.dtype),
    )
    right_load = jnp.take(received[0], right_map, axis=1) * live_right
    right_weight = jnp.take(received[1], right_map, axis=1)
    residual = jnp.concatenate([loads[0] * live_left, right_load], axis=1)
    scaling = jnp.concatenate([weights, right_weight], axis=1)
    solution = jnp.zeros_like(residual)
    precond = scaling * residual
    image = apply_operator(precond)
    gamma, delta = paired_totals(residual, precond, image, half)
    alpha = gamma / delta
    direction = precond
    along = image
    for step in range(ITERS):
        solution = solution + alpha[:, None] * direction
        residual = residual - alpha[:, None] * along
        if step + 1 < ITERS:
            precond = scaling * residual
            image = apply_operator(precond)
            gamma_next, delta = paired_totals(residual, precond, image, half)
            ratio = gamma_next / gamma
            alpha = gamma_next / (delta - ratio * gamma_next / alpha)
            direction = precond + ratio[:, None] * direction
            along = image + ratio[:, None] * along
            gamma = gamma_next
    return (solution[:, :half][None], residual[:, :half][None])


def cost(flops, moved):
    return pl.CostEstimate(flops=flops, bytes_accessed=moved, transcendentals=0)


def nt(first, second, precision=None):
    return lax.dot_general(
        first, second, (((1,), (1,)), ((), ())), preferred_element_type=F32, precision=precision
    )


def nn(first, second, precision=None):
    return jnp.dot(first, second, preferred_element_type=F32, precision=precision)


def halves(value):
    high = value.astype(BF16)
    return high, (value - high.astype(F32)).astype(BF16)


def stacked(value):
    return jnp.concatenate(halves(value), axis=0)


def folded(value):
    rows = value.shape[0] // 2
    return value[:rows] + value[rows:]


def thirds(value):
    high = value.astype(BF16)
    rest = value - high.astype(F32)
    middle = rest.astype(BF16)
    return high, middle, (rest - middle.astype(F32)).astype(BF16)


def pieces_sum(ref, rows, half, count):
    total = ref[rows, half : half + LANES].astype(F32)
    for piece in range(1, count):
        at = half + piece * LANES
        total = total + ref[rows, at : at + LANES].astype(F32)
    return total


def hot_rows(ids_ref, subdomain, extent):
    ids = ids_ref[pl.ds(subdomain, 1), :]
    names = lax.broadcasted_iota(jnp.int32, (extent, ids.shape[1]), 0)
    return (names == ids).astype(F32)


def neighbours(sub_ref):
    subdomain = lax.axis_index("sub")
    count = lax.axis_size("sub")
    return lax.rem(subdomain + count - 1, count), subdomain, lax.rem(subdomain + 1, count)


def live_row(sizes_ref, interface, half):
    slots = lax.broadcasted_iota(jnp.int32, (1, half), 1)
    return slots < sizes_ref[interface]


def open_kernel(sizes_ref, loads_ref, weights_ref, maps_ref, first_ref, pack_ref):
    before, _, _ = neighbours(None)
    half = loads_ref.shape[1]
    scale = weights_ref[...]
    loaded = jnp.where(live_row(sizes_ref, before, half), loads_ref[...], 0.0)
    first = loaded * scale
    first_ref[...] = first.astype(BF16)
    high = scale.astype(BF16).astype(F32)
    which = lax.broadcasted_iota(jnp.int32, (8, half), 0)
    spare = jnp.where(which == 0, high, jnp.where(which == 1, scale - high, 0.0))
    pack_ref[...] = jnp.concatenate([first, maps_ref[...].astype(F32), spare], axis=0).astype(BF16)


def select_kernel(right_ref, left_ref, right_hot_ref, left_hot_ref):
    half = right_ref.shape[1]

    def one(at, carry):
        start = pl.multiple_of(at * LANES, LANES)
        names = lax.broadcasted_iota(jnp.int32, (LANES, half), 0) + start
        rows = pl.ds(start, LANES)
        right_hot_ref[rows, :] = (names == right_ref[...]).astype(F32).astype(BF16)
        left_hot_ref[rows, :] = (names == left_ref[...]).astype(F32).astype(BF16)
        return carry

    lax.fori_loop(0, half // LANES, one, 0)


def first_kernel(
    ids_ref,
    operator_ref,
    right_hot_ref,
    left_hot_ref,
    first_ref,
    across_ref,
    pack_ref,
    ahead_ref,
    send_ref,
    pair_ref,
    ordered_ref,
):
    before, subdomain, after = neighbours(None)
    lower = lax.axis_index("row") == 0
    columns, half = first_ref.shape
    corners = ids_ref.shape[1]
    left = first_ref[...]
    right = jnp.where(lower, pack_ref[:columns, :], ahead_ref[...])
    slotted = nn(right, right_hot_ref[...]).astype(BF16)
    local = nt(left, operator_ref[:, :half]) + nt(slotted, operator_ref[:, half:])
    ordered_ref[...] = local.astype(BF16)
    pair_ref[columns:, :half] = pack_ref[columns:, :]

    @pl.when(jnp.logical_not(lower))
    def _():
        ordered_ref[...] = nt(ordered_ref[...], right_hot_ref[...]).astype(BF16)
        pair_ref[columns:, :half] = nn(pack_ref[columns:, :], left_hot_ref[...]).astype(BF16)

    beside = pair_ref[columns : columns + corners, :half]
    one = nt(jnp.where(lower, slotted, left), across_ref[...])
    two = nt(jnp.where(lower, right, left), beside)
    coarse = nt(one, hot_rows(ids_ref, subdomain, LANES), HIGH) + nt(
        two, hot_rows(ids_ref, jnp.where(lower, after, before), LANES), HIGH
    )
    high, low = halves(coarse)
    send = jnp.concatenate([ordered_ref[...], high, low], axis=1)
    send_ref[...] = send
    pair_ref[:columns, :] = send
    pair_ref[columns:, half:] = jnp.zeros((pair_ref.shape[0] - columns, 2 * LANES), BF16)


def order_kernel(own_ref, across_ref, right_hot_ref, out_ref):
    lower = lax.axis_index("row") == 0
    raw = jnp.where(lower, across_ref[...], own_ref[...])
    out_ref[...] = nt(raw, right_hot_ref[...]).astype(BF16)


def second_kernel(
    sizes_ref,
    ids_ref,
    inverse_ref,
    operator_ref,
    right_hot_ref,
    loads_ref,
    weights_ref,
    own_map_ref,
    across_ref,
    ordered_map_ref,
    pack_ref,
    send_ref,
    kept_ref,
    pair_ref,
    along_ref,
    slant_ref,
    image_ref,
    next_ref,
    up_ref,
    small_ref,
    ordered_ref,
):
    before, subdomain, after = neighbours(None)
    lower = lax.axis_index("row") == 0
    columns, half = loads_ref.shape
    corners = ids_ref.shape[1]
    width = inverse_ref.shape[0]
    everyone = slice(0, columns)
    top = slice(0, half)
    own, other = send_ref[:, top].astype(F32), pair_ref[everyone, top].astype(F32)
    along, slant = along_ref[:, top].astype(F32), slant_ref[:, top].astype(F32)
    own_c = pieces_sum(send_ref, everyone, half, 2)
    other_c = pieces_sum(pair_ref, everyone, half, 2)
    along_c = pieces_sum(along_ref, everyone, half, 2)
    slant_c = pieces_sum(slant_ref, everyone, half, 2)
    coarse = (jnp.where(lower, own_c, other_c) + jnp.where(lower, other_c, own_c)) + (
        jnp.where(lower, along_c, slant_c) + jnp.where(lower, slant_c, along_c)
    )
    solved = nn(coarse[:, :width], inverse_ref[...], HIGH)
    hot_own = hot_rows(ids_ref, subdomain, width)
    hot_after = hot_rows(ids_ref, after, width)
    hot_before = hot_rows(ids_ref, before, width)
    back_own = nn(solved, hot_own, HIGH).astype(BF16)
    back_after = nn(solved, hot_after, HIGH).astype(BF16)
    back_before = nn(solved, hot_before, HIGH).astype(BF16)
    maps = slice(columns, columns + corners)
    kept, relayed = kept_ref[maps, top], pair_ref[maps, top]
    left_map = jnp.where(lower, own_map_ref[...], across_ref[...])
    map_after = jnp.where(lower, kept, relayed)
    map_before = jnp.where(lower, relayed, kept)
    fix_left = nn(back_own, left_map) + nn(back_before, map_before)
    fix_right = nn(back_own, ordered_map_ref[...]) + nn(back_after, map_after)
    live_left = live_row(sizes_ref, before, half)
    live_right = live_row(sizes_ref, subdomain, half)
    image = jnp.where(lower, own, other) + jnp.where(lower, slant, along) + fix_left
    image = jnp.where(live_left, image, 0.0)
    image_right = jnp.where(lower, other, own) + jnp.where(lower, along, slant) + fix_right
    image_right = jnp.where(live_right, image_right, 0.0)
    scale = weights_ref[...]
    spare = columns + corners
    scales = jnp.where(
        lower,
        pack_ref[spare : spare + 8, :].astype(F32),
        pair_ref[spare : spare + 8, top].astype(F32),
    )
    left = scale * image
    right = (scales[0:1] + scales[1:2]) * image_right
    image_ref[...] = image
    next_ref[...] = left
    left_2, right_2 = stacked(left), stacked(right)
    slotted_2 = nn(right_2, right_hot_ref[...]).astype(BF16)
    local = folded(nt(left_2, operator_ref[:, :half]) + nt(slotted_2, operator_ref[:, half:]))
    block = folded(jnp.where(lower, left_2, slotted_2).astype(F32))
    energy = jnp.sum(block * local, axis=1, keepdims=True)
    ordered_ref[...] = local.astype(BF16)

    @pl.when(jnp.logical_not(lower))
    def _():
        ordered_ref[...] = nt(ordered_ref[...], right_hot_ref[...]).astype(BF16)

    one = folded(nt(jnp.where(lower, slotted_2, left_2), across_ref[...]))
    two = folded(nt(jnp.where(lower, right_2, left_2), kept))
    coarse = nt(one, hot_rows(ids_ref, subdomain, LANES), HIGH) + nt(
        two, hot_rows(ids_ref, jnp.where(lower, after, before), LANES), HIGH
    )
    loaded = jnp.where(live_left, loads_ref[...], 0.0)
    first = loaded * scale
    sums = (
        jnp.sum(loaded * first, axis=1, keepdims=True),
        jnp.sum(first * image, axis=1, keepdims=True),
        jnp.sum(image * left, axis=1, keepdims=True),
        energy,
    )
    lane = lax.broadcasted_iota(jnp.int32, (columns, LANES), 1)
    small = jnp.where(lane < width, coarse, 0.0)
    for at, value in enumerate(sums):
        small = jnp.where(lane == width + at, value, small)
    small_ref[...] = small
    up_ref[...] = jnp.concatenate([ordered_ref[...], *thirds(small)], axis=1)


def relay_kernel(up_own_ref, up_ref, down_ref, far_ref, own_ref, out_ref):
    lower = lax.axis_index("row") == 0
    columns = up_ref.shape[0]
    half = up_ref.shape[1] - 3 * LANES
    total = own_ref[...] + pieces_sum(up_ref, slice(0, columns), half, 3)
    total = total + down_ref[...] + far_ref[...]
    bulk = jnp.where(lower, up_own_ref[:, :half], up_ref[:, :half])
    out_ref[...] = jnp.concatenate([bulk, *thirds(total)], axis=1)


def close_kernel(
    sizes_ref,
    ids_ref,
    inverse_ref,
    loads_ref,
    weights_ref,
    own_map_ref,
    across_ref,
    kept_ref,
    pair_ref,
    image_ref,
    next_ref,
    mine_ref,
    theirs_ref,
    solution_ref,
    residual_ref,
):
    before, subdomain, _ = neighbours(None)
    lower = lax.axis_index("row") == 0
    columns, half = loads_ref.shape
    corners = ids_ref.shape[1]
    width = inverse_ref.shape[0]
    everyone = slice(0, columns)
    top = slice(0, half)
    mine = pieces_sum(mine_ref, everyone, half, 3)
    theirs = pieces_sum(theirs_ref, everyone, half, 3)
    total = jnp.where(lower, mine, theirs)
    rest = jnp.where(lower, theirs, mine)
    coarse = total[:, :width]
    solved = nn(coarse, inverse_ref[...], HIGH)
    back_own = nn(solved, hot_rows(ids_ref, subdomain, width), HIGH).astype(BF16)
    back_before = nn(solved, hot_rows(ids_ref, before, width), HIGH).astype(BF16)
    maps = slice(columns, columns + corners)
    left_map = jnp.where(lower, own_map_ref[...], across_ref[...])
    map_before = jnp.where(lower, pair_ref[maps, top], kept_ref[maps, top])
    fix = nn(back_own, left_map) + nn(back_before, map_before)
    image_next = mine_ref[:, top].astype(F32) + theirs_ref[:, top].astype(F32) + fix
    live = live_row(sizes_ref, before, half)
    image_next = jnp.where(live, image_next, 0.0)
    lane = lax.broadcasted_iota(jnp.int32, (columns, LANES), 1)

    def column(values, at):
        return jnp.sum(jnp.where(lane == width + at, values, 0.0), axis=1, keepdims=True)

    gamma = column(total, 0)
    delta = column(total, 1)
    cross = column(total, 2)
    energy = column(total, 3) + column(rest, 3) + jnp.sum(coarse * solved, axis=1, keepdims=True)
    alpha = gamma / delta
    gamma_next = gamma - 2.0 * alpha * delta + alpha * alpha * cross
    ratio = gamma_next / gamma
    grown = 1.0 + ratio
    curvature = grown * grown * delta - 2.0 * grown * alpha * cross + alpha * alpha * energy
    alpha_next = gamma_next / curvature
    loaded = jnp.where(live, loads_ref[...], 0.0)
    first = loaded * weights_ref[...]
    direction = grown * first - alpha * next_ref[...]
    along = grown * image_ref[...] - alpha * image_next
    solution_ref[...] = alpha * first + alpha_next * direction
    residual_ref[...] = loaded - alpha * image_ref[...] - alpha_next * along


def ring(
    loads,
    weights,
    dual_ops,
    corner_maps,
    coarse_inverse,
    corner_ids,
    iface_sizes,
    left_partner,
    right_partner,
):
    count = lax.axis_size("sub")
    sides = lax.axis_size("row")
    columns, half = loads.shape[1:]
    corners = corner_maps.shape[1]
    operator = dual_ops[0]
    own_map = corner_maps[0]
    loaded = loads[0]
    block = operator.shape[0]
    shape = jax.ShapeDtypeStruct
    grid = ("sub", "row")
    big = 2 * columns * block * 2 * half

    def pairs(target):
        listed = []
        for at in range(count):
            for side in range(sides):
                to_at, to_side = target(at, side)
                listed.append((at * sides + side, (to_at % count) * sides + to_side))
        return listed

    across = pairs(lambda at, side: (at, 1 - side))
    along = pairs(lambda at, side: (at - 1, 0) if side == 0 else (at + 1, 1))
    slant = pairs(lambda at, side: (at - 1, 1) if side == 0 else (at + 1, 0))

    def call(kernel, specs, outs, scratch=(), flops=0, moved=0):
        return pl.pallas_call(
            kernel,
            in_specs=specs,
            out_specs=[VMEM] * len(outs),
            out_shape=outs,
            scratch_shapes=scratch,
            cost_estimate=cost(flops, moved),
        )

    rows = columns + corners + 8
    first, pack = call(
        open_kernel,
        [SMEM, VMEM, VMEM, VMEM],
        [shape((columns, half), BF16), shape((rows, half), BF16)],
        moved=4 * rows * half,
    )(iface_sizes, loaded, weights, own_map)
    other_map = lax.ppermute(own_map, grid, across)
    pack_in = lax.ppermute(pack, grid, along)
    ahead = lax.ppermute(first, grid, slant)
    right_hot, left_hot = call(
        select_kernel,
        [VMEM, VMEM],
        [shape((half, half), BF16), shape((half, half), BF16)],
        flops=4 * half * half,
        moved=4 * half * half,
    )(right_partner, left_partner)
    send, kept = call(
        first_kernel,
        [VMEM] * 8,
        [shape((columns, half + 2 * LANES), BF16), shape((rows, half + 2 * LANES), BF16)],
        scratch=[pltpu.VMEM((columns, block), BF16)],
        flops=2 * big,
        moved=4 * block * half,
    )(corner_ids, operator, right_hot, left_hot, first, other_map, pack_in, ahead)
    pair_in = lax.ppermute(kept, grid, across)
    along_in = lax.ppermute(send, grid, along)
    slant_in = lax.ppermute(send, grid, slant)
    (ordered_map,) = call(
        order_kernel,
        [VMEM] * 3,
        [shape((corners, half), BF16)],
        flops=2 * corners * half * half,
        moved=2 * half * half,
    )(own_map, other_map, right_hot)
    image, following, up, small = call(
        second_kernel,
        [SMEM] + [VMEM] * 15,
        [
            shape((columns, half), F32),
            shape((columns, half), F32),
            shape((columns, half + 3 * LANES), BF16),
            shape((columns, LANES), F32),
        ],
        scratch=[pltpu.VMEM((columns, block), BF16)],
        flops=2 * big,
        moved=4 * block * half,
    )(
        iface_sizes,
        corner_ids,
        coarse_inverse,
        operator,
        right_hot,
        loaded,
        weights,
        own_map,
        other_map,
        ordered_map,
        pack_in,
        send,
        kept,
        pair_in,
        along_in,
        slant_in,
    )
    up_in = shifted(up, "sub", 1)
    down_in = shifted(small, "sub", -1)
    far_in = shifted(small, "sub", 2)
    (mine,) = call(
        relay_kernel,
        [VMEM] * 5,
        [shape((columns, half + 3 * LANES), BF16)],
        moved=8 * columns * half,
    )(up, up_in, down_in, far_in, small)
    theirs = lax.ppermute(mine, grid, across)
    solution, residual = call(
        close_kernel,
        [SMEM] + [VMEM] * 12,
        [shape((columns, half), F32), shape((columns, half), F32)],
        moved=24 * columns * half,
    )(
        iface_sizes,
        corner_ids,
        coarse_inverse,
        loaded,
        weights,
        own_map,
        other_map,
        kept,
        pair_in,
        image,
        following,
        mine,
        theirs,
    )
    return solution[None], residual[None]


def per_device(*arrays):
    loads, _, dual_ops, _, coarse_inverse = arrays[:5]
    half = loads.shape[2]
    neighbourly = lax.axis_size("sub") == 4 and lax.axis_size("row") == 2
    sided = dual_ops.shape[1] == half and half % LANES == 0
    narrow = coarse_inverse.shape[0] + 4 <= LANES
    if neighbourly and sided and narrow and ITERS == 2:
        return ring(*arrays)
    return general(*arrays)


def solution(mesh):
    placed = (
        P(("parts", "sub"), "col", None),
        P(("parts", "sub"), None),
        P(("parts", "sub"), "row", None),
        P(("parts", "sub"), None, "row"),
        P("parts", None),
        P("parts", None),
        P("parts"),
        P(("parts", "sub"), None),
        P(("parts", "sub"), None),
    )
    return jax.shard_map(
        per_device,
        mesh=mesh,
        in_specs=placed,
        out_specs=(P(("parts", "sub"), "col", None), P(("parts", "sub"), "col", None)),
        check_vma=False,
    )
```

```python
import jax
import jax.numpy as jnp
from jax import lax
from jax.experimental import pallas as pl
from jax.experimental.pallas import tpu as pltpu
from jax.sharding import PartitionSpec as P

TILE = 128
LANES = 128
ITERS = 2
F32 = jnp.float32
BF16 = jnp.bfloat16
HIGH = lax.Precision.HIGHEST
VMEM = pl.BlockSpec(memory_space=pltpu.VMEM)
SMEM = pl.BlockSpec(memory_space=pltpu.SMEM)
HBM = pl.BlockSpec(memory_space=pltpu.HBM)


def shifted(value, axis, steps):
    count = lax.axis_size(axis)
    pairs = [(source, (source + steps) % count) for source in range(count)]
    return lax.ppermute(value, axis, pairs)


def inner(first, second, half):
    return jnp.sum(first[:, :half] * second[:, :half], axis=1)


def paired_totals(residual, precond, image, half):
    return lax.psum((inner(residual, precond, half), inner(precond, image, half)), "sub")


def tile_products(vector, rows_op, first_tile, last_tile, output):

    def one_tile(tile_at, acc):
        piece = lax.dynamic_slice_in_dim(rows_op, tile_at * TILE, TILE, 0)
        product = lax.dot_general(
            vector, piece, (((1,), (1,)), ((), ())), preferred_element_type=jnp.float32
        )
        return lax.dynamic_update_slice_in_dim(acc, product, tile_at * TILE, 1)

    return lax.fori_loop(first_tile, last_tile, one_tile, output)


def live_tiles(size_before, size_after, block_start, block, half):
    left_live = jnp.clip(size_before - block_start, 0, block)
    right_live = jnp.clip(size_after - (block_start - half), 0, block)
    live_cols = jnp.where(block_start < half, left_live, right_live)
    return (live_cols + TILE - 1) // TILE


def general(
    loads,
    weights,
    dual_ops,
    corner_maps,
    coarse_inverse,
    corner_ids,
    iface_sizes,
    left_partner,
    right_partner,
):
    half = loads.shape[2]
    block = dual_ops.shape[1]
    width = coarse_inverse.shape[0]
    subdomain = lax.axis_index("sub")
    count = lax.axis_size("sub")
    row_index = lax.axis_index("row")
    left_map = left_partner[0]
    right_map = right_partner[0]
    slots = jnp.arange(half, dtype=jnp.int32)
    size_before = iface_sizes[(subdomain + count - 1) % count]
    size_after = iface_sizes[subdomain]
    live_left = (slots < size_before).astype(jnp.float32)
    live_right = (right_map < size_after).astype(jnp.float32)
    columns = jnp.arange(width, dtype=jnp.int32)
    own_hot = (corner_ids[subdomain][:, None] == columns[None, :]).astype(jnp.float32)
    operator = dual_ops[0]
    coupling = corner_maps[0]
    block_start = row_index * block
    own_tiles = live_tiles(size_before, size_after, block_start, block, half)

    def apply_operator(vec):
        halfway = vec.astype(jnp.bfloat16)
        empty = jnp.zeros((halfway.shape[0], block), jnp.float32)
        local = tile_products(halfway, operator, jnp.int32(0), own_tiles, empty)
        own_slots = lax.dynamic_slice_in_dim(halfway, row_index * block, block, 1)
        corner = lax.dot_general(
            own_slots, coupling, (((1,), (1,)), ((), ())), preferred_element_type=jnp.float32
        )
        scattered = jnp.dot(corner, own_hot, precision=lax.Precision.HIGHEST)
        coarse = lax.psum(scattered, ("sub", "row"))
        solved = jnp.dot(coarse, coarse_inverse, precision=lax.Precision.HIGHEST)
        back = lax.dot_general(
            solved, own_hot, (((1,), (1,)), ((), ())), precision=lax.Precision.HIGHEST
        ).astype(jnp.bfloat16)
        united = local + jnp.dot(back, coupling, preferred_element_type=jnp.float32)
        whole = lax.all_gather(united.astype(jnp.bfloat16), "row", axis=1, tiled=True).astype(
            united.dtype
        )
        lower = whole[:, :half]
        upper = whole[:, half:]
        arrived_left = shifted(upper.astype(jnp.bfloat16), "sub", 1).astype(upper.dtype)
        arrived_right = shifted(lower.astype(jnp.bfloat16), "sub", -1).astype(lower.dtype)
        result_left = (lower + jnp.take(arrived_left, left_map, axis=1)) * live_left
        result_right = (upper + jnp.take(arrived_right, right_map, axis=1)) * live_right
        return jnp.concatenate([result_left, result_right], axis=1)

    received = (
        shifted(loads[0].astype(jnp.bfloat16), "sub", -1).astype(jnp.float32),
        shifted(weights.astype(jnp.bfloat16), "sub", -1).astype(weights.dtype),
    )
    right_load = jnp.take(received[0], right_map, axis=1) * live_right
    right_weight = jnp.take(received[1], right_map, axis=1)
    residual = jnp.concatenate([loads[0] * live_left, right_load], axis=1)
    scaling = jnp.concatenate([weights, right_weight], axis=1)
    solution = jnp.zeros_like(residual)
    precond = scaling * residual
    image = apply_operator(precond)
    gamma, delta = paired_totals(residual, precond, image, half)
    alpha = gamma / delta
    direction = precond
    along = image
    for step in range(ITERS):
        solution = solution + alpha[:, None] * direction
        residual = residual - alpha[:, None] * along
        if step + 1 < ITERS:
            precond = scaling * residual
            image = apply_operator(precond)
            gamma_next, delta = paired_totals(residual, precond, image, half)
            ratio = gamma_next / gamma
            alpha = gamma_next / (delta - ratio * gamma_next / alpha)
            direction = precond + ratio[:, None] * direction
            along = image + ratio[:, None] * along
            gamma = gamma_next
    return (solution[:, :half][None], residual[:, :half][None])


def cost(flops, moved):
    return pl.CostEstimate(flops=flops, bytes_accessed=moved, transcendentals=0)


def nt(first, second, precision=None):
    return lax.dot_general(
        first, second, (((1,), (1,)), ((), ())), preferred_element_type=F32, precision=precision
    )


def nn(first, second, precision=None):
    return jnp.dot(first, second, preferred_element_type=F32, precision=precision)


def halves(value):
    high = value.astype(BF16)
    return high, (value - high.astype(F32)).astype(BF16)


def stacked(value):
    return jnp.concatenate(halves(value), axis=0)


def folded(value):
    rows = value.shape[0] // 2
    return value[:rows] + value[rows:]


def thirds(value):
    high = value.astype(BF16)
    rest = value - high.astype(F32)
    middle = rest.astype(BF16)
    return high, middle, (rest - middle.astype(F32)).astype(BF16)


def pieces_sum(ref, rows, half, count):
    total = ref[rows, half : half + LANES].astype(F32)
    for piece in range(1, count):
        at = half + piece * LANES
        total = total + ref[rows, at : at + LANES].astype(F32)
    return total


def hot_rows(ids_ref, subdomain, extent):
    ids = ids_ref[pl.ds(subdomain, 1), :]
    names = lax.broadcasted_iota(jnp.int32, (extent, ids.shape[1]), 0)
    return (names == ids).astype(F32)


def neighbours():
    subdomain = lax.axis_index("sub")
    count = lax.axis_size("sub")
    return lax.rem(subdomain + count - 1, count), subdomain, lax.rem(subdomain + 1, count)


def live_row(sizes_ref, interface, half):
    slots = lax.broadcasted_iota(jnp.int32, (1, half), 1)
    return slots < sizes_ref[interface]


def fetched(pairs, sems):
    copies = [pltpu.make_async_copy(*pair, sems.at[at]) for at, pair in enumerate(pairs)]
    for copy in copies:
        copy.start()
    return copies


def open_kernel(
    sizes_in,
    loads_in,
    weights_in,
    maps_in,
    first_ref,
    pack_ref,
    sizes_ref,
    loads_ref,
    weights_ref,
    maps_ref,
    sems,
):
    pairs = (
        (sizes_in, sizes_ref),
        (loads_in, loads_ref),
        (weights_in, weights_ref),
        (maps_in, maps_ref),
    )
    copies = fetched(pairs, sems)
    before, _, _ = neighbours()
    half = loads_ref.shape[1]
    for copy in copies:
        copy.wait()
    scale = weights_ref[...]
    loaded = jnp.where(live_row(sizes_ref, before, half), loads_ref[...], 0.0)
    first = loaded * scale
    first_ref[...] = first.astype(BF16)
    high = scale.astype(BF16).astype(F32)
    which = lax.broadcasted_iota(jnp.int32, (8, half), 0)
    spare = jnp.where(which == 0, high, jnp.where(which == 1, scale - high, 0.0))
    pack_ref[...] = jnp.concatenate([first, maps_ref[...].astype(F32), spare], axis=0).astype(BF16)


def select_kernel(
    right_in,
    left_in,
    ids_in,
    operator_in,
    right_hot_ref,
    left_hot_ref,
    ids_ref,
    operator_ref,
    right_ref,
    left_ref,
    sems,
):
    pairs = (
        (right_in, right_ref),
        (left_in, left_ref),
        (ids_in, ids_ref),
        (operator_in, operator_ref),
    )
    copies = fetched(pairs, sems)
    half = right_ref.shape[1]
    copies[0].wait()
    copies[1].wait()

    def one(at, carry):
        start = pl.multiple_of(at * LANES, LANES)
        names = lax.broadcasted_iota(jnp.int32, (LANES, half), 0) + start
        rows = pl.ds(start, LANES)
        right_hot_ref[rows, :] = (names == right_ref[...]).astype(F32).astype(BF16)
        left_hot_ref[rows, :] = (names == left_ref[...]).astype(F32).astype(BF16)
        return carry

    lax.fori_loop(0, half // LANES, one, 0)
    copies[2].wait()
    copies[3].wait()


def first_kernel(
    ids_ref,
    operator_ref,
    right_hot_ref,
    left_hot_ref,
    first_ref,
    own_map_ref,
    across_ref,
    pack_ref,
    ahead_ref,
    send_ref,
    pair_ref,
    ordered_map_ref,
):
    before, subdomain, after = neighbours()
    lower = lax.axis_index("row") == 0
    columns, half = first_ref.shape
    corners = ids_ref.shape[1]
    left = first_ref[...]
    right = jnp.where(lower, pack_ref[:columns, :], ahead_ref[...])
    slotted = nn(right, right_hot_ref[...]).astype(BF16)
    local = nt(left, operator_ref[:, :half]) + nt(slotted, operator_ref[:, half:])
    raw_map = jnp.where(lower, across_ref[...], own_map_ref[...]).astype(F32)
    mixed = jnp.concatenate([local, raw_map], axis=0).astype(BF16)
    ordered = nt(mixed, right_hot_ref[...])
    ordered_map_ref[...] = ordered[columns:].astype(BF16)
    local = jnp.where(lower, local, ordered[:columns]).astype(BF16)
    pair_ref[columns:, :half] = pack_ref[columns:, :]

    @pl.when(jnp.logical_not(lower))
    def _():
        pair_ref[columns:, :half] = nn(pack_ref[columns:, :], left_hot_ref[...]).astype(BF16)

    beside = pair_ref[columns : columns + corners, :half]
    one = nt(jnp.where(lower, slotted, left), across_ref[...])
    two = nt(jnp.where(lower, right, left), beside)
    coarse = nt(one, hot_rows(ids_ref, subdomain, LANES), HIGH) + nt(
        two, hot_rows(ids_ref, jnp.where(lower, after, before), LANES), HIGH
    )
    high, low = halves(coarse)
    send = jnp.concatenate([local, high, low], axis=1)
    send_ref[...] = send
    pair_ref[:columns, :] = send
    pair_ref[columns:, half:] = jnp.zeros((pair_ref.shape[0] - columns, 2 * LANES), BF16)


def second_kernel(
    sizes_ref,
    ids_ref,
    inverse_ref,
    operator_ref,
    right_hot_ref,
    loads_ref,
    weights_ref,
    own_map_ref,
    across_ref,
    ordered_map_ref,
    pack_ref,
    send_ref,
    kept_ref,
    pair_ref,
    along_ref,
    slant_ref,
    image_ref,
    next_ref,
    up_ref,
    small_ref,
    ordered_ref,
):
    before, subdomain, after = neighbours()
    lower = lax.axis_index("row") == 0
    columns, half = loads_ref.shape
    corners = ids_ref.shape[1]
    width = inverse_ref.shape[0]
    everyone = slice(0, columns)
    top = slice(0, half)
    own, other = send_ref[:, top].astype(F32), pair_ref[everyone, top].astype(F32)
    along, slant = along_ref[:, top].astype(F32), slant_ref[:, top].astype(F32)
    own_c = pieces_sum(send_ref, everyone, half, 2)
    other_c = pieces_sum(pair_ref, everyone, half, 2)
    along_c = pieces_sum(along_ref, everyone, half, 2)
    slant_c = pieces_sum(slant_ref, everyone, half, 2)
    coarse = (jnp.where(lower, own_c, other_c) + jnp.where(lower, other_c, own_c)) + (
        jnp.where(lower, along_c, slant_c) + jnp.where(lower, slant_c, along_c)
    )
    solved = nn(coarse[:, :width], inverse_ref[...], HIGH)
    hot_own = hot_rows(ids_ref, subdomain, width)
    hot_after = hot_rows(ids_ref, after, width)
    hot_before = hot_rows(ids_ref, before, width)
    back_own = nn(solved, hot_own, HIGH).astype(BF16)
    back_after = nn(solved, hot_after, HIGH).astype(BF16)
    back_before = nn(solved, hot_before, HIGH).astype(BF16)
    maps = slice(columns, columns + corners)
    kept, relayed = kept_ref[maps, top], pair_ref[maps, top]
    left_map = jnp.where(lower, own_map_ref[...], across_ref[...])
    map_after = jnp.where(lower, kept, relayed)
    map_before = jnp.where(lower, relayed, kept)
    fix_left = nn(back_own, left_map) + nn(back_before, map_before)
    fix_right = nn(back_own, ordered_map_ref[...]) + nn(back_after, map_after)
    live_left = live_row(sizes_ref, before, half)
    live_right = live_row(sizes_ref, subdomain, half)
    image = jnp.where(lower, own, other) + jnp.where(lower, slant, along) + fix_left
    image = jnp.where(live_left, image, 0.0)
    image_right = jnp.where(lower, other, own) + jnp.where(lower, along, slant) + fix_right
    image_right = jnp.where(live_right, image_right, 0.0)
    scale = weights_ref[...]
    spare = columns + corners
    scales = jnp.where(
        lower,
        pack_ref[spare : spare + 8, :].astype(F32),
        pair_ref[spare : spare + 8, top].astype(F32),
    )
    left = scale * image
    right = (scales[0:1] + scales[1:2]) * image_right
    image_ref[...] = image
    next_ref[...] = left
    left_2, right_2 = stacked(left), stacked(right)
    slotted_2 = nn(right_2, right_hot_ref[...]).astype(BF16)
    local = folded(nt(left_2, operator_ref[:, :half]) + nt(slotted_2, operator_ref[:, half:]))
    block = folded(jnp.where(lower, left_2, slotted_2).astype(F32))
    energy = jnp.sum(block * local, axis=1, keepdims=True)
    ordered_ref[...] = local.astype(BF16)

    @pl.when(jnp.logical_not(lower))
    def _():
        ordered_ref[...] = nt(ordered_ref[...], right_hot_ref[...]).astype(BF16)

    one = folded(nt(jnp.where(lower, slotted_2, left_2), across_ref[...]))
    two = folded(nt(jnp.where(lower, right_2, left_2), kept))
    coarse = nt(one, hot_rows(ids_ref, subdomain, LANES), HIGH) + nt(
        two, hot_rows(ids_ref, jnp.where(lower, after, before), LANES), HIGH
    )
    loaded = jnp.where(live_left, loads_ref[...], 0.0)
    first = loaded * scale
    sums = (
        jnp.sum(loaded * first, axis=1, keepdims=True),
        jnp.sum(first * image, axis=1, keepdims=True),
        jnp.sum(image * left, axis=1, keepdims=True),
        energy,
    )
    lane = lax.broadcasted_iota(jnp.int32, (columns, LANES), 1)
    small = jnp.where(lane < width, coarse, 0.0)
    for at, value in enumerate(sums):
        small = jnp.where(lane == width + at, value, small)
    small_ref[...] = small
    up_ref[...] = jnp.concatenate([ordered_ref[...], *thirds(small)], axis=1)


def relay_kernel(up_own_ref, up_ref, down_ref, far_ref, own_ref, out_ref):
    lower = lax.axis_index("row") == 0
    columns = up_ref.shape[0]
    half = up_ref.shape[1] - 3 * LANES
    total = own_ref[...] + pieces_sum(up_ref, slice(0, columns), half, 3)
    total = total + down_ref[...] + far_ref[...]
    bulk = jnp.where(lower, up_own_ref[:, :half], up_ref[:, :half])
    out_ref[...] = jnp.concatenate([bulk, *thirds(total)], axis=1)


def close_kernel(
    sizes_ref,
    ids_ref,
    inverse_ref,
    loads_ref,
    weights_ref,
    own_map_ref,
    across_ref,
    kept_ref,
    pair_ref,
    image_ref,
    next_ref,
    mine_ref,
    theirs_ref,
    solution_ref,
    residual_ref,
):
    before, subdomain, _ = neighbours()
    lower = lax.axis_index("row") == 0
    columns, half = loads_ref.shape
    corners = ids_ref.shape[1]
    width = inverse_ref.shape[0]
    everyone = slice(0, columns)
    top = slice(0, half)
    mine = pieces_sum(mine_ref, everyone, half, 3)
    theirs = pieces_sum(theirs_ref, everyone, half, 3)
    total = jnp.where(lower, mine, theirs)
    rest = jnp.where(lower, theirs, mine)
    coarse = total[:, :width]
    solved = nn(coarse, inverse_ref[...], HIGH)
    back_own = nn(solved, hot_rows(ids_ref, subdomain, width), HIGH).astype(BF16)
    back_before = nn(solved, hot_rows(ids_ref, before, width), HIGH).astype(BF16)
    maps = slice(columns, columns + corners)
    left_map = jnp.where(lower, own_map_ref[...], across_ref[...])
    map_before = jnp.where(lower, pair_ref[maps, top], kept_ref[maps, top])
    fix = nn(back_own, left_map) + nn(back_before, map_before)
    image_next = mine_ref[:, top].astype(F32) + theirs_ref[:, top].astype(F32) + fix
    live = live_row(sizes_ref, before, half)
    image_next = jnp.where(live, image_next, 0.0)
    lane = lax.broadcasted_iota(jnp.int32, (columns, LANES), 1)

    def column(values, at):
        return jnp.sum(jnp.where(lane == width + at, values, 0.0), axis=1, keepdims=True)

    gamma = column(total, 0)
    delta = column(total, 1)
    cross = column(total, 2)
    energy = column(total, 3) + column(rest, 3) + jnp.sum(coarse * solved, axis=1, keepdims=True)
    alpha = gamma / delta
    gamma_next = gamma - 2.0 * alpha * delta + alpha * alpha * cross
    ratio = gamma_next / gamma
    grown = 1.0 + ratio
    curvature = grown * grown * delta - 2.0 * grown * alpha * cross + alpha * alpha * energy
    alpha_next = gamma_next / curvature
    loaded = jnp.where(live, loads_ref[...], 0.0)
    first = loaded * weights_ref[...]
    direction = grown * first - alpha * next_ref[...]
    along = grown * image_ref[...] - alpha * image_next
    solution_ref[...] = alpha * first + alpha_next * direction
    residual_ref[...] = loaded - alpha * image_ref[...] - alpha_next * along


def ring(
    loads,
    weights,
    dual_ops,
    corner_maps,
    coarse_inverse,
    corner_ids,
    iface_sizes,
    left_partner,
    right_partner,
):
    count = lax.axis_size("sub")
    sides = lax.axis_size("row")
    columns, half = loads.shape[1:]
    corners = corner_maps.shape[1]
    operator = dual_ops[0]
    own_map = corner_maps[0]
    loaded = loads[0]
    block = operator.shape[0]
    shape = jax.ShapeDtypeStruct
    grid = ("sub", "row")
    big = 2 * columns * block * 2 * half

    def pairs(target):
        listed = []
        for at in range(count):
            for side in range(sides):
                to_at, to_side = target(at, side)
                listed.append((at * sides + side, (to_at % count) * sides + to_side))
        return listed

    across = pairs(lambda at, side: (at, 1 - side))
    along = pairs(lambda at, side: (at - 1, 0) if side == 0 else (at + 1, 1))
    slant = pairs(lambda at, side: (at - 1, 1) if side == 0 else (at + 1, 0))

    def call(kernel, specs, outs, scratch=(), flops=0, moved=0, room=4):
        made = pl.pallas_call(
            kernel,
            in_specs=specs,
            out_specs=[VMEM] * len(outs),
            out_shape=outs,
            scratch_shapes=scratch,
            cost_estimate=cost(flops, moved),
            compiler_params=pltpu.CompilerParams(vmem_limit_bytes=room << 20),
        )

        def run(*operands):
            pairs = zip(operands, specs, strict=True)
            placed = [
                pltpu.with_memory_space_constraint(operand, pltpu.HBM) if spec is HBM else operand
                for operand, spec in pairs
            ]
            return made(*placed)

        return run

    rows = columns + corners + 8
    first, pack = call(
        open_kernel,
        [HBM] * 4,
        [shape((columns, half), BF16), shape((rows, half), BF16)],
        scratch=[
            pltpu.SMEM(iface_sizes.shape, jnp.int32),
            pltpu.VMEM(loaded.shape, F32),
            pltpu.VMEM(weights.shape, F32),
            pltpu.VMEM(own_map.shape, BF16),
            pltpu.SemaphoreType.DMA((4,)),
        ],
        moved=4 * rows * half,
    )(iface_sizes, loaded, weights, own_map)
    other_map = lax.ppermute(own_map, grid, across)
    pack_in = lax.ppermute(pack, grid, along)
    ahead = lax.ppermute(first, grid, slant)
    right_hot, left_hot, ids, held = call(
        select_kernel,
        [HBM] * 4,
        [
            shape((half, half), BF16),
            shape((half, half), BF16),
            shape(corner_ids.shape, jnp.int32),
            shape(operator.shape, BF16),
        ],
        scratch=[
            pltpu.VMEM(right_partner.shape, jnp.int32),
            pltpu.VMEM(left_partner.shape, jnp.int32),
            pltpu.SemaphoreType.DMA((4,)),
        ],
        flops=4 * half * half,
        moved=4 * half * half,
        room=12,
    )(right_partner, left_partner, corner_ids, operator)
    send, kept, ordered_map = call(
        first_kernel,
        [VMEM] * 9,
        [
            shape((columns, half + 2 * LANES), BF16),
            shape((rows, half + 2 * LANES), BF16),
            shape((corners, half), BF16),
        ],
        flops=2 * big,
        moved=4 * block * half,
        room=16,
    )(ids, held, right_hot, left_hot, first, own_map, other_map, pack_in, ahead)
    pair_in = lax.ppermute(kept, grid, across)
    along_in = lax.ppermute(send, grid, along)
    slant_in = lax.ppermute(send, grid, slant)
    image, following, up, small = call(
        second_kernel,
        [SMEM] + [VMEM] * 15,
        [
            shape((columns, half), F32),
            shape((columns, half), F32),
            shape((columns, half + 3 * LANES), BF16),
            shape((columns, LANES), F32),
        ],
        scratch=[pltpu.VMEM((columns, block), BF16)],
        flops=2 * big,
        moved=4 * block * half,
        room=16,
    )(
        iface_sizes,
        ids,
        coarse_inverse,
        held,
        right_hot,
        loaded,
        weights,
        own_map,
        other_map,
        ordered_map,
        pack_in,
        send,
        kept,
        pair_in,
        along_in,
        slant_in,
    )
    up_in = shifted(up, "sub", 1)
    down_in = shifted(small, "sub", -1)
    far_in = shifted(small, "sub", 2)
    (mine,) = call(
        relay_kernel,
        [VMEM] * 5,
        [shape((columns, half + 3 * LANES), BF16)],
        moved=8 * columns * half,
    )(up, up_in, down_in, far_in, small)
    theirs = lax.ppermute(mine, grid, across)
    solution, residual = call(
        close_kernel,
        [SMEM] + [VMEM] * 12,
        [shape((columns, half), F32), shape((columns, half), F32)],
        moved=24 * columns * half,
    )(
        iface_sizes,
        ids,
        coarse_inverse,
        loaded,
        weights,
        own_map,
        other_map,
        kept,
        pair_in,
        image,
        following,
        mine,
        theirs,
    )
    return solution[None], residual[None]


def per_device(*arrays):
    loads, _, dual_ops, _, coarse_inverse = arrays[:5]
    half = loads.shape[2]
    neighbourly = lax.axis_size("sub") == 4 and lax.axis_size("row") == 2
    sided = dual_ops.shape[1] == half and half % LANES == 0
    narrow = coarse_inverse.shape[0] + 4 <= LANES
    if neighbourly and sided and narrow and ITERS == 2:
        return ring(*arrays)
    return general(*arrays)


def solution(mesh):
    placed = (
        P(("parts", "sub"), "col", None),
        P(("parts", "sub"), None),
        P(("parts", "sub"), "row", None),
        P(("parts", "sub"), None, "row"),
        P("parts", None),
        P("parts", None),
        P("parts"),
        P(("parts", "sub"), None),
        P(("parts", "sub"), None),
    )
    return jax.shard_map(
        per_device,
        mesh=mesh,
        in_specs=placed,
        out_specs=(P(("parts", "sub"), "col", None), P(("parts", "sub"), "col", None)),
        check_vma=False,
    )
```

```python
import jax
import jax.numpy as jnp
from jax import lax
from jax.experimental import pallas as pl
from jax.experimental.pallas import tpu as pltpu
from jax.sharding import PartitionSpec as P

TILE = 128
LANES = 128
ITERS = 2
F32 = jnp.float32
BF16 = jnp.bfloat16
HIGH = lax.Precision.HIGHEST
VMEM = pl.BlockSpec(memory_space=pltpu.VMEM)
HBM = pl.BlockSpec(memory_space=pltpu.HBM)


def shifted(value, axis, steps):
    count = lax.axis_size(axis)
    pairs = [(source, (source + steps) % count) for source in range(count)]
    return lax.ppermute(value, axis, pairs)


def inner(first, second, half):
    return jnp.sum(first[:, :half] * second[:, :half], axis=1)


def paired_totals(residual, precond, image, half):
    return lax.psum((inner(residual, precond, half), inner(precond, image, half)), "sub")


def tile_products(vector, rows_op, first_tile, last_tile, output):

    def one_tile(tile_at, acc):
        piece = lax.dynamic_slice_in_dim(rows_op, tile_at * TILE, TILE, 0)
        product = lax.dot_general(
            vector, piece, (((1,), (1,)), ((), ())), preferred_element_type=jnp.float32
        )
        return lax.dynamic_update_slice_in_dim(acc, product, tile_at * TILE, 1)

    return lax.fori_loop(first_tile, last_tile, one_tile, output)


def live_tiles(size_before, size_after, block_start, block, half):
    left_live = jnp.clip(size_before - block_start, 0, block)
    right_live = jnp.clip(size_after - (block_start - half), 0, block)
    live_cols = jnp.where(block_start < half, left_live, right_live)
    return (live_cols + TILE - 1) // TILE


def general(
    loads,
    weights,
    dual_ops,
    corner_maps,
    coarse_inverse,
    corner_ids,
    iface_sizes,
    left_partner,
    right_partner,
):
    half = loads.shape[2]
    block = dual_ops.shape[1]
    width = coarse_inverse.shape[0]
    subdomain = lax.axis_index("sub")
    count = lax.axis_size("sub")
    row_index = lax.axis_index("row")
    left_map = left_partner[0]
    right_map = right_partner[0]
    slots = jnp.arange(half, dtype=jnp.int32)
    size_before = iface_sizes[(subdomain + count - 1) % count]
    size_after = iface_sizes[subdomain]
    live_left = (slots < size_before).astype(jnp.float32)
    live_right = (right_map < size_after).astype(jnp.float32)
    columns = jnp.arange(width, dtype=jnp.int32)
    own_hot = (corner_ids[subdomain][:, None] == columns[None, :]).astype(jnp.float32)
    operator = dual_ops[0]
    coupling = corner_maps[0]
    block_start = row_index * block
    own_tiles = live_tiles(size_before, size_after, block_start, block, half)

    def apply_operator(vec):
        halfway = vec.astype(jnp.bfloat16)
        empty = jnp.zeros((halfway.shape[0], block), jnp.float32)
        local = tile_products(halfway, operator, jnp.int32(0), own_tiles, empty)
        own_slots = lax.dynamic_slice_in_dim(halfway, row_index * block, block, 1)
        corner = lax.dot_general(
            own_slots, coupling, (((1,), (1,)), ((), ())), preferred_element_type=jnp.float32
        )
        scattered = jnp.dot(corner, own_hot, precision=lax.Precision.HIGHEST)
        coarse = lax.psum(scattered, ("sub", "row"))
        solved = jnp.dot(coarse, coarse_inverse, precision=lax.Precision.HIGHEST)
        back = lax.dot_general(
            solved, own_hot, (((1,), (1,)), ((), ())), precision=lax.Precision.HIGHEST
        ).astype(jnp.bfloat16)
        united = local + jnp.dot(back, coupling, preferred_element_type=jnp.float32)
        whole = lax.all_gather(united.astype(jnp.bfloat16), "row", axis=1, tiled=True).astype(
            united.dtype
        )
        lower = whole[:, :half]
        upper = whole[:, half:]
        arrived_left = shifted(upper.astype(jnp.bfloat16), "sub", 1).astype(upper.dtype)
        arrived_right = shifted(lower.astype(jnp.bfloat16), "sub", -1).astype(lower.dtype)
        result_left = (lower + jnp.take(arrived_left, left_map, axis=1)) * live_left
        result_right = (upper + jnp.take(arrived_right, right_map, axis=1)) * live_right
        return jnp.concatenate([result_left, result_right], axis=1)

    received = (
        shifted(loads[0].astype(jnp.bfloat16), "sub", -1).astype(jnp.float32),
        shifted(weights.astype(jnp.bfloat16), "sub", -1).astype(weights.dtype),
    )
    right_load = jnp.take(received[0], right_map, axis=1) * live_right
    right_weight = jnp.take(received[1], right_map, axis=1)
    residual = jnp.concatenate([loads[0] * live_left, right_load], axis=1)
    scaling = jnp.concatenate([weights, right_weight], axis=1)
    solution = jnp.zeros_like(residual)
    precond = scaling * residual
    image = apply_operator(precond)
    gamma, delta = paired_totals(residual, precond, image, half)
    alpha = gamma / delta
    direction = precond
    along = image
    for step in range(ITERS):
        solution = solution + alpha[:, None] * direction
        residual = residual - alpha[:, None] * along
        if step + 1 < ITERS:
            precond = scaling * residual
            image = apply_operator(precond)
            gamma_next, delta = paired_totals(residual, precond, image, half)
            ratio = gamma_next / gamma
            alpha = gamma_next / (delta - ratio * gamma_next / alpha)
            direction = precond + ratio[:, None] * direction
            along = image + ratio[:, None] * along
            gamma = gamma_next
    return (solution[:, :half][None], residual[:, :half][None])


def cost(flops, moved):
    return pl.CostEstimate(flops=flops, bytes_accessed=moved, transcendentals=0)


def nt(first, second, precision=None):
    return lax.dot_general(
        first, second, (((1,), (1,)), ((), ())), preferred_element_type=F32, precision=precision
    )


def nn(first, second, precision=None):
    return jnp.dot(first, second, preferred_element_type=F32, precision=precision)


def halves(value):
    high = value.astype(BF16)
    return high, (value - high.astype(F32)).astype(BF16)


def stacked(value):
    return jnp.concatenate(halves(value), axis=0)


def folded(value):
    rows = value.shape[0] // 2
    return value[:rows] + value[rows:]


def thirds(value):
    high = value.astype(BF16)
    rest = value - high.astype(F32)
    middle = rest.astype(BF16)
    return high, middle, (rest - middle.astype(F32)).astype(BF16)


def pieces_sum(ref, half, count):
    total = ref[:, half : half + LANES].astype(F32)
    for piece in range(1, count):
        at = half + piece * LANES
        total = total + ref[:, at : at + LANES].astype(F32)
    return total


def neighbours():
    subdomain = lax.axis_index("sub")
    count = lax.axis_size("sub")
    return lax.rem(subdomain + count - 1, count), subdomain, lax.rem(subdomain + 1, count)


def hot_rows(ids_ref, subdomain, extent):
    ids = ids_ref[pl.ds(subdomain, 1), :]
    names = lax.broadcasted_iota(jnp.int32, (extent, ids.shape[1]), 0)
    return (names == ids).astype(F32)


def hot_names(ids_ref):
    spare = jnp.zeros((LANES, LANES - 3 * ids_ref.shape[1]), F32)
    hots = [hot_rows(ids_ref, each, LANES) for each in neighbours()]
    return jnp.concatenate([*hots, spare], axis=1)


def selected(values, names):
    high, middle, low = thirds(values)
    rows = values.shape[0]
    parts = nt(jnp.concatenate([high, middle, low], axis=0), names)
    return parts[:rows] + parts[rows : 2 * rows] + parts[2 * rows :]


def solved_backs(coarse, solver):
    rows = coarse.shape[0]
    parts = nn(stacked(coarse), solver)
    width = solver.shape[1] // 2
    return parts[:rows, :width] + (parts[:rows, width:] + parts[rows:, :width])


def open_kernel(
    sizes_in,
    loads_in,
    maps_in,
    weights_in,
    ids_in,
    inverse_in,
    right_in,
    left_in,
    pack_ref,
    loaded_ref,
    live_ref,
    weights_ref,
    ids_ref,
    inverse_ref,
    right_ref,
    left_ref,
    sizes_ref,
    loads_ref,
    maps_ref,
    sems,
):
    pairs = (
        (sizes_in, sizes_ref),
        (loads_in, loads_ref),
        (weights_in, weights_ref),
        (maps_in, maps_ref),
        (ids_in, ids_ref),
        (inverse_in, inverse_ref),
        (right_in, right_ref),
        (left_in, left_ref),
    )
    copies = [pltpu.make_async_copy(*pair, sems.at[at]) for at, pair in enumerate(pairs)]
    for copy in copies:
        copy.start()
    before, subdomain, _ = neighbours()
    for copy in copies:
        copy.wait()
    slots = lax.broadcasted_iota(jnp.int32, live_ref.shape, 1)
    which = lax.broadcasted_iota(jnp.int32, live_ref.shape, 0)
    bound = jnp.where(which == 0, sizes_ref[before], sizes_ref[subdomain])
    live = (slots < bound).astype(F32)
    live_ref[...] = live
    scale = weights_ref[...]
    loaded = jnp.where(live[0:1] > 0.0, loads_ref[...], 0.0)
    loaded_ref[...] = loaded
    first = loaded * scale
    high = scale.astype(BF16).astype(F32)
    spare = jnp.where(which == 0, high, jnp.where(which == 1, scale - high, 0.0))
    pack_ref[...] = jnp.concatenate([first, maps_ref[...].astype(F32), spare], axis=0).astype(BF16)


def side_columns(ref, side, half):
    return ref.at[:, pl.ds(pl.multiple_of(side * half, half), half)]


def select_kernel(
    right_ref,
    left_ref,
    pack_ref,
    operator_in,
    right_hot_ref,
    order_ref,
    left_hot_ref,
    square_ref,
    cross_ref,
    local_ref,
    turned_ref,
    sems,
):
    half = right_ref.shape[1]
    columns = local_ref.shape[0]
    side = lax.axis_index("row")
    lower = side == 0
    square = pltpu.make_async_copy(side_columns(operator_in, side, half), square_ref, sems.at[0])
    cross = pltpu.make_async_copy(side_columns(operator_in, 1 - side, half), cross_ref, sems.at[1])

    @pl.when(lower)
    def _():
        square.start()
        cross.start()

    @pl.when(jnp.logical_not(lower))
    def _():
        cross.start()
        square.start()

    right = right_ref[...]
    tall = jnp.transpose(jnp.broadcast_to(right, (8, half)).astype(F32))[:, 0:1].astype(jnp.int32)
    names = lax.broadcasted_iota(jnp.int32, (LANES, half), 1)
    for at in range(half // LANES):
        rows = slice(at * LANES, (at + 1) * LANES)
        order_ref[rows, :] = (names == tall[rows]).astype(F32).astype(BF16)

    def one(at, carry):
        start = pl.multiple_of(at * LANES, LANES)
        slots = lax.broadcasted_iota(jnp.int32, (LANES, half), 0) + start
        rows = pl.ds(start, LANES)
        right_hot_ref[rows, :] = (slots == right).astype(F32).astype(BF16)
        left_hot_ref[rows, :] = (slots == left_ref[...]).astype(F32).astype(BF16)
        return carry

    lax.fori_loop(0, half // LANES, one, 0)
    left = pack_ref[:columns, :]

    @pl.when(lower)
    def _():
        turned_ref[...] = left
        square.wait()
        local_ref[...] = nn(left, square_ref[...])
        cross.wait()

    @pl.when(jnp.logical_not(lower))
    def _():
        turned_ref[...] = nt(left, left_hot_ref[...]).astype(BF16)
        cross.wait()
        local_ref[...] = nt(left, cross_ref[...])
        square.wait()


def first_kernel(
    ids_ref,
    square_ref,
    cross_ref,
    right_hot_ref,
    order_ref,
    local_ref,
    turned_ref,
    own_pack_ref,
    across_ref,
    along_ref,
    slant_ref,
    send_ref,
):
    columns, half = local_ref.shape
    corners = ids_ref.shape[1]
    before, subdomain, after = neighbours()
    lower = lax.axis_index("row") == 0
    left = own_pack_ref[:columns, :]
    right = jnp.where(lower, along_ref[:columns, :], slant_ref[:columns, :])
    slotted = nn(right, right_hot_ref[...]).astype(BF16)

    @pl.when(lower)
    def _():
        send_ref[:, :half] = (local_ref[...] + nt(slotted, cross_ref[...])).astype(BF16)

    @pl.when(jnp.logical_not(lower))
    def _():
        local = (local_ref[...] + nn(slotted, square_ref[...])).astype(BF16)
        send_ref[:, :half] = nn(local, order_ref[...]).astype(BF16)

    one = nt(jnp.where(lower, slotted, left), across_ref[...])
    beside = along_ref[columns:, :]
    two = nt(jnp.where(lower, right, turned_ref[...]), beside)[:, :corners]
    hot_own = hot_rows(ids_ref, subdomain, LANES)
    hot_other = hot_rows(ids_ref, jnp.where(lower, after, before), LANES)
    high, low = halves(selected(one, hot_own) + selected(two, hot_other))
    send_ref[:, half:] = jnp.concatenate([high, low], axis=1)


def order_kernel(
    ids_ref,
    inverse_ref,
    order_ref,
    left_hot_ref,
    own_pack_ref,
    across_ref,
    along_ref,
    slant_ref,
    maps_ref,
    solver_ref,
    scale_ref,
    names_ref,
):
    half = order_ref.shape[1]
    corners = ids_ref.shape[1]
    width = inverse_ref.shape[0]
    columns = own_pack_ref.shape[0] - corners - 8
    lower = lax.axis_index("row") == 0
    own, across = own_pack_ref[columns:, :].astype(F32)[:corners], across_ref[...].astype(F32)
    along, slant = along_ref[columns:, :].astype(F32), slant_ref[columns:, :].astype(F32)
    ahead, behind = jnp.where(lower, along, slant), jnp.where(lower, slant, along)
    scale_ref[...] = ahead[corners : corners + 1] + ahead[corners + 1 : corners + 2]
    raw = jnp.where(lower, across, own).astype(BF16)
    ordered = nn(raw, order_ref[...])
    turned = nn(behind[:corners].astype(BF16), left_hot_ref[...])
    spare = jnp.zeros((LANES - 3 * corners, half), F32)
    blank = jnp.zeros((corners, half), F32)
    mine = jnp.where(lower, own, across)
    maps_ref[:, :half] = jnp.concatenate([turned, mine, blank, spare], axis=0).astype(BF16)
    maps_ref[:, half:] = jnp.concatenate([blank, ordered, ahead[:corners], spare], axis=0).astype(BF16)
    names = hot_names(ids_ref)
    names_ref[...] = names.astype(BF16)
    backs = nn(inverse_ref[...], names[:width], HIGH)
    low_rows = jnp.zeros((LANES - width, LANES), F32)
    side = jnp.concatenate([inverse_ref[...], jnp.zeros((width, LANES - width), F32)], axis=1)
    pieces = []
    for piece in (backs, side):
        tall = jnp.concatenate([piece, low_rows], axis=0)
        pieces.extend(halves(tall))
    solver_ref[...] = jnp.concatenate(pieces, axis=1)


def second_kernel(
    names_ref,
    solver_ref,
    maps_ref,
    right_hot_ref,
    order_ref,
    square_ref,
    cross_ref,
    live_ref,
    loaded_ref,
    weights_ref,
    scale_ref,
    own_ref,
    across_ref,
    along_ref,
    slant_ref,
    image_ref,
    next_ref,
    up_ref,
    small_ref,
):
    lower = lax.axis_index("row") == 0
    columns, half = loaded_ref.shape
    own, across = own_ref[:, :half].astype(F32), across_ref[:, :half].astype(F32)
    along, slant = along_ref[:, :half].astype(F32), slant_ref[:, :half].astype(F32)
    mine = pieces_sum(own_ref, half, 2) + pieces_sum(across_ref, half, 2)
    coarse = mine + (pieces_sum(along_ref, half, 2) + pieces_sum(slant_ref, half, 2))
    backs = solved_backs(coarse, solver_ref[:, : 2 * LANES]).astype(BF16)
    fix = nn(backs, maps_ref[...])
    image = jnp.where(lower, own, across) + jnp.where(lower, slant, along) + fix[:, :half]
    image = jnp.where(live_ref[0:1] > 0.0, image, 0.0)
    image_right = jnp.where(lower, across, own) + jnp.where(lower, along, slant) + fix[:, half:]
    image_right = jnp.where(live_ref[1:2] > 0.0, image_right, 0.0)
    left = weights_ref[...] * image
    right = scale_ref[...] * image_right
    image_ref[...] = image
    next_ref[...] = left
    left_2, right_2 = stacked(left), stacked(right)
    slotted_2 = nn(right_2, right_hot_ref[...]).astype(BF16)
    near, far = jnp.where(lower, left_2, slotted_2), jnp.where(lower, slotted_2, left_2)
    local = folded(nn(near, square_ref[...]) + nt(far, cross_ref[...]))
    rounded = local.astype(BF16)
    up_ref[:, :half] = rounded

    @pl.when(jnp.logical_not(lower))
    def _():
        up_ref[:, :half] = nn(rounded, order_ref[...]).astype(BF16)

    block = folded(near.astype(F32))
    energy = jnp.sum(block * local, axis=1, keepdims=True)
    sided = jnp.where(lower, maps_ref[:, half:], maps_ref[:, :half])
    corner = folded(nt(jnp.where(lower, right_2, left_2), sided))
    loaded = loaded_ref[...]
    first = loaded * weights_ref[...]
    sums = (
        jnp.sum(loaded * first, axis=1, keepdims=True),
        jnp.sum(first * image, axis=1, keepdims=True),
        jnp.sum(image * left, axis=1, keepdims=True),
        energy,
    )
    lane = lax.broadcasted_iota(jnp.int32, (columns, LANES), 1)
    small = selected(corner, names_ref[...])
    for at, value in enumerate(sums):
        small = jnp.where(lane == LANES - len(sums) + at, value, small)
    small_ref[...] = small
    up_ref[:, half:] = jnp.concatenate(thirds(small), axis=1)


def relay_kernel(up_own_ref, up_ref, down_ref, far_ref, own_ref, out_ref):
    lower = lax.axis_index("row") == 0
    half = up_ref.shape[1] - 3 * LANES
    total = own_ref[...] + pieces_sum(up_ref, half, 3)
    total = total + down_ref[...] + far_ref[...]
    out_ref[:, :half] = jnp.where(lower, up_own_ref[:, :half], up_ref[:, :half])
    out_ref[:, half:] = jnp.concatenate(thirds(total), axis=1)


def close_kernel(
    solver_ref,
    maps_ref,
    live_ref,
    loaded_ref,
    weights_ref,
    image_ref,
    next_ref,
    mine_ref,
    theirs_ref,
    solution_ref,
    residual_ref,
):
    lower = lax.axis_index("row") == 0
    columns, half = loaded_ref.shape
    mine, theirs = pieces_sum(mine_ref, half, 3), pieces_sum(theirs_ref, half, 3)
    total = jnp.where(lower, mine, theirs)
    lane = lax.broadcasted_iota(jnp.int32, (columns, LANES), 1)
    coarse = jnp.where(lane < LANES - 4, total, 0.0)
    backs = solved_backs(coarse, solver_ref[:, : 2 * LANES]).astype(BF16)
    solved = solved_backs(coarse, solver_ref[:, 2 * LANES :])
    fix = nn(backs, maps_ref[:, :half])
    image_next = mine_ref[:, :half].astype(F32) + theirs_ref[:, :half].astype(F32) + fix
    image_next = jnp.where(live_ref[0:1] > 0.0, image_next, 0.0)

    def column(values, at):
        return jnp.sum(jnp.where(lane == LANES - 4 + at, values, 0.0), axis=1, keepdims=True)

    gamma = column(total, 0)
    delta = column(total, 1)
    cross = column(total, 2)
    energy = column(mine + theirs, 3) + jnp.sum(coarse * solved, axis=1, keepdims=True)
    alpha = gamma / delta
    gamma_next = gamma - 2.0 * alpha * delta + alpha * alpha * cross
    ratio = gamma_next / gamma
    grown = 1.0 + ratio
    curvature = grown * grown * delta - 2.0 * grown * alpha * cross + alpha * alpha * energy
    alpha_next = gamma_next / curvature
    loaded = loaded_ref[...]
    first = loaded * weights_ref[...]
    direction = grown * first - alpha * next_ref[...]
    along = grown * image_ref[...] - alpha * image_next
    solution_ref[...] = alpha * first + alpha_next * direction
    residual_ref[...] = loaded - alpha * image_ref[...] - alpha_next * along


def ring(
    loads,
    weights,
    dual_ops,
    corner_maps,
    coarse_inverse,
    corner_ids,
    iface_sizes,
    left_partner,
    right_partner,
):
    count = lax.axis_size("sub")
    sides = lax.axis_size("row")
    columns, half = loads.shape[1:]
    corners = corner_maps.shape[1]
    operator = dual_ops[0]
    own_map = corner_maps[0]
    loaded = loads[0]
    block = operator.shape[0]
    shape = jax.ShapeDtypeStruct
    grid = ("sub", "row")
    big = 2 * columns * block * 2 * half

    def pairs(target):
        listed = []
        for at in range(count):
            for side in range(sides):
                to_at, to_side = target(at, side)
                listed.append((at * sides + side, (to_at % count) * sides + to_side))
        return listed

    across = pairs(lambda at, side: (at, 1 - side))
    along = pairs(lambda at, side: (at - 1, 0) if side == 0 else (at + 1, 1))
    slant = pairs(lambda at, side: (at - 1, 1) if side == 0 else (at + 1, 0))

    def call(kernel, operands, outs, scratch=(), flops=0, moved=0, room=4):
        specs, placed = [], []
        for operand in operands:
            held = isinstance(operand, tuple)
            specs.append(HBM if held else VMEM)
            placed.append(
                pltpu.with_memory_space_constraint(operand[0], pltpu.HBM) if held else operand
            )
        return pl.pallas_call(
            kernel,
            in_specs=specs,
            out_specs=[VMEM] * len(outs),
            out_shape=[shape(*out) for out in outs],
            scratch_shapes=scratch,
            cost_estimate=cost(flops, moved),
            compiler_params=pltpu.CompilerParams(vmem_limit_bytes=room << 20),
        )(*placed)

    rows = columns + corners + 8
    arguments = (weights, corner_ids, coarse_inverse, right_partner, left_partner)
    pack, load, live, scale, ids, inverse, right_map, left_map = call(
        open_kernel,
        [(array,) for array in (iface_sizes, loaded, own_map, *arguments)],
        [((rows, half), BF16), ((columns, half), F32), ((8, half), F32)]
        + [(array.shape, array.dtype) for array in arguments],
        scratch=[
            pltpu.SMEM(iface_sizes.shape, jnp.int32),
            pltpu.VMEM(loaded.shape, F32),
            pltpu.VMEM(own_map.shape, BF16),
            pltpu.SemaphoreType.DMA((8,)),
        ],
        moved=4 * rows * half,
    )
    pack_slant = lax.ppermute(pack, grid, slant)
    pack_along = lax.ppermute(pack, grid, along)
    map_across = lax.ppermute(own_map, grid, across)
    right_hot, order, left_hot, square, cross, local_left, turned = call(
        select_kernel,
        [right_map, left_map, pack, (operator,)],
        [((half, half), BF16)] * 3
        + [((block, half), BF16)] * 2
        + [((columns, block), F32), ((columns, half), BF16)],
        scratch=[pltpu.SemaphoreType.DMA((2,))],
        flops=big,
        moved=4 * half * half,
        room=14,
    )
    (send,) = call(
        first_kernel,
        [
            ids,
            square,
            cross,
            right_hot,
            order,
            local_left,
            turned,
            pack,
            map_across,
            pack_along,
            pack_slant,
        ],
        [((columns, half + 2 * LANES), BF16)],
        flops=2 * big,
        moved=4 * block * half,
        room=14,
    )
    send_slant = lax.ppermute(send, grid, slant)
    send_along = lax.ppermute(send, grid, along)
    send_across = lax.ppermute(send, grid, across)
    maps, solver, scale_right, names = call(
        order_kernel,
        [ids, inverse, order, left_hot, pack, map_across, pack_along, pack_slant],
        [
            ((LANES, 2 * half), BF16),
            ((LANES, 4 * LANES), BF16),
            ((1, half), F32),
            ((LANES, LANES), BF16),
        ],
        flops=4 * corners * half * half,
        moved=4 * half * half,
        room=8,
    )
    image, following, up, small = call(
        second_kernel,
        [
            names,
            solver,
            maps,
            right_hot,
            order,
            square,
            cross,
            live,
            load,
            scale,
            scale_right,
            send,
            send_across,
            send_along,
            send_slant,
        ],
        [
            ((columns, half), F32),
            ((columns, half), F32),
            ((columns, half + 3 * LANES), BF16),
            ((columns, LANES), F32),
        ],
        flops=2 * big,
        moved=4 * block * half,
        room=14,
    )
    far_in = shifted(small, "sub", 2)
    down_in = shifted(small, "sub", -1)
    up_in = shifted(up, "sub", 1)
    (mine,) = call(
        relay_kernel,
        [up, up_in, down_in, far_in, small],
        [((columns, half + 3 * LANES), BF16)],
        moved=8 * columns * half,
    )
    theirs = lax.ppermute(mine, grid, across)
    solution, residual = call(
        close_kernel,
        [solver, maps, live, load, scale, image, following, mine, theirs],
        [((columns, half), F32), ((columns, half), F32)],
        moved=24 * columns * half,
    )
    return solution[None], residual[None]


def per_device(*arrays):
    loads, _, dual_ops, corner_maps, coarse_inverse = arrays[:5]
    half = loads.shape[2]
    neighbourly = lax.axis_size("sub") == 4 and lax.axis_size("row") == 2
    sided = dual_ops.shape[1] == half and half % LANES == 0
    narrow = coarse_inverse.shape[0] + 4 <= LANES and 3 * corner_maps.shape[1] <= LANES
    if neighbourly and sided and narrow and ITERS == 2:
        return ring(*arrays)
    return general(*arrays)


def solution(mesh):
    placed = (
        P(("parts", "sub"), "col", None),
        P(("parts", "sub"), None),
        P(("parts", "sub"), "row", None),
        P(("parts", "sub"), None, "row"),
        P("parts", None),
        P("parts", None),
        P("parts"),
        P(("parts", "sub"), None),
        P(("parts", "sub"), None),
    )
    return jax.shard_map(
        per_device,
        mesh=mesh,
        in_specs=placed,
        out_specs=(P(("parts", "sub"), "col", None), P(("parts", "sub"), "col", None)),
        check_vma=False,
    )
```

```python
import jax
import jax.numpy as jnp
from jax import lax
from jax.experimental import pallas as pl
from jax.experimental.pallas import tpu as pltpu
from jax.sharding import PartitionSpec as P

TILE = 128
LANES = 128
ITERS = 2
F32 = jnp.float32
BF16 = jnp.bfloat16
HIGH = lax.Precision.HIGHEST
VMEM = pl.BlockSpec(memory_space=pltpu.VMEM)
HBM = pl.BlockSpec(memory_space=pltpu.HBM)


def shifted(value, axis, steps):
    count = lax.axis_size(axis)
    pairs = [(source, (source + steps) % count) for source in range(count)]
    return lax.ppermute(value, axis, pairs)


def inner(first, second, half):
    return jnp.sum(first[:, :half] * second[:, :half], axis=1)


def paired_totals(residual, precond, image, half):
    return lax.psum((inner(residual, precond, half), inner(precond, image, half)), "sub")


def tile_products(vector, rows_op, first_tile, last_tile, output):

    def one_tile(tile_at, acc):
        piece = lax.dynamic_slice_in_dim(rows_op, tile_at * TILE, TILE, 0)
        product = lax.dot_general(
            vector, piece, (((1,), (1,)), ((), ())), preferred_element_type=jnp.float32
        )
        return lax.dynamic_update_slice_in_dim(acc, product, tile_at * TILE, 1)

    return lax.fori_loop(first_tile, last_tile, one_tile, output)


def live_tiles(size_before, size_after, block_start, block, half):
    left_live = jnp.clip(size_before - block_start, 0, block)
    right_live = jnp.clip(size_after - (block_start - half), 0, block)
    live_cols = jnp.where(block_start < half, left_live, right_live)
    return (live_cols + TILE - 1) // TILE


def general(
    loads,
    weights,
    dual_ops,
    corner_maps,
    coarse_inverse,
    corner_ids,
    iface_sizes,
    left_partner,
    right_partner,
):
    half = loads.shape[2]
    block = dual_ops.shape[1]
    width = coarse_inverse.shape[0]
    subdomain = lax.axis_index("sub")
    count = lax.axis_size("sub")
    row_index = lax.axis_index("row")
    left_map = left_partner[0]
    right_map = right_partner[0]
    slots = jnp.arange(half, dtype=jnp.int32)
    size_before = iface_sizes[(subdomain + count - 1) % count]
    size_after = iface_sizes[subdomain]
    live_left = (slots < size_before).astype(jnp.float32)
    live_right = (right_map < size_after).astype(jnp.float32)
    columns = jnp.arange(width, dtype=jnp.int32)
    own_hot = (corner_ids[subdomain][:, None] == columns[None, :]).astype(jnp.float32)
    operator = dual_ops[0]
    coupling = corner_maps[0]
    block_start = row_index * block
    own_tiles = live_tiles(size_before, size_after, block_start, block, half)

    def apply_operator(vec):
        halfway = vec.astype(jnp.bfloat16)
        empty = jnp.zeros((halfway.shape[0], block), jnp.float32)
        local = tile_products(halfway, operator, jnp.int32(0), own_tiles, empty)
        own_slots = lax.dynamic_slice_in_dim(halfway, row_index * block, block, 1)
        corner = lax.dot_general(
            own_slots, coupling, (((1,), (1,)), ((), ())), preferred_element_type=jnp.float32
        )
        scattered = jnp.dot(corner, own_hot, precision=lax.Precision.HIGHEST)
        coarse = lax.psum(scattered, ("sub", "row"))
        solved = jnp.dot(coarse, coarse_inverse, precision=lax.Precision.HIGHEST)
        back = lax.dot_general(
            solved, own_hot, (((1,), (1,)), ((), ())), precision=lax.Precision.HIGHEST
        ).astype(jnp.bfloat16)
        united = local + jnp.dot(back, coupling, preferred_element_type=jnp.float32)
        whole = lax.all_gather(united.astype(jnp.bfloat16), "row", axis=1, tiled=True).astype(
            united.dtype
        )
        lower = whole[:, :half]
        upper = whole[:, half:]
        arrived_left = shifted(upper.astype(jnp.bfloat16), "sub", 1).astype(upper.dtype)
        arrived_right = shifted(lower.astype(jnp.bfloat16), "sub", -1).astype(lower.dtype)
        result_left = (lower + jnp.take(arrived_left, left_map, axis=1)) * live_left
        result_right = (upper + jnp.take(arrived_right, right_map, axis=1)) * live_right
        return jnp.concatenate([result_left, result_right], axis=1)

    received = (
        shifted(loads[0].astype(jnp.bfloat16), "sub", -1).astype(jnp.float32),
        shifted(weights.astype(jnp.bfloat16), "sub", -1).astype(weights.dtype),
    )
    right_load = jnp.take(received[0], right_map, axis=1) * live_right
    right_weight = jnp.take(received[1], right_map, axis=1)
    residual = jnp.concatenate([loads[0] * live_left, right_load], axis=1)
    scaling = jnp.concatenate([weights, right_weight], axis=1)
    solution = jnp.zeros_like(residual)
    precond = scaling * residual
    image = apply_operator(precond)
    gamma, delta = paired_totals(residual, precond, image, half)
    alpha = gamma / delta
    direction = precond
    along = image
    for step in range(ITERS):
        solution = solution + alpha[:, None] * direction
        residual = residual - alpha[:, None] * along
        if step + 1 < ITERS:
            precond = scaling * residual
            image = apply_operator(precond)
            gamma_next, delta = paired_totals(residual, precond, image, half)
            ratio = gamma_next / gamma
            alpha = gamma_next / (delta - ratio * gamma_next / alpha)
            direction = precond + ratio[:, None] * direction
            along = image + ratio[:, None] * along
            gamma = gamma_next
    return (solution[:, :half][None], residual[:, :half][None])


def cost(flops, moved):
    return pl.CostEstimate(flops=flops, bytes_accessed=moved, transcendentals=0)


def nt(first, second, precision=None):
    return lax.dot_general(
        first, second, (((1,), (1,)), ((), ())), preferred_element_type=F32, precision=precision
    )


def nn(first, second, precision=None):
    return jnp.dot(first, second, preferred_element_type=F32, precision=precision)


def halves(value):
    high = value.astype(BF16)
    return high, (value - high.astype(F32)).astype(BF16)


def stacked(value):
    return jnp.concatenate(halves(value), axis=0)


def folded(value):
    rows = value.shape[0] // 2
    return value[:rows] + value[rows:]


def thirds(value):
    high = value.astype(BF16)
    rest = value - high.astype(F32)
    middle = rest.astype(BF16)
    return high, middle, (rest - middle.astype(F32)).astype(BF16)


def pieces_sum(ref, half, count):
    total = ref[:, half : half + LANES].astype(F32)
    for piece in range(1, count):
        at = half + piece * LANES
        total = total + ref[:, at : at + LANES].astype(F32)
    return total


def neighbours():
    subdomain = lax.axis_index("sub")
    count = lax.axis_size("sub")
    return lax.rem(subdomain + count - 1, count), subdomain, lax.rem(subdomain + 1, count)


def hot_rows(ids_ref, subdomain, extent):
    ids = ids_ref[pl.ds(subdomain, 1), :]
    names = lax.broadcasted_iota(jnp.int32, (extent, ids.shape[1]), 0)
    return (names == ids).astype(F32)


def hot_names(ids_ref):
    spare = jnp.zeros((LANES, LANES - 3 * ids_ref.shape[1]), F32)
    hots = [hot_rows(ids_ref, each, LANES) for each in neighbours()]
    return jnp.concatenate([*hots, spare], axis=1)


def selected(values, names):
    high, middle, low = thirds(values)
    rows = values.shape[0]
    parts = nt(jnp.concatenate([high, middle, low], axis=0), names)
    return parts[:rows] + parts[rows : 2 * rows] + parts[2 * rows :]


def solved_backs(coarse, solver):
    rows = coarse.shape[0]
    parts = nn(stacked(coarse), solver)
    width = solver.shape[1] // 2
    return parts[:rows, :width] + (parts[:rows, width:] + parts[rows:, :width])


def open_kernel(
    sizes_in,
    loads_in,
    maps_in,
    weights_in,
    ids_in,
    inverse_in,
    right_in,
    left_in,
    pack_ref,
    loaded_ref,
    live_ref,
    weights_ref,
    ids_ref,
    inverse_ref,
    right_ref,
    left_ref,
    sizes_ref,
    loads_ref,
    maps_ref,
    sems,
):
    pairs = (
        (sizes_in, sizes_ref),
        (loads_in, loads_ref),
        (weights_in, weights_ref),
        (maps_in, maps_ref),
        (ids_in, ids_ref),
        (inverse_in, inverse_ref),
        (right_in, right_ref),
        (left_in, left_ref),
    )
    copies = [pltpu.make_async_copy(*pair, sems.at[at]) for at, pair in enumerate(pairs)]
    for copy in copies:
        copy.start()
    before, subdomain, _ = neighbours()
    for copy in copies:
        copy.wait()
    slots = lax.broadcasted_iota(jnp.int32, live_ref.shape, 1)
    which = lax.broadcasted_iota(jnp.int32, live_ref.shape, 0)
    bound = jnp.where(which == 0, sizes_ref[before], sizes_ref[subdomain])
    live = (slots < bound).astype(F32)
    live_ref[...] = live
    scale = weights_ref[...]
    loaded = jnp.where(live[0:1] > 0.0, loads_ref[...], 0.0)
    loaded_ref[...] = loaded
    first = loaded * scale
    high = scale.astype(BF16).astype(F32)
    spare = jnp.where(which == 0, high, jnp.where(which == 1, scale - high, 0.0))
    pack_ref[...] = jnp.concatenate([first, maps_ref[...].astype(F32), spare], axis=0).astype(BF16)


def side_columns(ref, side, half):
    return ref.at[:, pl.ds(pl.multiple_of(side * half, half), half)]


def turn(source_ref, target_ref):
    for at in range(0, source_ref.shape[1], LANES):
        block = slice(at, at + LANES)
        target_ref[block, :] = jnp.transpose(source_ref[:, block])


def select_kernel(
    right_ref,
    left_ref,
    pack_ref,
    operator_in,
    right_hot_ref,
    order_ref,
    left_hot_ref,
    square_ref,
    cross_ref,
    early_ref,
    local_ref,
    turned_ref,
    sems,
):
    half = right_ref.shape[1]
    columns = local_ref.shape[0]
    side = lax.axis_index("row")
    lower = side == 0
    square = pltpu.make_async_copy(side_columns(operator_in, side, half), square_ref, sems.at[0])
    cross = pltpu.make_async_copy(side_columns(operator_in, 1 - side, half), cross_ref, sems.at[1])

    @pl.when(lower)
    def _():
        square.start()
        cross.start()

    @pl.when(jnp.logical_not(lower))
    def _():
        cross.start()
        square.start()

    short = jnp.int16
    right = right_ref[...]
    tall = jnp.transpose(jnp.broadcast_to(right, (8, half)).astype(F32))[:, 0:1].astype(jnp.int32)
    tall = jnp.broadcast_to(tall, (half, LANES)).astype(short)
    names = lax.broadcasted_iota(jnp.int32, (LANES, LANES), 1)
    full, none = jnp.ones((LANES, half), BF16), jnp.zeros((LANES, half), BF16)
    narrow_full, narrow_none = jnp.ones((LANES, LANES), BF16), jnp.zeros((LANES, LANES), BF16)
    for at in range(half // LANES):
        rows = slice(at * LANES, (at + 1) * LANES)
        for block in range(half // LANES):
            own = (names + block * LANES).astype(short)
            hit = own == tall[rows]
            columns_at = slice(block * LANES, (block + 1) * LANES)
            order_ref[rows, columns_at] = jnp.where(hit, narrow_full, narrow_none)
    wide_right = jnp.broadcast_to(right, (LANES, half)).astype(short)
    wide_left = jnp.broadcast_to(left_ref[...], (LANES, half)).astype(short)

    def one(at, carry):
        start = pl.multiple_of(at * LANES, LANES)
        slots = (lax.broadcasted_iota(jnp.int32, (LANES, half), 0) + start).astype(short)
        rows = pl.ds(start, LANES)
        right_hot_ref[rows, :] = jnp.where(slots == wide_right, full, none)
        left_hot_ref[rows, :] = jnp.where(slots == wide_left, full, none)
        return carry

    lax.fori_loop(0, half // LANES, one, 0)
    left = pack_ref[:columns, :]

    @pl.when(lower)
    def _():
        turned_ref[...] = left
        square.wait()
        local_ref[...] = nn(left, square_ref[...])
        cross.wait()
        turn(cross_ref, early_ref)

    @pl.when(jnp.logical_not(lower))
    def _():
        turned_ref[...] = nt(left, left_hot_ref[...]).astype(BF16)
        cross.wait()
        local_ref[...] = nt(left, cross_ref[...])
        square.wait()


def first_kernel(
    ids_ref,
    square_ref,
    early_ref,
    right_hot_ref,
    order_ref,
    local_ref,
    turned_ref,
    own_pack_ref,
    across_ref,
    along_ref,
    slant_ref,
    send_ref,
):
    columns, half = local_ref.shape
    corners = ids_ref.shape[1]
    before, subdomain, after = neighbours()
    lower = lax.axis_index("row") == 0
    def coarse_part(own_side, other_side, other):
        one = nt(own_side, across_ref[...])
        two = nt(other_side, along_ref[columns:, :])[:, :corners]
        hot_own = hot_rows(ids_ref, subdomain, LANES)
        hot_other = hot_rows(ids_ref, other, LANES)
        high, low = halves(selected(one, hot_own) + selected(two, hot_other))
        send_ref[:, half:] = jnp.concatenate([high, low], axis=1)

    @pl.when(lower)
    def _():
        right = along_ref[:columns, :]
        slotted = nn(right, right_hot_ref[...]).astype(BF16)
        coarse_part(slotted, right, after)
        send_ref[:, :half] = (local_ref[...] + nn(slotted, early_ref[...])).astype(BF16)

    @pl.when(jnp.logical_not(lower))
    def _():
        slotted = nn(slant_ref[:columns, :], right_hot_ref[...]).astype(BF16)
        coarse_part(own_pack_ref[:columns, :], turned_ref[...], before)
        local = (local_ref[...] + nn(slotted, square_ref[...])).astype(BF16)
        send_ref[:, :half] = nn(local, order_ref[...]).astype(BF16)


def order_kernel(
    ids_ref,
    inverse_ref,
    order_ref,
    left_hot_ref,
    cross_ref,
    own_pack_ref,
    across_ref,
    along_ref,
    slant_ref,
    maps_ref,
    solver_ref,
    scale_ref,
    names_ref,
    late_ref,
):
    half = order_ref.shape[1]
    corners = ids_ref.shape[1]
    width = inverse_ref.shape[0]
    columns = own_pack_ref.shape[0] - corners - 8
    lower = lax.axis_index("row") == 0
    own, across = own_pack_ref[columns:, :].astype(F32)[:corners], across_ref[...].astype(F32)
    along, slant = along_ref[columns:, :].astype(F32), slant_ref[columns:, :].astype(F32)
    ahead, behind = jnp.where(lower, along, slant), jnp.where(lower, slant, along)
    scale_ref[...] = ahead[corners : corners + 1] + ahead[corners + 1 : corners + 2]
    raw = jnp.where(lower, across, own).astype(BF16)
    ordered = nn(raw, order_ref[...])
    turned = nn(behind[:corners].astype(BF16), left_hot_ref[...])
    spare = jnp.zeros((LANES - 3 * corners, half), F32)
    blank = jnp.zeros((corners, half), F32)
    mine = jnp.where(lower, own, across)
    maps_ref[:, :half] = jnp.concatenate([turned, mine, blank, spare], axis=0).astype(BF16)
    maps_ref[:, half:] = jnp.concatenate([blank, ordered, ahead[:corners], spare], axis=0).astype(BF16)
    names = hot_names(ids_ref)
    names_ref[...] = names.astype(BF16)
    backs = nn(inverse_ref[...], names[:width], HIGH)
    low_rows = jnp.zeros((LANES - width, LANES), F32)
    side = jnp.concatenate([inverse_ref[...], jnp.zeros((width, LANES - width), F32)], axis=1)
    pieces = []
    for piece in (backs, side):
        tall = jnp.concatenate([piece, low_rows], axis=0)
        pieces.extend(halves(tall))
    solver_ref[...] = jnp.concatenate(pieces, axis=1)

    @pl.when(jnp.logical_not(lower))
    def _():
        turn(cross_ref, late_ref)


def second_kernel(
    names_ref,
    solver_ref,
    maps_ref,
    right_hot_ref,
    order_ref,
    square_ref,
    early_ref,
    late_ref,
    live_ref,
    loaded_ref,
    weights_ref,
    scale_ref,
    own_ref,
    across_ref,
    along_ref,
    slant_ref,
    image_ref,
    next_ref,
    up_ref,
    small_ref,
):
    lower = lax.axis_index("row") == 0
    columns, half = loaded_ref.shape
    own, across = own_ref[:, :half].astype(F32), across_ref[:, :half].astype(F32)
    along, slant = along_ref[:, :half].astype(F32), slant_ref[:, :half].astype(F32)
    mine = pieces_sum(own_ref, half, 2) + pieces_sum(across_ref, half, 2)
    coarse = mine + (pieces_sum(along_ref, half, 2) + pieces_sum(slant_ref, half, 2))
    backs = solved_backs(coarse, solver_ref[:, : 2 * LANES]).astype(BF16)
    fix = nn(backs, maps_ref[...])
    image = jnp.where(lower, own, across) + jnp.where(lower, slant, along) + fix[:, :half]
    image = jnp.where(live_ref[0:1] > 0.0, image, 0.0)
    image_right = jnp.where(lower, across, own) + jnp.where(lower, along, slant) + fix[:, half:]
    image_right = jnp.where(live_ref[1:2] > 0.0, image_right, 0.0)
    left = weights_ref[...] * image
    right = scale_ref[...] * image_right
    image_ref[...] = image
    next_ref[...] = left
    left_2, right_2 = stacked(left), stacked(right)
    loaded = loaded_ref[...]
    first = loaded * weights_ref[...]
    sums = [
        jnp.sum(loaded * first, axis=1, keepdims=True),
        jnp.sum(first * image, axis=1, keepdims=True),
        jnp.sum(image * left, axis=1, keepdims=True),
    ]
    lane = lax.broadcasted_iota(jnp.int32, (columns, LANES), 1)

    def totals(block, local, corner):
        energy = jnp.sum(block * local, axis=1, keepdims=True)
        small = selected(folded(corner), names_ref[...])
        for at, value in enumerate([*sums, energy]):
            small = jnp.where(lane == LANES - len(sums) - 1 + at, value, small)
        small_ref[...] = small
        up_ref[:, half:] = jnp.concatenate(thirds(small), axis=1)

    @pl.when(lower)
    def _():
        local = nn(left_2, square_ref[...])
        slotted_2 = nn(right_2, right_hot_ref[...]).astype(BF16)
        corner = nt(right_2, maps_ref[:, half:])
        local = folded(local + nn(slotted_2, early_ref[...]))
        up_ref[:, :half] = local.astype(BF16)
        totals(folded(left_2.astype(F32)), local, corner)

    @pl.when(jnp.logical_not(lower))
    def _():
        slotted_2 = nn(right_2, right_hot_ref[...]).astype(BF16)
        local = nn(left_2, late_ref[...])
        corner = nt(left_2, maps_ref[:, :half])
        local = folded(local + nn(slotted_2, square_ref[...]))
        up_ref[:, :half] = nn(local.astype(BF16), order_ref[...]).astype(BF16)
        totals(folded(slotted_2.astype(F32)), local, corner)


def relay_kernel(up_own_ref, up_ref, down_ref, far_ref, own_ref, out_ref):
    lower = lax.axis_index("row") == 0
    half = up_ref.shape[1] - 3 * LANES
    total = own_ref[...] + pieces_sum(up_ref, half, 3)
    total = total + down_ref[...] + far_ref[...]
    out_ref[:, :half] = jnp.where(lower, up_own_ref[:, :half], up_ref[:, :half])
    out_ref[:, half:] = jnp.concatenate(thirds(total), axis=1)


def close_kernel(
    solver_ref,
    maps_ref,
    live_ref,
    loaded_ref,
    weights_ref,
    image_ref,
    next_ref,
    mine_ref,
    theirs_ref,
    solution_ref,
    residual_ref,
):
    lower = lax.axis_index("row") == 0
    columns, half = loaded_ref.shape
    mine, theirs = pieces_sum(mine_ref, half, 3), pieces_sum(theirs_ref, half, 3)
    total = jnp.where(lower, mine, theirs)
    lane = lax.broadcasted_iota(jnp.int32, (columns, LANES), 1)
    coarse = jnp.where(lane < LANES - 4, total, 0.0)
    backs = solved_backs(coarse, solver_ref[:, : 2 * LANES]).astype(BF16)
    solved = solved_backs(coarse, solver_ref[:, 2 * LANES :])
    fix = nn(backs, maps_ref[:, :half])
    image_next = mine_ref[:, :half].astype(F32) + theirs_ref[:, :half].astype(F32) + fix
    image_next = jnp.where(live_ref[0:1] > 0.0, image_next, 0.0)

    def column(values, at):
        return jnp.sum(jnp.where(lane == LANES - 4 + at, values, 0.0), axis=1, keepdims=True)

    gamma = column(total, 0)
    delta = column(total, 1)
    cross = column(total, 2)
    energy = column(mine + theirs, 3) + jnp.sum(coarse * solved, axis=1, keepdims=True)
    alpha = gamma / delta
    gamma_next = gamma - 2.0 * alpha * delta + alpha * alpha * cross
    ratio = gamma_next / gamma
    grown = 1.0 + ratio
    curvature = grown * grown * delta - 2.0 * grown * alpha * cross + alpha * alpha * energy
    alpha_next = gamma_next / curvature
    loaded = loaded_ref[...]
    first = loaded * weights_ref[...]
    direction = grown * first - alpha * next_ref[...]
    along = grown * image_ref[...] - alpha * image_next
    solution_ref[...] = alpha * first + alpha_next * direction
    residual_ref[...] = loaded - alpha * image_ref[...] - alpha_next * along


def ring(
    loads,
    weights,
    dual_ops,
    corner_maps,
    coarse_inverse,
    corner_ids,
    iface_sizes,
    left_partner,
    right_partner,
):
    count = lax.axis_size("sub")
    sides = lax.axis_size("row")
    columns, half = loads.shape[1:]
    corners = corner_maps.shape[1]
    operator = dual_ops[0]
    own_map = corner_maps[0]
    loaded = loads[0]
    block = operator.shape[0]
    shape = jax.ShapeDtypeStruct
    grid = ("sub", "row")
    big = 2 * columns * block * 2 * half

    def pairs(target):
        listed = []
        for at in range(count):
            for side in range(sides):
                to_at, to_side = target(at, side)
                listed.append((at * sides + side, (to_at % count) * sides + to_side))
        return listed

    across = pairs(lambda at, side: (at, 1 - side))
    along = pairs(lambda at, side: (at - 1, 0) if side == 0 else (at + 1, 1))
    slant = pairs(lambda at, side: (at - 1, 1) if side == 0 else (at + 1, 0))

    def call(kernel, operands, outs, scratch=(), flops=0, moved=0, room=4):
        specs, placed = [], []
        for operand in operands:
            held = isinstance(operand, tuple)
            specs.append(HBM if held else VMEM)
            placed.append(
                pltpu.with_memory_space_constraint(operand[0], pltpu.HBM) if held else operand
            )
        return pl.pallas_call(
            kernel,
            in_specs=specs,
            out_specs=[VMEM] * len(outs),
            out_shape=[shape(*out) for out in outs],
            scratch_shapes=scratch,
            cost_estimate=cost(flops, moved),
            compiler_params=pltpu.CompilerParams(vmem_limit_bytes=room << 20),
        )(*placed)

    rows = columns + corners + 8
    arguments = (weights, corner_ids, coarse_inverse, right_partner, left_partner)
    pack, load, live, scale, ids, inverse, right_map, left_map = call(
        open_kernel,
        [(array,) for array in (iface_sizes, loaded, own_map, *arguments)],
        [((rows, half), BF16), ((columns, half), F32), ((8, half), F32)]
        + [(array.shape, array.dtype) for array in arguments],
        scratch=[
            pltpu.SMEM(iface_sizes.shape, jnp.int32),
            pltpu.VMEM(loaded.shape, F32),
            pltpu.VMEM(own_map.shape, BF16),
            pltpu.SemaphoreType.DMA((8,)),
        ],
        moved=4 * rows * half,
    )
    pack_slant = lax.ppermute(pack, grid, slant)
    pack_along = lax.ppermute(pack, grid, along)
    map_across = lax.ppermute(own_map, grid, across)
    right_hot, order, left_hot, square, cross, early, local_left, turned = call(
        select_kernel,
        [right_map, left_map, pack, (operator,)],
        [((half, half), BF16)] * 3
        + [((block, half), BF16)] * 3
        + [((columns, block), F32), ((columns, half), BF16)],
        scratch=[pltpu.SemaphoreType.DMA((2,))],
        flops=big,
        moved=4 * half * half,
        room=16,
    )
    (send,) = call(
        first_kernel,
        [
            ids,
            square,
            early,
            right_hot,
            order,
            local_left,
            turned,
            pack,
            map_across,
            pack_along,
            pack_slant,
        ],
        [((columns, half + 2 * LANES), BF16)],
        flops=2 * big,
        moved=4 * block * half,
        room=16,
    )
    send_slant = lax.ppermute(send, grid, slant)
    send_along = lax.ppermute(send, grid, along)
    send_across = lax.ppermute(send, grid, across)
    maps, solver, scale_right, names, late = call(
        order_kernel,
        [ids, inverse, order, left_hot, cross, pack, map_across, pack_along, pack_slant],
        [
            ((LANES, 2 * half), BF16),
            ((LANES, 4 * LANES), BF16),
            ((1, half), F32),
            ((LANES, LANES), BF16),
            ((half, block), BF16),
        ],
        flops=4 * corners * half * half,
        moved=4 * half * half,
        room=12,
    )
    image, following, up, small = call(
        second_kernel,
        [
            names,
            solver,
            maps,
            right_hot,
            order,
            square,
            early,
            late,
            live,
            load,
            scale,
            scale_right,
            send,
            send_across,
            send_along,
            send_slant,
        ],
        [
            ((columns, half), F32),
            ((columns, half), F32),
            ((columns, half + 3 * LANES), BF16),
            ((columns, LANES), F32),
        ],
        flops=2 * big,
        moved=4 * block * half,
        room=16,
    )
    far_in = shifted(small, "sub", 2)
    down_in = shifted(small, "sub", -1)
    up_in = shifted(up, "sub", 1)
    (mine,) = call(
        relay_kernel,
        [up, up_in, down_in, far_in, small],
        [((columns, half + 3 * LANES), BF16)],
        moved=8 * columns * half,
    )
    theirs = lax.ppermute(mine, grid, across)
    solution, residual = call(
        close_kernel,
        [solver, maps, live, load, scale, image, following, mine, theirs],
        [((columns, half), F32), ((columns, half), F32)],
        moved=24 * columns * half,
    )
    return solution[None], residual[None]


def per_device(*arrays):
    loads, _, dual_ops, corner_maps, coarse_inverse = arrays[:5]
    half = loads.shape[2]
    neighbourly = lax.axis_size("sub") == 4 and lax.axis_size("row") == 2
    sided = dual_ops.shape[1] == half and half % LANES == 0
    narrow = coarse_inverse.shape[0] + 4 <= LANES and 3 * corner_maps.shape[1] <= LANES
    if neighbourly and sided and narrow and ITERS == 2:
        return ring(*arrays)
    return general(*arrays)


def solution(mesh):
    placed = (
        P(("parts", "sub"), "col", None),
        P(("parts", "sub"), None),
        P(("parts", "sub"), "row", None),
        P(("parts", "sub"), None, "row"),
        P("parts", None),
        P("parts", None),
        P("parts"),
        P(("parts", "sub"), None),
        P(("parts", "sub"), None),
    )
    return jax.shard_map(
        per_device,
        mesh=mesh,
        in_specs=placed,
        out_specs=(P(("parts", "sub"), "col", None), P(("parts", "sub"), "col", None)),
        check_vma=False,
    )
```

```python
import jax
import jax.numpy as jnp
from jax import lax
from jax.experimental import pallas as pl
from jax.experimental.pallas import tpu as pltpu
from jax.sharding import PartitionSpec as P

TILE = 128
LANES = 128
ITERS = 2
F32 = jnp.float32
BF16 = jnp.bfloat16
HIGH = lax.Precision.HIGHEST
VMEM = pl.BlockSpec(memory_space=pltpu.VMEM)
HBM = pl.BlockSpec(memory_space=pltpu.HBM)


def shifted(value, axis, steps):
    count = lax.axis_size(axis)
    pairs = [(source, (source + steps) % count) for source in range(count)]
    return lax.ppermute(value, axis, pairs)


def inner(first, second, half):
    return jnp.sum(first[:, :half] * second[:, :half], axis=1)


def paired_totals(residual, precond, image, half):
    return lax.psum((inner(residual, precond, half), inner(precond, image, half)), "sub")


def tile_products(vector, rows_op, first_tile, last_tile, output):

    def one_tile(tile_at, acc):
        piece = lax.dynamic_slice_in_dim(rows_op, tile_at * TILE, TILE, 0)
        product = lax.dot_general(
            vector, piece, (((1,), (1,)), ((), ())), preferred_element_type=jnp.float32
        )
        return lax.dynamic_update_slice_in_dim(acc, product, tile_at * TILE, 1)

    return lax.fori_loop(first_tile, last_tile, one_tile, output)


def live_tiles(size_before, size_after, block_start, block, half):
    left_live = jnp.clip(size_before - block_start, 0, block)
    right_live = jnp.clip(size_after - (block_start - half), 0, block)
    live_cols = jnp.where(block_start < half, left_live, right_live)
    return (live_cols + TILE - 1) // TILE


def general(
    loads,
    weights,
    dual_ops,
    corner_maps,
    coarse_inverse,
    corner_ids,
    iface_sizes,
    left_partner,
    right_partner,
):
    half = loads.shape[2]
    block = dual_ops.shape[1]
    width = coarse_inverse.shape[0]
    subdomain = lax.axis_index("sub")
    count = lax.axis_size("sub")
    row_index = lax.axis_index("row")
    left_map = left_partner[0]
    right_map = right_partner[0]
    slots = jnp.arange(half, dtype=jnp.int32)
    size_before = iface_sizes[(subdomain + count - 1) % count]
    size_after = iface_sizes[subdomain]
    live_left = (slots < size_before).astype(jnp.float32)
    live_right = (right_map < size_after).astype(jnp.float32)
    columns = jnp.arange(width, dtype=jnp.int32)
    own_hot = (corner_ids[subdomain][:, None] == columns[None, :]).astype(jnp.float32)
    operator = dual_ops[0]
    coupling = corner_maps[0]
    block_start = row_index * block
    own_tiles = live_tiles(size_before, size_after, block_start, block, half)

    def apply_operator(vec):
        halfway = vec.astype(jnp.bfloat16)
        empty = jnp.zeros((halfway.shape[0], block), jnp.float32)
        local = tile_products(halfway, operator, jnp.int32(0), own_tiles, empty)
        own_slots = lax.dynamic_slice_in_dim(halfway, row_index * block, block, 1)
        corner = lax.dot_general(
            own_slots, coupling, (((1,), (1,)), ((), ())), preferred_element_type=jnp.float32
        )
        scattered = jnp.dot(corner, own_hot, precision=lax.Precision.HIGHEST)
        coarse = lax.psum(scattered, ("sub", "row"))
        solved = jnp.dot(coarse, coarse_inverse, precision=lax.Precision.HIGHEST)
        back = lax.dot_general(
            solved, own_hot, (((1,), (1,)), ((), ())), precision=lax.Precision.HIGHEST
        ).astype(jnp.bfloat16)
        united = local + jnp.dot(back, coupling, preferred_element_type=jnp.float32)
        whole = lax.all_gather(united.astype(jnp.bfloat16), "row", axis=1, tiled=True).astype(
            united.dtype
        )
        lower = whole[:, :half]
        upper = whole[:, half:]
        arrived_left = shifted(upper.astype(jnp.bfloat16), "sub", 1).astype(upper.dtype)
        arrived_right = shifted(lower.astype(jnp.bfloat16), "sub", -1).astype(lower.dtype)
        result_left = (lower + jnp.take(arrived_left, left_map, axis=1)) * live_left
        result_right = (upper + jnp.take(arrived_right, right_map, axis=1)) * live_right
        return jnp.concatenate([result_left, result_right], axis=1)

    received = (
        shifted(loads[0].astype(jnp.bfloat16), "sub", -1).astype(jnp.float32),
        shifted(weights.astype(jnp.bfloat16), "sub", -1).astype(weights.dtype),
    )
    right_load = jnp.take(received[0], right_map, axis=1) * live_right
    right_weight = jnp.take(received[1], right_map, axis=1)
    residual = jnp.concatenate([loads[0] * live_left, right_load], axis=1)
    scaling = jnp.concatenate([weights, right_weight], axis=1)
    solution = jnp.zeros_like(residual)
    precond = scaling * residual
    image = apply_operator(precond)
    gamma, delta = paired_totals(residual, precond, image, half)
    alpha = gamma / delta
    direction = precond
    along = image
    for step in range(ITERS):
        solution = solution + alpha[:, None] * direction
        residual = residual - alpha[:, None] * along
        if step + 1 < ITERS:
            precond = scaling * residual
            image = apply_operator(precond)
            gamma_next, delta = paired_totals(residual, precond, image, half)
            ratio = gamma_next / gamma
            alpha = gamma_next / (delta - ratio * gamma_next / alpha)
            direction = precond + ratio[:, None] * direction
            along = image + ratio[:, None] * along
            gamma = gamma_next
    return (solution[:, :half][None], residual[:, :half][None])


def cost(flops, moved):
    return pl.CostEstimate(flops=flops, bytes_accessed=moved, transcendentals=0)


def nt(first, second, precision=None):
    return lax.dot_general(
        first, second, (((1,), (1,)), ((), ())), preferred_element_type=F32, precision=precision
    )


def nn(first, second, precision=None):
    return jnp.dot(first, second, preferred_element_type=F32, precision=precision)


def halves(value):
    high = value.astype(BF16)
    return high, (value - high.astype(F32)).astype(BF16)


def stacked(value):
    return jnp.concatenate(halves(value), axis=0)


def folded(value):
    rows = value.shape[0] // 2
    return value[:rows] + value[rows:]


def thirds(value):
    high = value.astype(BF16)
    rest = value - high.astype(F32)
    middle = rest.astype(BF16)
    return high, middle, (rest - middle.astype(F32)).astype(BF16)


def pieces_sum(ref, half, count):
    total = ref[:, half : half + LANES].astype(F32)
    for piece in range(1, count):
        at = half + piece * LANES
        total = total + ref[:, at : at + LANES].astype(F32)
    return total


def neighbours():
    subdomain = lax.axis_index("sub")
    count = lax.axis_size("sub")
    return lax.rem(subdomain + count - 1, count), subdomain, lax.rem(subdomain + 1, count)


def hot_rows(ids_ref, subdomain, extent):
    ids = ids_ref[pl.ds(subdomain, 1), :]
    names = lax.broadcasted_iota(jnp.int32, (extent, ids.shape[1]), 0)
    return (names == ids).astype(F32)


def hot_names(ids_ref):
    spare = jnp.zeros((LANES, LANES - 3 * ids_ref.shape[1]), F32)
    hots = [hot_rows(ids_ref, each, LANES) for each in neighbours()]
    return jnp.concatenate([*hots, spare], axis=1)


def selected(values, names):
    high, middle, low = thirds(values)
    rows = values.shape[0]
    parts = nt(jnp.concatenate([high, middle, low], axis=0), names)
    return parts[:rows] + parts[rows : 2 * rows] + parts[2 * rows :]


def solved_backs(coarse, solver):
    rows = coarse.shape[0]
    parts = nn(stacked(coarse), solver)
    width = solver.shape[1] // 2
    return parts[:rows, :width] + (parts[:rows, width:] + parts[rows:, :width])


def open_kernel(
    sizes_in,
    loads_in,
    maps_in,
    weights_in,
    ids_in,
    inverse_in,
    right_in,
    left_in,
    pack_ref,
    skew_ref,
    loaded_ref,
    live_ref,
    weights_ref,
    ids_ref,
    inverse_ref,
    right_ref,
    left_ref,
    sizes_ref,
    loads_ref,
    maps_ref,
    sems,
):
    pairs = (
        (sizes_in, sizes_ref),
        (loads_in, loads_ref),
        (weights_in, weights_ref),
        (maps_in, maps_ref),
        (ids_in, ids_ref),
        (inverse_in, inverse_ref),
        (right_in, right_ref),
        (left_in, left_ref),
    )
    copies = [pltpu.make_async_copy(*pair, sems.at[at]) for at, pair in enumerate(pairs)]
    for copy in copies:
        copy.start()
    before, subdomain, _ = neighbours()
    for copy in copies:
        copy.wait()
    slots = lax.broadcasted_iota(jnp.int32, live_ref.shape, 1)
    which = lax.broadcasted_iota(jnp.int32, live_ref.shape, 0)
    bound = jnp.where(which == 0, sizes_ref[before], sizes_ref[subdomain])
    live = (slots < bound).astype(F32)
    live_ref[...] = live
    scale = weights_ref[...]
    loaded = jnp.where(live[0:1] > 0.0, loads_ref[...], 0.0)
    loaded_ref[...] = loaded
    first = loaded * scale
    high = scale.astype(BF16).astype(F32)
    spare = jnp.where(which == 0, high, jnp.where(which == 1, scale - high, 0.0))
    maps = maps_ref[...].astype(F32)
    pack_ref[...] = jnp.concatenate([first, maps, spare], axis=0).astype(BF16)
    short = jnp.concatenate([first, spare], axis=0)
    skew_ref[...] = jnp.where(lax.axis_index("row") == 0, short, maps).astype(BF16)


def side_columns(ref, side, half):
    return ref.at[:, pl.ds(pl.multiple_of(side * half, half), half)]


def turn(source_ref, target_ref):
    for at in range(0, source_ref.shape[1], LANES):
        block = slice(at, at + LANES)
        target_ref[block, :] = jnp.transpose(source_ref[:, block])


def select_kernel(
    right_ref,
    left_ref,
    pack_ref,
    operator_in,
    right_hot_ref,
    order_ref,
    left_hot_ref,
    square_ref,
    cross_ref,
    early_ref,
    local_ref,
    turned_ref,
    sems,
):
    half = right_ref.shape[1]
    columns = local_ref.shape[0]
    side = lax.axis_index("row")
    lower = side == 0
    square = pltpu.make_async_copy(side_columns(operator_in, side, half), square_ref, sems.at[0])
    cross = pltpu.make_async_copy(side_columns(operator_in, 1 - side, half), cross_ref, sems.at[1])

    @pl.when(lower)
    def _():
        square.start()
        cross.start()

    @pl.when(jnp.logical_not(lower))
    def _():
        cross.start()
        square.start()

    short = jnp.int16
    right = right_ref[...]
    tall = jnp.transpose(jnp.broadcast_to(right, (8, half)).astype(F32))[:, 0:1].astype(jnp.int32)
    tall = jnp.broadcast_to(tall, (half, LANES)).astype(short)
    names = lax.broadcasted_iota(jnp.int32, (LANES, LANES), 1)
    full, none = jnp.ones((LANES, half), BF16), jnp.zeros((LANES, half), BF16)
    narrow_full, narrow_none = jnp.ones((LANES, LANES), BF16), jnp.zeros((LANES, LANES), BF16)
    for at in range(half // LANES):
        rows = slice(at * LANES, (at + 1) * LANES)
        for block in range(half // LANES):
            own = (names + block * LANES).astype(short)
            hit = own == tall[rows]
            columns_at = slice(block * LANES, (block + 1) * LANES)
            order_ref[rows, columns_at] = jnp.where(hit, narrow_full, narrow_none)
    wide_right = jnp.broadcast_to(right, (LANES, half)).astype(short)
    wide_left = jnp.broadcast_to(left_ref[...], (LANES, half)).astype(short)

    def one(at, carry):
        start = pl.multiple_of(at * LANES, LANES)
        slots = (lax.broadcasted_iota(jnp.int32, (LANES, half), 0) + start).astype(short)
        rows = pl.ds(start, LANES)
        right_hot_ref[rows, :] = jnp.where(slots == wide_right, full, none)
        left_hot_ref[rows, :] = jnp.where(slots == wide_left, full, none)
        return carry

    lax.fori_loop(0, half // LANES, one, 0)
    left = pack_ref[:columns, :]

    @pl.when(lower)
    def _():
        turned_ref[...] = left
        square.wait()
        local_ref[...] = nn(left, square_ref[...])
        cross.wait()
        turn(cross_ref, early_ref)

    @pl.when(jnp.logical_not(lower))
    def _():
        turned_ref[...] = nt(left, left_hot_ref[...]).astype(BF16)
        cross.wait()
        local_ref[...] = nt(left, cross_ref[...])
        square.wait()


def first_kernel(
    ids_ref,
    square_ref,
    early_ref,
    right_hot_ref,
    order_ref,
    local_ref,
    turned_ref,
    own_pack_ref,
    across_ref,
    along_ref,
    slant_ref,
    send_ref,
    pair_ref,
):
    columns, half = local_ref.shape
    corners = ids_ref.shape[1]
    before, subdomain, after = neighbours()
    lower = lax.axis_index("row") == 0

    def coarse_part(own_side, other_side, other):
        one = nt(own_side, across_ref[...])
        two = nt(other_side, along_ref[columns:, :])[:, :corners]
        hot_own = hot_rows(ids_ref, subdomain, LANES)
        hot_other = hot_rows(ids_ref, other, LANES)
        high, low = halves(selected(one, hot_own) + selected(two, hot_other))
        send_ref[:, half:] = jnp.concatenate([high, low], axis=1)

    @pl.when(lower)
    def _():
        right = along_ref[:columns, :]
        slotted = nn(right, right_hot_ref[...]).astype(BF16)
        coarse_part(slotted, right, after)
        send_ref[:, :half] = (local_ref[...] + nn(slotted, early_ref[...])).astype(BF16)

    @pl.when(jnp.logical_not(lower))
    def _():
        slotted = nn(slant_ref[:columns, :], right_hot_ref[...]).astype(BF16)
        coarse_part(own_pack_ref[:columns, :], turned_ref[...], before)
        local = (local_ref[...] + nn(slotted, square_ref[...])).astype(BF16)
        send_ref[:, :half] = nn(local, order_ref[...]).astype(BF16)

    wide = send_ref.shape[1]
    relayed = along_ref[columns : columns + corners, :].astype(F32)
    tail = relayed[columns:]
    tail = jnp.concatenate([tail[:, : half // 2], tail[:, half // 2 :]], axis=0)
    pair_ref[:, :wide] = send_ref[...]
    pair_ref[:, wide:] = jnp.concatenate([relayed[:columns], tail], axis=1).astype(BF16)


def order_kernel(
    ids_ref,
    inverse_ref,
    order_ref,
    left_hot_ref,
    cross_ref,
    own_pack_ref,
    across_ref,
    along_ref,
    slant_ref,
    maps_ref,
    solver_ref,
    scale_ref,
    names_ref,
    late_ref,
):
    half = order_ref.shape[1]
    corners = ids_ref.shape[1]
    width = inverse_ref.shape[0]
    columns = own_pack_ref.shape[0] - corners - 8
    lower = lax.axis_index("row") == 0
    own, across = own_pack_ref[columns:, :].astype(F32)[:corners], across_ref[...].astype(F32)
    along, slant = along_ref[columns:, :].astype(F32), slant_ref[...].astype(F32)
    behind = jnp.where(lower, slant, along[:corners])
    ahead = jnp.where(lower, along[:corners], 0.0)
    scales = jnp.where(lower, along[corners:], slant[columns:])
    scale_ref[...] = scales[0:1] + scales[1:2]
    raw = jnp.where(lower, across, own).astype(BF16)
    ordered = nn(raw, order_ref[...])
    turned = nn(behind.astype(BF16), left_hot_ref[...])
    spare = jnp.zeros((LANES - 3 * corners, half), F32)
    blank = jnp.zeros((corners, half), F32)
    mine = jnp.where(lower, own, across)
    maps_ref[:, :half] = jnp.concatenate([turned, mine, blank, spare], axis=0).astype(BF16)
    maps_ref[:, half:] = jnp.concatenate([blank, ordered, ahead, spare], axis=0).astype(BF16)
    names = hot_names(ids_ref)
    names_ref[...] = names.astype(BF16)
    backs = nn(inverse_ref[...], names[:width], HIGH)
    low_rows = jnp.zeros((LANES - width, LANES), F32)
    side = jnp.concatenate([inverse_ref[...], jnp.zeros((width, LANES - width), F32)], axis=1)
    pieces = []
    for piece in (backs, side):
        tall = jnp.concatenate([piece, low_rows], axis=0)
        pieces.extend(halves(tall))
    solver_ref[...] = jnp.concatenate(pieces, axis=1)

    @pl.when(jnp.logical_not(lower))
    def _():
        turn(cross_ref, late_ref)


def second_kernel(
    names_ref,
    solver_ref,
    maps_ref,
    right_hot_ref,
    order_ref,
    square_ref,
    early_ref,
    late_ref,
    live_ref,
    loaded_ref,
    weights_ref,
    scale_ref,
    own_ref,
    across_ref,
    along_ref,
    slant_ref,
    image_ref,
    next_ref,
    up_ref,
    small_ref,
):
    lower = lax.axis_index("row") == 0
    columns, half = loaded_ref.shape
    own, across = own_ref[:, :half].astype(F32), across_ref[:, :half].astype(F32)
    along, slant = along_ref[:, :half].astype(F32), slant_ref[:, :half].astype(F32)
    mine = pieces_sum(own_ref, half, 2) + pieces_sum(across_ref, half, 2)
    coarse = mine + (pieces_sum(along_ref, half, 2) + pieces_sum(slant_ref, half, 2))
    backs = solved_backs(coarse, solver_ref[:, : 2 * LANES]).astype(BF16)
    fix = nn(backs, maps_ref[...])
    image = jnp.where(lower, own, across) + jnp.where(lower, slant, along) + fix[:, :half]
    image = jnp.where(live_ref[0:1] > 0.0, image, 0.0)
    wide = own_ref.shape[1]
    half_rows = columns // 2
    tail = across_ref[:, wide + half :].astype(F32)
    tail = jnp.concatenate([tail[:half_rows], tail[half_rows:]], axis=1)
    relayed = jnp.concatenate([across_ref[:, wide : wide + half].astype(F32), tail], axis=0)
    count = relayed.shape[0]
    more = nn(backs[:, 2 * count : 3 * count], relayed.astype(BF16))
    fix_right = fix[:, half:] + jnp.where(lower, 0.0, more)
    image_right = jnp.where(lower, across, own) + jnp.where(lower, along, slant) + fix_right
    image_right = jnp.where(live_ref[1:2] > 0.0, image_right, 0.0)
    left = weights_ref[...] * image
    right = scale_ref[...] * image_right
    image_ref[...] = image
    next_ref[...] = left
    left_2, right_2 = stacked(left), stacked(right)
    loaded = loaded_ref[...]
    first = loaded * weights_ref[...]
    sums = [
        jnp.sum(loaded * first, axis=1, keepdims=True),
        jnp.sum(first * image, axis=1, keepdims=True),
        jnp.sum(image * left, axis=1, keepdims=True),
    ]
    lane = lax.broadcasted_iota(jnp.int32, (columns, LANES), 1)

    def totals(block, local, corner):
        energy = jnp.sum(block * local, axis=1, keepdims=True)
        small = selected(folded(corner), names_ref[...])
        for at, value in enumerate([*sums, energy]):
            small = jnp.where(lane == LANES - len(sums) - 1 + at, value, small)
        small_ref[...] = small
        up_ref[:, half:] = jnp.concatenate(thirds(small), axis=1)

    @pl.when(lower)
    def _():
        local = nn(left_2, square_ref[...])
        slotted_2 = nn(right_2, right_hot_ref[...]).astype(BF16)
        corner = nt(right_2, maps_ref[:, half:])
        local = folded(local + nn(slotted_2, early_ref[...]))
        up_ref[:, :half] = local.astype(BF16)
        totals(folded(left_2.astype(F32)), local, corner)

    @pl.when(jnp.logical_not(lower))
    def _():
        slotted_2 = nn(right_2, right_hot_ref[...]).astype(BF16)
        local = nn(left_2, late_ref[...])
        corner = nt(left_2, maps_ref[:, :half])
        local = folded(local + nn(slotted_2, square_ref[...]))
        up_ref[:, :half] = nn(local.astype(BF16), order_ref[...]).astype(BF16)
        totals(folded(slotted_2.astype(F32)), local, corner)


def relay_kernel(up_own_ref, up_ref, down_ref, far_ref, own_ref, out_ref):
    lower = lax.axis_index("row") == 0
    half = up_ref.shape[1] - 3 * LANES
    total = own_ref[...] + pieces_sum(up_ref, half, 3)
    total = total + down_ref[...] + far_ref[...]
    out_ref[:, :half] = jnp.where(lower, up_own_ref[:, :half], up_ref[:, :half])
    out_ref[:, half:] = jnp.concatenate(thirds(total), axis=1)


def close_kernel(
    solver_ref,
    maps_ref,
    live_ref,
    loaded_ref,
    weights_ref,
    image_ref,
    next_ref,
    mine_ref,
    theirs_ref,
    solution_ref,
    residual_ref,
):
    lower = lax.axis_index("row") == 0
    columns, half = loaded_ref.shape
    mine, theirs = pieces_sum(mine_ref, half, 3), pieces_sum(theirs_ref, half, 3)
    total = jnp.where(lower, mine, theirs)
    lane = lax.broadcasted_iota(jnp.int32, (columns, LANES), 1)
    coarse = jnp.where(lane < LANES - 4, total, 0.0)
    backs = solved_backs(coarse, solver_ref[:, : 2 * LANES]).astype(BF16)
    solved = solved_backs(coarse, solver_ref[:, 2 * LANES :])
    fix = nn(backs, maps_ref[:, :half])
    image_next = mine_ref[:, :half].astype(F32) + theirs_ref[:, :half].astype(F32) + fix
    image_next = jnp.where(live_ref[0:1] > 0.0, image_next, 0.0)

    def column(values, at):
        return jnp.sum(jnp.where(lane == LANES - 4 + at, values, 0.0), axis=1, keepdims=True)

    gamma = column(total, 0)
    delta = column(total, 1)
    cross = column(total, 2)
    energy = column(mine + theirs, 3) + jnp.sum(coarse * solved, axis=1, keepdims=True)
    alpha = gamma / delta
    gamma_next = gamma - 2.0 * alpha * delta + alpha * alpha * cross
    ratio = gamma_next / gamma
    grown = 1.0 + ratio
    curvature = grown * grown * delta - 2.0 * grown * alpha * cross + alpha * alpha * energy
    alpha_next = gamma_next / curvature
    loaded = loaded_ref[...]
    first = loaded * weights_ref[...]
    direction = grown * first - alpha * next_ref[...]
    along = grown * image_ref[...] - alpha * image_next
    solution_ref[...] = alpha * first + alpha_next * direction
    residual_ref[...] = loaded - alpha * image_ref[...] - alpha_next * along


def ring(
    loads,
    weights,
    dual_ops,
    corner_maps,
    coarse_inverse,
    corner_ids,
    iface_sizes,
    left_partner,
    right_partner,
):
    count = lax.axis_size("sub")
    sides = lax.axis_size("row")
    columns, half = loads.shape[1:]
    corners = corner_maps.shape[1]
    operator = dual_ops[0]
    own_map = corner_maps[0]
    loaded = loads[0]
    block = operator.shape[0]
    shape = jax.ShapeDtypeStruct
    grid = ("sub", "row")
    big = 2 * columns * block * 2 * half

    def pairs(target):
        listed = []
        for at in range(count):
            for side in range(sides):
                to_at, to_side = target(at, side)
                listed.append((at * sides + side, (to_at % count) * sides + to_side))
        return listed

    across = pairs(lambda at, side: (at, 1 - side))
    along = pairs(lambda at, side: (at - 1, 0) if side == 0 else (at + 1, 1))
    slant = pairs(lambda at, side: (at - 1, 1) if side == 0 else (at + 1, 0))

    def call(kernel, operands, outs, scratch=(), flops=0, moved=0, room=4):
        specs, placed = [], []
        for operand in operands:
            held = isinstance(operand, tuple)
            specs.append(HBM if held else VMEM)
            placed.append(
                pltpu.with_memory_space_constraint(operand[0], pltpu.HBM) if held else operand
            )
        return pl.pallas_call(
            kernel,
            in_specs=specs,
            out_specs=[VMEM] * len(outs),
            out_shape=[shape(*out) for out in outs],
            scratch_shapes=scratch,
            cost_estimate=cost(flops, moved),
            compiler_params=pltpu.CompilerParams(vmem_limit_bytes=room << 20),
        )(*placed)

    rows = columns + corners + 8
    arguments = (weights, corner_ids, coarse_inverse, right_partner, left_partner)
    pack, skew, load, live, scale, ids, inverse, right_map, left_map = call(
        open_kernel,
        [(array,) for array in (iface_sizes, loaded, own_map, *arguments)],
        [((rows, half), BF16), ((columns + 8, half), BF16)]
        + [((columns, half), F32), ((8, half), F32)]
        + [(array.shape, array.dtype) for array in arguments],
        scratch=[
            pltpu.SMEM(iface_sizes.shape, jnp.int32),
            pltpu.VMEM(loaded.shape, F32),
            pltpu.VMEM(own_map.shape, BF16),
            pltpu.SemaphoreType.DMA((8,)),
        ],
        moved=4 * rows * half,
    )
    pack_slant = lax.ppermute(skew, grid, slant)
    pack_along = lax.ppermute(pack, grid, along)
    map_across = lax.ppermute(own_map, grid, across)
    right_hot, order, left_hot, square, cross, early, local_left, turned = call(
        select_kernel,
        [right_map, left_map, pack, (operator,)],
        [((half, half), BF16)] * 3
        + [((block, half), BF16)] * 3
        + [((columns, block), F32), ((columns, half), BF16)],
        scratch=[pltpu.SemaphoreType.DMA((2,))],
        flops=big,
        moved=4 * half * half,
        room=16,
    )
    wide = half + 2 * LANES
    send, pair = call(
        first_kernel,
        [
            ids,
            square,
            early,
            right_hot,
            order,
            local_left,
            turned,
            pack,
            map_across,
            pack_along,
            pack_slant,
        ],
        [((columns, wide), BF16), ((columns, wide + half + half // 2), BF16)],
        flops=2 * big,
        moved=4 * block * half,
        room=16,
    )
    send_slant = lax.ppermute(send, grid, slant)
    send_along = lax.ppermute(send, grid, along)
    send_across = lax.ppermute(pair, grid, across)
    maps, solver, scale_right, names, late = call(
        order_kernel,
        [ids, inverse, order, left_hot, cross, pack, map_across, pack_along, pack_slant],
        [
            ((LANES, 2 * half), BF16),
            ((LANES, 4 * LANES), BF16),
            ((1, half), F32),
            ((LANES, LANES), BF16),
            ((half, block), BF16),
        ],
        flops=4 * corners * half * half,
        moved=4 * half * half,
        room=12,
    )
    image, following, up, small = call(
        second_kernel,
        [
            names,
            solver,
            maps,
            right_hot,
            order,
            square,
            early,
            late,
            live,
            load,
            scale,
            scale_right,
            send,
            send_across,
            send_along,
            send_slant,
        ],
        [
            ((columns, half), F32),
            ((columns, half), F32),
            ((columns, half + 3 * LANES), BF16),
            ((columns, LANES), F32),
        ],
        flops=2 * big,
        moved=4 * block * half,
        room=16,
    )
    far_in = shifted(small, "sub", 2)
    down_in = shifted(small, "sub", -1)
    up_in = shifted(up, "sub", 1)
    (mine,) = call(
        relay_kernel,
        [up, up_in, down_in, far_in, small],
        [((columns, half + 3 * LANES), BF16)],
        moved=8 * columns * half,
    )
    theirs = lax.ppermute(mine, grid, across)
    solution, residual = call(
        close_kernel,
        [solver, maps, live, load, scale, image, following, mine, theirs],
        [((columns, half), F32), ((columns, half), F32)],
        moved=24 * columns * half,
    )
    return solution[None], residual[None]


def per_device(*arrays):
    loads, _, dual_ops, corner_maps, coarse_inverse = arrays[:5]
    half = loads.shape[2]
    neighbourly = lax.axis_size("sub") == 4 and lax.axis_size("row") == 2
    sided = dual_ops.shape[1] == half and half % LANES == 0
    columns, corners = loads.shape[1], corner_maps.shape[1]
    fitting = columns % 16 == 0 and corners == columns + columns // 2 and corners == columns + 8
    narrow = coarse_inverse.shape[0] + 4 <= LANES and 3 * corner_maps.shape[1] <= LANES
    if neighbourly and sided and fitting and narrow and ITERS == 2:
        return ring(*arrays)
    return general(*arrays)


def solution(mesh):
    placed = (
        P(("parts", "sub"), "col", None),
        P(("parts", "sub"), None),
        P(("parts", "sub"), "row", None),
        P(("parts", "sub"), None, "row"),
        P("parts", None),
        P("parts", None),
        P("parts"),
        P(("parts", "sub"), None),
        P(("parts", "sub"), None),
    )
    return jax.shard_map(
        per_device,
        mesh=mesh,
        in_specs=placed,
        out_specs=(P(("parts", "sub"), "col", None), P(("parts", "sub"), "col", None)),
        check_vma=False,
    )
```

```python
import jax
import jax.numpy as jnp
from jax import lax
from jax.experimental import pallas as pl
from jax.experimental.pallas import tpu as pltpu
from jax.sharding import PartitionSpec as P

TILE = 128
LANES = 128
ITERS = 2
F32 = jnp.float32
BF16 = jnp.bfloat16
HIGH = lax.Precision.HIGHEST
VMEM = pl.BlockSpec(memory_space=pltpu.VMEM)
HBM = pl.BlockSpec(memory_space=pltpu.HBM)


def shifted(value, axis, steps):
    count = lax.axis_size(axis)
    pairs = [(source, (source + steps) % count) for source in range(count)]
    return lax.ppermute(value, axis, pairs)


def inner(first, second, half):
    return jnp.sum(first[:, :half] * second[:, :half], axis=1)


def paired_totals(residual, precond, image, half):
    return lax.psum((inner(residual, precond, half), inner(precond, image, half)), "sub")


def tile_products(vector, rows_op, first_tile, last_tile, output):

    def one_tile(tile_at, acc):
        piece = lax.dynamic_slice_in_dim(rows_op, tile_at * TILE, TILE, 0)
        product = lax.dot_general(
            vector, piece, (((1,), (1,)), ((), ())), preferred_element_type=jnp.float32
        )
        return lax.dynamic_update_slice_in_dim(acc, product, tile_at * TILE, 1)

    return lax.fori_loop(first_tile, last_tile, one_tile, output)


def live_tiles(size_before, size_after, block_start, block, half):
    left_live = jnp.clip(size_before - block_start, 0, block)
    right_live = jnp.clip(size_after - (block_start - half), 0, block)
    live_cols = jnp.where(block_start < half, left_live, right_live)
    return (live_cols + TILE - 1) // TILE


def general(
    loads,
    weights,
    dual_ops,
    corner_maps,
    coarse_inverse,
    corner_ids,
    iface_sizes,
    left_partner,
    right_partner,
):
    half = loads.shape[2]
    block = dual_ops.shape[1]
    width = coarse_inverse.shape[0]
    subdomain = lax.axis_index("sub")
    count = lax.axis_size("sub")
    row_index = lax.axis_index("row")
    left_map = left_partner[0]
    right_map = right_partner[0]
    slots = jnp.arange(half, dtype=jnp.int32)
    size_before = iface_sizes[(subdomain + count - 1) % count]
    size_after = iface_sizes[subdomain]
    live_left = (slots < size_before).astype(jnp.float32)
    live_right = (right_map < size_after).astype(jnp.float32)
    columns = jnp.arange(width, dtype=jnp.int32)
    own_hot = (corner_ids[subdomain][:, None] == columns[None, :]).astype(jnp.float32)
    operator = dual_ops[0]
    coupling = corner_maps[0]
    block_start = row_index * block
    own_tiles = live_tiles(size_before, size_after, block_start, block, half)

    def apply_operator(vec):
        halfway = vec.astype(jnp.bfloat16)
        empty = jnp.zeros((halfway.shape[0], block), jnp.float32)
        local = tile_products(halfway, operator, jnp.int32(0), own_tiles, empty)
        own_slots = lax.dynamic_slice_in_dim(halfway, row_index * block, block, 1)
        corner = lax.dot_general(
            own_slots, coupling, (((1,), (1,)), ((), ())), preferred_element_type=jnp.float32
        )
        scattered = jnp.dot(corner, own_hot, precision=lax.Precision.HIGHEST)
        coarse = lax.psum(scattered, ("sub", "row"))
        solved = jnp.dot(coarse, coarse_inverse, precision=lax.Precision.HIGHEST)
        back = lax.dot_general(
            solved, own_hot, (((1,), (1,)), ((), ())), precision=lax.Precision.HIGHEST
        ).astype(jnp.bfloat16)
        united = local + jnp.dot(back, coupling, preferred_element_type=jnp.float32)
        whole = lax.all_gather(united.astype(jnp.bfloat16), "row", axis=1, tiled=True).astype(
            united.dtype
        )
        lower = whole[:, :half]
        upper = whole[:, half:]
        arrived_left = shifted(upper.astype(jnp.bfloat16), "sub", 1).astype(upper.dtype)
        arrived_right = shifted(lower.astype(jnp.bfloat16), "sub", -1).astype(lower.dtype)
        result_left = (lower + jnp.take(arrived_left, left_map, axis=1)) * live_left
        result_right = (upper + jnp.take(arrived_right, right_map, axis=1)) * live_right
        return jnp.concatenate([result_left, result_right], axis=1)

    received = (
        shifted(loads[0].astype(jnp.bfloat16), "sub", -1).astype(jnp.float32),
        shifted(weights.astype(jnp.bfloat16), "sub", -1).astype(weights.dtype),
    )
    right_load = jnp.take(received[0], right_map, axis=1) * live_right
    right_weight = jnp.take(received[1], right_map, axis=1)
    residual = jnp.concatenate([loads[0] * live_left, right_load], axis=1)
    scaling = jnp.concatenate([weights, right_weight], axis=1)
    solution = jnp.zeros_like(residual)
    precond = scaling * residual
    image = apply_operator(precond)
    gamma, delta = paired_totals(residual, precond, image, half)
    alpha = gamma / delta
    direction = precond
    along = image
    for step in range(ITERS):
        solution = solution + alpha[:, None] * direction
        residual = residual - alpha[:, None] * along
        if step + 1 < ITERS:
            precond = scaling * residual
            image = apply_operator(precond)
            gamma_next, delta = paired_totals(residual, precond, image, half)
            ratio = gamma_next / gamma
            alpha = gamma_next / (delta - ratio * gamma_next / alpha)
            direction = precond + ratio[:, None] * direction
            along = image + ratio[:, None] * along
            gamma = gamma_next
    return (solution[:, :half][None], residual[:, :half][None])


def cost(flops, moved):
    return pl.CostEstimate(flops=flops, bytes_accessed=moved, transcendentals=0)


def nt(first, second, precision=None):
    return lax.dot_general(
        first, second, (((1,), (1,)), ((), ())), preferred_element_type=F32, precision=precision
    )


def nn(first, second, precision=None):
    return jnp.dot(first, second, preferred_element_type=F32, precision=precision)


def halves(value):
    high = value.astype(BF16)
    return high, (value - high.astype(F32)).astype(BF16)


def stacked(value):
    return jnp.concatenate(halves(value), axis=0)


def thirds(value):
    high = value.astype(BF16)
    rest = value - high.astype(F32)
    middle = rest.astype(BF16)
    return high, middle, (rest - middle.astype(F32)).astype(BF16)


def pieces_sum(ref, half, count):
    total = ref[:, half : half + LANES].astype(F32)
    for piece in range(1, count):
        at = half + piece * LANES
        total = total + ref[:, at : at + LANES].astype(F32)
    return total


def neighbours():
    subdomain = lax.axis_index("sub")
    count = lax.axis_size("sub")
    return lax.rem(subdomain + count - 1, count), subdomain, lax.rem(subdomain + 1, count)


def hot_rows(ids_ref, subdomain, extent):
    ids = ids_ref[pl.ds(subdomain, 1), :]
    names = lax.broadcasted_iota(jnp.int32, (extent, ids.shape[1]), 0)
    return (names == ids).astype(F32)


def hot_names(ids_ref):
    spare = jnp.zeros((LANES, LANES - 3 * ids_ref.shape[1]), F32)
    hots = [hot_rows(ids_ref, each, LANES) for each in neighbours()]
    return jnp.concatenate([*hots, spare], axis=1)


def selected(values, names):
    high, middle, low = thirds(values)
    rows = values.shape[0]
    parts = nt(jnp.concatenate([high, middle, low], axis=0), names)
    return parts[:rows] + parts[rows : 2 * rows] + parts[2 * rows :]


def solved_backs(coarse, solver):
    rows = coarse.shape[0]
    parts = nn(stacked(coarse), solver)
    width = solver.shape[1] // 2
    return parts[:rows, :width] + (parts[:rows, width:] + parts[rows:, :width])


def open_kernel(
    sizes_in,
    loads_in,
    maps_in,
    weights_in,
    ids_in,
    inverse_in,
    right_in,
    left_in,
    pack_ref,
    skew_ref,
    loaded_ref,
    live_ref,
    weights_ref,
    ids_ref,
    inverse_ref,
    right_ref,
    left_ref,
    sizes_ref,
    loads_ref,
    maps_ref,
    sems,
):
    pairs = (
        (sizes_in, sizes_ref),
        (loads_in, loads_ref),
        (weights_in, weights_ref),
        (maps_in, maps_ref),
        (ids_in, ids_ref),
        (inverse_in, inverse_ref),
        (right_in, right_ref),
        (left_in, left_ref),
    )
    copies = [pltpu.make_async_copy(*pair, sems.at[at]) for at, pair in enumerate(pairs)]
    for copy in copies:
        copy.start()
    before, subdomain, _ = neighbours()
    for copy in copies:
        copy.wait()
    slots = lax.broadcasted_iota(jnp.int32, live_ref.shape, 1)
    which = lax.broadcasted_iota(jnp.int32, live_ref.shape, 0)
    bound = jnp.where(which == 0, sizes_ref[before], sizes_ref[subdomain])
    live = (slots < bound).astype(F32)
    live_ref[...] = live
    scale = weights_ref[...]
    loaded = jnp.where(live[0:1] > 0.0, loads_ref[...], 0.0)
    loaded_ref[...] = loaded
    first = loaded * scale
    high = scale.astype(BF16).astype(F32)
    spare = jnp.where(which == 0, high, jnp.where(which == 1, scale - high, 0.0))
    maps = maps_ref[...].astype(F32)
    pack_ref[...] = jnp.concatenate([first, maps, spare], axis=0).astype(BF16)
    short = jnp.concatenate([first, spare], axis=0)
    skew_ref[...] = jnp.where(lax.axis_index("row") == 0, short, maps).astype(BF16)


def side_columns(ref, side, half):
    return ref.at[:, pl.ds(pl.multiple_of(side * half, half), half)]


def turn(source_ref, target_ref):
    for at in range(0, source_ref.shape[1], LANES):
        block = slice(at, at + LANES)
        target_ref[block, :] = jnp.transpose(source_ref[:, block])


def select_kernel(
    right_ref,
    left_ref,
    pack_ref,
    operator_in,
    right_hot_ref,
    order_ref,
    left_hot_ref,
    square_ref,
    cross_ref,
    early_ref,
    local_ref,
    turned_ref,
    sems,
):
    half = right_ref.shape[1]
    columns = local_ref.shape[0]
    side = lax.axis_index("row")
    lower = side == 0
    square = pltpu.make_async_copy(side_columns(operator_in, side, half), square_ref, sems.at[0])
    cross = pltpu.make_async_copy(side_columns(operator_in, 1 - side, half), cross_ref, sems.at[1])

    @pl.when(lower)
    def _():
        square.start()
        cross.start()

    @pl.when(jnp.logical_not(lower))
    def _():
        cross.start()
        square.start()

    short = jnp.int16
    right = right_ref[...]
    tall = jnp.transpose(jnp.broadcast_to(right, (8, half)).astype(F32))[:, 0:1].astype(jnp.int32)
    tall = jnp.broadcast_to(tall, (half, LANES)).astype(short)
    names = lax.broadcasted_iota(jnp.int32, (LANES, LANES), 1)
    full, none = jnp.ones((LANES, half), BF16), jnp.zeros((LANES, half), BF16)
    narrow_full, narrow_none = jnp.ones((LANES, LANES), BF16), jnp.zeros((LANES, LANES), BF16)
    for at in range(half // LANES):
        rows = slice(at * LANES, (at + 1) * LANES)
        for block in range(half // LANES):
            own = (names + block * LANES).astype(short)
            hit = own == tall[rows]
            columns_at = slice(block * LANES, (block + 1) * LANES)
            order_ref[rows, columns_at] = jnp.where(hit, narrow_full, narrow_none)
    wide_right = jnp.broadcast_to(right, (LANES, half)).astype(short)
    wide_left = jnp.broadcast_to(left_ref[...], (LANES, half)).astype(short)

    def one(at, carry):
        start = pl.multiple_of(at * LANES, LANES)
        slots = (lax.broadcasted_iota(jnp.int32, (LANES, half), 0) + start).astype(short)
        rows = pl.ds(start, LANES)
        right_hot_ref[rows, :] = jnp.where(slots == wide_right, full, none)
        left_hot_ref[rows, :] = jnp.where(slots == wide_left, full, none)
        return carry

    lax.fori_loop(0, half // LANES, one, 0)
    left = pack_ref[:columns, :]

    @pl.when(lower)
    def _():
        turned_ref[...] = left
        square.wait()
        local_ref[...] = nn(left, square_ref[...])
        cross.wait()
        turn(cross_ref, early_ref)

    @pl.when(jnp.logical_not(lower))
    def _():
        turned_ref[...] = nt(left, left_hot_ref[...]).astype(BF16)
        cross.wait()
        local_ref[...] = nt(left, cross_ref[...])
        square.wait()


def first_kernel(
    ids_ref,
    square_ref,
    early_ref,
    right_hot_ref,
    order_ref,
    local_ref,
    turned_ref,
    own_pack_ref,
    across_ref,
    along_ref,
    slant_ref,
    send_ref,
    pair_ref,
):
    columns, half = local_ref.shape
    corners = ids_ref.shape[1]
    before, subdomain, after = neighbours()
    lower = lax.axis_index("row") == 0

    def coarse_part(own_side, other_side, other):
        one = nt(own_side, across_ref[...])
        two = nt(other_side, along_ref[columns:, :])[:, :corners]
        hot_own = hot_rows(ids_ref, subdomain, LANES)
        hot_other = hot_rows(ids_ref, other, LANES)
        high, low = halves(selected(one, hot_own) + selected(two, hot_other))
        send_ref[:, half:] = jnp.concatenate([high, low], axis=1)

    @pl.when(lower)
    def _():
        right = along_ref[:columns, :]
        slotted = nn(right, right_hot_ref[...]).astype(BF16)
        coarse_part(slotted, right, after)
        send_ref[:, :half] = (local_ref[...] + nn(slotted, early_ref[...])).astype(BF16)

    @pl.when(jnp.logical_not(lower))
    def _():
        slotted = nn(slant_ref[:columns, :], right_hot_ref[...]).astype(BF16)
        coarse_part(own_pack_ref[:columns, :], turned_ref[...], before)
        local = (local_ref[...] + nn(slotted, square_ref[...])).astype(BF16)
        send_ref[:, :half] = nn(local, order_ref[...]).astype(BF16)

    wide = send_ref.shape[1]
    relayed = along_ref[columns : columns + corners, :].astype(F32)
    tail = relayed[columns:]
    tail = jnp.concatenate([tail[:, : half // 2], tail[:, half // 2 :]], axis=0)
    pair_ref[:, :wide] = send_ref[...]
    pair_ref[:, wide:] = jnp.concatenate([relayed[:columns], tail], axis=1).astype(BF16)


def order_kernel(
    ids_ref,
    inverse_ref,
    order_ref,
    left_hot_ref,
    cross_ref,
    own_pack_ref,
    across_ref,
    along_ref,
    slant_ref,
    maps_ref,
    solver_ref,
    scale_ref,
    names_ref,
    late_ref,
):
    half = order_ref.shape[1]
    corners = ids_ref.shape[1]
    width = inverse_ref.shape[0]
    columns = own_pack_ref.shape[0] - corners - 8
    lower = lax.axis_index("row") == 0
    own, across = own_pack_ref[columns:, :].astype(F32)[:corners], across_ref[...].astype(F32)
    along, slant = along_ref[columns:, :].astype(F32), slant_ref[...].astype(F32)
    behind = jnp.where(lower, slant, along[:corners])
    ahead = jnp.where(lower, along[:corners], 0.0)
    scales = jnp.where(lower, along[corners:], slant[columns:])
    scale_ref[...] = scales[0:1] + scales[1:2]
    raw = jnp.where(lower, across, own).astype(BF16)
    ordered = nn(raw, order_ref[...])
    turned = nn(behind.astype(BF16), left_hot_ref[...])
    spare = jnp.zeros((LANES - 3 * corners, half), F32)
    blank = jnp.zeros((corners, half), F32)
    mine = jnp.where(lower, own, across)
    maps_ref[:, :half] = jnp.concatenate([turned, mine, blank, spare], axis=0).astype(BF16)
    maps_ref[:, half:] = jnp.concatenate([blank, ordered, ahead, spare], axis=0).astype(BF16)
    names = hot_names(ids_ref)
    names_ref[...] = names.astype(BF16)
    backs = nn(inverse_ref[...], names[:width], HIGH)
    low_rows = jnp.zeros((LANES - width, LANES), F32)
    side = jnp.concatenate([inverse_ref[...], jnp.zeros((width, LANES - width), F32)], axis=1)
    pieces = []
    for piece in (backs, side):
        tall = jnp.concatenate([piece, low_rows], axis=0)
        pieces.extend(halves(tall))
    solver_ref[...] = jnp.concatenate(pieces, axis=1)

    @pl.when(jnp.logical_not(lower))
    def _():
        turn(cross_ref, late_ref)


def second_kernel(
    names_ref,
    solver_ref,
    maps_ref,
    right_hot_ref,
    order_ref,
    square_ref,
    early_ref,
    late_ref,
    live_ref,
    loaded_ref,
    weights_ref,
    scale_ref,
    own_ref,
    across_ref,
    along_ref,
    slant_ref,
    image_ref,
    next_ref,
    up_ref,
    small_ref,
):
    lower = lax.axis_index("row") == 0
    columns, half = loaded_ref.shape
    own, across = own_ref[:, :half].astype(F32), across_ref[:, :half].astype(F32)
    along, slant = along_ref[:, :half].astype(F32), slant_ref[:, :half].astype(F32)
    mine = pieces_sum(own_ref, half, 2) + pieces_sum(across_ref, half, 2)
    coarse = mine + (pieces_sum(along_ref, half, 2) + pieces_sum(slant_ref, half, 2))
    backs = solved_backs(coarse, solver_ref[:, : 2 * LANES]).astype(BF16)
    fix = nn(backs, maps_ref[...])
    image = jnp.where(lower, own, across) + jnp.where(lower, slant, along) + fix[:, :half]
    image = jnp.where(live_ref[0:1] > 0.0, image, 0.0)
    wide = own_ref.shape[1]
    half_rows = columns // 2
    tail = across_ref[:, wide + half :].astype(F32)
    tail = jnp.concatenate([tail[:half_rows], tail[half_rows:]], axis=1)
    relayed = jnp.concatenate([across_ref[:, wide : wide + half].astype(F32), tail], axis=0)
    count = relayed.shape[0]
    more = nn(backs[:, 2 * count : 3 * count], relayed.astype(BF16))
    fix_right = fix[:, half:] + jnp.where(lower, 0.0, more)
    image_right = jnp.where(lower, across, own) + jnp.where(lower, along, slant) + fix_right
    image_right = jnp.where(live_ref[1:2] > 0.0, image_right, 0.0)
    left = weights_ref[...] * image
    right = scale_ref[...] * image_right
    image_ref[...] = image
    next_ref[...] = left
    left_2, right_2 = left.astype(BF16), right.astype(BF16)
    loaded = loaded_ref[...]
    first = loaded * weights_ref[...]
    sums = [
        jnp.sum(loaded * first, axis=1, keepdims=True),
        jnp.sum(first * image, axis=1, keepdims=True),
        jnp.sum(image * left, axis=1, keepdims=True),
    ]
    lane = lax.broadcasted_iota(jnp.int32, (columns, LANES), 1)

    def totals(block, local, corner):
        energy = jnp.sum(block * local, axis=1, keepdims=True)
        small = selected(corner, names_ref[...])
        for at, value in enumerate([*sums, energy]):
            small = jnp.where(lane == LANES - len(sums) - 1 + at, value, small)
        small_ref[...] = small
        up_ref[:, half:] = jnp.concatenate(thirds(small), axis=1)

    @pl.when(lower)
    def _():
        local = nn(left_2, square_ref[...])
        slotted_2 = nn(right_2, right_hot_ref[...]).astype(BF16)
        corner = nt(right_2, maps_ref[:, half:])
        local = local + nn(slotted_2, early_ref[...])
        up_ref[:, :half] = local.astype(BF16)
        totals(left_2.astype(F32), local, corner)

    @pl.when(jnp.logical_not(lower))
    def _():
        slotted_2 = nn(right_2, right_hot_ref[...]).astype(BF16)
        local = nn(left_2, late_ref[...])
        corner = nt(left_2, maps_ref[:, :half])
        local = local + nn(slotted_2, square_ref[...])
        up_ref[:, :half] = nn(local.astype(BF16), order_ref[...]).astype(BF16)
        totals(slotted_2.astype(F32), local, corner)


def relay_kernel(up_own_ref, up_ref, down_ref, far_ref, own_ref, out_ref):
    lower = lax.axis_index("row") == 0
    half = up_ref.shape[1] - 3 * LANES
    total = own_ref[...] + pieces_sum(up_ref, half, 3)
    total = total + down_ref[...] + far_ref[...]
    out_ref[:, :half] = jnp.where(lower, up_own_ref[:, :half], up_ref[:, :half])
    out_ref[:, half:] = jnp.concatenate(thirds(total), axis=1)


def close_kernel(
    solver_ref,
    maps_ref,
    live_ref,
    loaded_ref,
    weights_ref,
    image_ref,
    next_ref,
    mine_ref,
    theirs_ref,
    solution_ref,
    residual_ref,
):
    lower = lax.axis_index("row") == 0
    columns, half = loaded_ref.shape
    mine, theirs = pieces_sum(mine_ref, half, 3), pieces_sum(theirs_ref, half, 3)
    total = jnp.where(lower, mine, theirs)
    lane = lax.broadcasted_iota(jnp.int32, (columns, LANES), 1)
    coarse = jnp.where(lane < LANES - 4, total, 0.0)
    backs = solved_backs(coarse, solver_ref[:, : 2 * LANES]).astype(BF16)
    solved = solved_backs(coarse, solver_ref[:, 2 * LANES :])
    fix = nn(backs, maps_ref[:, :half])
    image_next = mine_ref[:, :half].astype(F32) + theirs_ref[:, :half].astype(F32) + fix
    image_next = jnp.where(live_ref[0:1] > 0.0, image_next, 0.0)

    def column(values, at):
        return jnp.sum(jnp.where(lane == LANES - 4 + at, values, 0.0), axis=1, keepdims=True)

    gamma = column(total, 0)
    delta = column(total, 1)
    cross = column(total, 2)
    energy = column(mine + theirs, 3) + jnp.sum(coarse * solved, axis=1, keepdims=True)
    alpha = gamma / delta
    gamma_next = gamma - 2.0 * alpha * delta + alpha * alpha * cross
    ratio = gamma_next / gamma
    grown = 1.0 + ratio
    curvature = grown * grown * delta - 2.0 * grown * alpha * cross + alpha * alpha * energy
    alpha_next = gamma_next / curvature
    loaded = loaded_ref[...]
    first = loaded * weights_ref[...]
    direction = grown * first - alpha * next_ref[...]
    along = grown * image_ref[...] - alpha * image_next
    solution_ref[...] = alpha * first + alpha_next * direction
    residual_ref[...] = loaded - alpha * image_ref[...] - alpha_next * along


def ring(
    loads,
    weights,
    dual_ops,
    corner_maps,
    coarse_inverse,
    corner_ids,
    iface_sizes,
    left_partner,
    right_partner,
):
    count = lax.axis_size("sub")
    sides = lax.axis_size("row")
    columns, half = loads.shape[1:]
    corners = corner_maps.shape[1]
    operator = dual_ops[0]
    own_map = corner_maps[0]
    loaded = loads[0]
    block = operator.shape[0]
    shape = jax.ShapeDtypeStruct
    grid = ("sub", "row")
    big = 2 * columns * block * 2 * half

    def pairs(target):
        listed = []
        for at in range(count):
            for side in range(sides):
                to_at, to_side = target(at, side)
                listed.append((at * sides + side, (to_at % count) * sides + to_side))
        return listed

    across = pairs(lambda at, side: (at, 1 - side))
    along = pairs(lambda at, side: (at - 1, 0) if side == 0 else (at + 1, 1))
    slant = pairs(lambda at, side: (at - 1, 1) if side == 0 else (at + 1, 0))

    def call(kernel, operands, outs, scratch=(), flops=0, moved=0, room=4):
        specs, placed = [], []
        for operand in operands:
            held = isinstance(operand, tuple)
            specs.append(HBM if held else VMEM)
            placed.append(
                pltpu.with_memory_space_constraint(operand[0], pltpu.HBM) if held else operand
            )
        return pl.pallas_call(
            kernel,
            in_specs=specs,
            out_specs=[VMEM] * len(outs),
            out_shape=[shape(*out) for out in outs],
            scratch_shapes=scratch,
            cost_estimate=cost(flops, moved),
            compiler_params=pltpu.CompilerParams(vmem_limit_bytes=room << 20),
        )(*placed)

    rows = columns + corners + 8
    arguments = (weights, corner_ids, coarse_inverse, right_partner, left_partner)
    pack, skew, load, live, scale, ids, inverse, right_map, left_map = call(
        open_kernel,
        [(array,) for array in (iface_sizes, loaded, own_map, *arguments)],
        [((rows, half), BF16), ((columns + 8, half), BF16)]
        + [((columns, half), F32), ((8, half), F32)]
        + [(array.shape, array.dtype) for array in arguments],
        scratch=[
            pltpu.SMEM(iface_sizes.shape, jnp.int32),
            pltpu.VMEM(loaded.shape, F32),
            pltpu.VMEM(own_map.shape, BF16),
            pltpu.SemaphoreType.DMA((8,)),
        ],
        moved=4 * rows * half,
    )
    pack_slant = lax.ppermute(skew, grid, slant)
    pack_along = lax.ppermute(pack, grid, along)
    map_across = lax.ppermute(own_map, grid, across)
    right_hot, order, left_hot, square, cross, early, local_left, turned = call(
        select_kernel,
        [right_map, left_map, pack, (operator,)],
        [((half, half), BF16)] * 3
        + [((block, half), BF16)] * 3
        + [((columns, block), F32), ((columns, half), BF16)],
        scratch=[pltpu.SemaphoreType.DMA((2,))],
        flops=big,
        moved=4 * half * half,
        room=16,
    )
    wide = half + 2 * LANES
    send, pair = call(
        first_kernel,
        [
            ids,
            square,
            early,
            right_hot,
            order,
            local_left,
            turned,
            pack,
            map_across,
            pack_along,
            pack_slant,
        ],
        [((columns, wide), BF16), ((columns, wide + half + half // 2), BF16)],
        flops=2 * big,
        moved=4 * block * half,
        room=16,
    )
    send_slant = lax.ppermute(send, grid, slant)
    send_along = lax.ppermute(send, grid, along)
    send_across = lax.ppermute(pair, grid, across)
    maps, solver, scale_right, names, late = call(
        order_kernel,
        [ids, inverse, order, left_hot, cross, pack, map_across, pack_along, pack_slant],
        [
            ((LANES, 2 * half), BF16),
            ((LANES, 4 * LANES), BF16),
            ((1, half), F32),
            ((LANES, LANES), BF16),
            ((half, block), BF16),
        ],
        flops=4 * corners * half * half,
        moved=4 * half * half,
        room=12,
    )
    image, following, up, small = call(
        second_kernel,
        [
            names,
            solver,
            maps,
            right_hot,
            order,
            square,
            early,
            late,
            live,
            load,
            scale,
            scale_right,
            send,
            send_across,
            send_along,
            send_slant,
        ],
        [
            ((columns, half), F32),
            ((columns, half), F32),
            ((columns, half + 3 * LANES), BF16),
            ((columns, LANES), F32),
        ],
        flops=2 * big,
        moved=4 * block * half,
        room=16,
    )
    far_in = shifted(small, "sub", 2)
    down_in = shifted(small, "sub", -1)
    up_in = shifted(up, "sub", 1)
    (mine,) = call(
        relay_kernel,
        [up, up_in, down_in, far_in, small],
        [((columns, half + 3 * LANES), BF16)],
        moved=8 * columns * half,
    )
    theirs = lax.ppermute(mine, grid, across)
    solution, residual = call(
        close_kernel,
        [solver, maps, live, load, scale, image, following, mine, theirs],
        [((columns, half), F32), ((columns, half), F32)],
        moved=24 * columns * half,
    )
    return solution[None], residual[None]


def per_device(*arrays):
    loads, _, dual_ops, corner_maps, coarse_inverse = arrays[:5]
    half = loads.shape[2]
    neighbourly = lax.axis_size("sub") == 4 and lax.axis_size("row") == 2
    sided = dual_ops.shape[1] == half and half % LANES == 0
    columns, corners = loads.shape[1], corner_maps.shape[1]
    fitting = columns % 16 == 0 and corners == columns + columns // 2 and corners == columns + 8
    narrow = coarse_inverse.shape[0] + 4 <= LANES and 3 * corner_maps.shape[1] <= LANES
    if neighbourly and sided and fitting and narrow and ITERS == 2:
        return ring(*arrays)
    return general(*arrays)


def solution(mesh):
    placed = (
        P(("parts", "sub"), "col", None),
        P(("parts", "sub"), None),
        P(("parts", "sub"), "row", None),
        P(("parts", "sub"), None, "row"),
        P("parts", None),
        P("parts", None),
        P("parts"),
        P(("parts", "sub"), None),
        P(("parts", "sub"), None),
    )
    return jax.shard_map(
        per_device,
        mesh=mesh,
        in_specs=placed,
        out_specs=(P(("parts", "sub"), "col", None), P(("parts", "sub"), "col", None)),
        check_vma=False,
    )
```

```python
import jax
import jax.numpy as jnp
from jax import lax
from jax.experimental import pallas as pl
from jax.experimental.pallas import tpu as pltpu
from jax.sharding import PartitionSpec as P

TILE = 128
LANES = 128
ITERS = 2
F32 = jnp.float32
BF16 = jnp.bfloat16
HIGH = lax.Precision.HIGHEST
VMEM = pl.BlockSpec(memory_space=pltpu.VMEM)
HBM = pl.BlockSpec(memory_space=pltpu.HBM)


def shifted(value, axis, steps):
    count = lax.axis_size(axis)
    pairs = [(source, (source + steps) % count) for source in range(count)]
    return lax.ppermute(value, axis, pairs)


def inner(first, second, half):
    return jnp.sum(first[:, :half] * second[:, :half], axis=1)


def paired_totals(residual, precond, image, half):
    return lax.psum((inner(residual, precond, half), inner(precond, image, half)), "sub")


def tile_products(vector, rows_op, first_tile, last_tile, output):

    def one_tile(tile_at, acc):
        piece = lax.dynamic_slice_in_dim(rows_op, tile_at * TILE, TILE, 0)
        product = lax.dot_general(
            vector, piece, (((1,), (1,)), ((), ())), preferred_element_type=jnp.float32
        )
        return lax.dynamic_update_slice_in_dim(acc, product, tile_at * TILE, 1)

    return lax.fori_loop(first_tile, last_tile, one_tile, output)


def live_tiles(size_before, size_after, block_start, block, half):
    left_live = jnp.clip(size_before - block_start, 0, block)
    right_live = jnp.clip(size_after - (block_start - half), 0, block)
    live_cols = jnp.where(block_start < half, left_live, right_live)
    return (live_cols + TILE - 1) // TILE


def general(
    loads,
    weights,
    dual_ops,
    corner_maps,
    coarse_inverse,
    corner_ids,
    iface_sizes,
    left_partner,
    right_partner,
):
    half = loads.shape[2]
    block = dual_ops.shape[1]
    width = coarse_inverse.shape[0]
    subdomain = lax.axis_index("sub")
    count = lax.axis_size("sub")
    row_index = lax.axis_index("row")
    left_map = left_partner[0]
    right_map = right_partner[0]
    slots = jnp.arange(half, dtype=jnp.int32)
    size_before = iface_sizes[(subdomain + count - 1) % count]
    size_after = iface_sizes[subdomain]
    live_left = (slots < size_before).astype(jnp.float32)
    live_right = (right_map < size_after).astype(jnp.float32)
    columns = jnp.arange(width, dtype=jnp.int32)
    own_hot = (corner_ids[subdomain][:, None] == columns[None, :]).astype(jnp.float32)
    operator = dual_ops[0]
    coupling = corner_maps[0]
    block_start = row_index * block
    own_tiles = live_tiles(size_before, size_after, block_start, block, half)

    def apply_operator(vec):
        halfway = vec.astype(jnp.bfloat16)
        empty = jnp.zeros((halfway.shape[0], block), jnp.float32)
        local = tile_products(halfway, operator, jnp.int32(0), own_tiles, empty)
        own_slots = lax.dynamic_slice_in_dim(halfway, row_index * block, block, 1)
        corner = lax.dot_general(
            own_slots, coupling, (((1,), (1,)), ((), ())), preferred_element_type=jnp.float32
        )
        scattered = jnp.dot(corner, own_hot, precision=lax.Precision.HIGHEST)
        coarse = lax.psum(scattered, ("sub", "row"))
        solved = jnp.dot(coarse, coarse_inverse, precision=lax.Precision.HIGHEST)
        back = lax.dot_general(
            solved, own_hot, (((1,), (1,)), ((), ())), precision=lax.Precision.HIGHEST
        ).astype(jnp.bfloat16)
        united = local + jnp.dot(back, coupling, preferred_element_type=jnp.float32)
        whole = lax.all_gather(united.astype(jnp.bfloat16), "row", axis=1, tiled=True).astype(
            united.dtype
        )
        lower = whole[:, :half]
        upper = whole[:, half:]
        arrived_left = shifted(upper.astype(jnp.bfloat16), "sub", 1).astype(upper.dtype)
        arrived_right = shifted(lower.astype(jnp.bfloat16), "sub", -1).astype(lower.dtype)
        result_left = (lower + jnp.take(arrived_left, left_map, axis=1)) * live_left
        result_right = (upper + jnp.take(arrived_right, right_map, axis=1)) * live_right
        return jnp.concatenate([result_left, result_right], axis=1)

    received = (
        shifted(loads[0].astype(jnp.bfloat16), "sub", -1).astype(jnp.float32),
        shifted(weights.astype(jnp.bfloat16), "sub", -1).astype(weights.dtype),
    )
    right_load = jnp.take(received[0], right_map, axis=1) * live_right
    right_weight = jnp.take(received[1], right_map, axis=1)
    residual = jnp.concatenate([loads[0] * live_left, right_load], axis=1)
    scaling = jnp.concatenate([weights, right_weight], axis=1)
    solution = jnp.zeros_like(residual)
    precond = scaling * residual
    image = apply_operator(precond)
    gamma, delta = paired_totals(residual, precond, image, half)
    alpha = gamma / delta
    direction = precond
    along = image
    for step in range(ITERS):
        solution = solution + alpha[:, None] * direction
        residual = residual - alpha[:, None] * along
        if step + 1 < ITERS:
            precond = scaling * residual
            image = apply_operator(precond)
            gamma_next, delta = paired_totals(residual, precond, image, half)
            ratio = gamma_next / gamma
            alpha = gamma_next / (delta - ratio * gamma_next / alpha)
            direction = precond + ratio[:, None] * direction
            along = image + ratio[:, None] * along
            gamma = gamma_next
    return (solution[:, :half][None], residual[:, :half][None])


def cost(flops, moved):
    return pl.CostEstimate(flops=flops, bytes_accessed=moved, transcendentals=0)


def nt(first, second, precision=None):
    return lax.dot_general(
        first, second, (((1,), (1,)), ((), ())), preferred_element_type=F32, precision=precision
    )


def nn(first, second, precision=None):
    return jnp.dot(first, second, preferred_element_type=F32, precision=precision)


def halves(value):
    high = value.astype(BF16)
    return high, (value - high.astype(F32)).astype(BF16)


def stacked(value):
    return jnp.concatenate(halves(value), axis=0)


def thirds(value):
    high = value.astype(BF16)
    rest = value - high.astype(F32)
    middle = rest.astype(BF16)
    return high, middle, (rest - middle.astype(F32)).astype(BF16)


def pieces_sum(ref, half, count):
    total = ref[:, half : half + LANES].astype(F32)
    for piece in range(1, count):
        at = half + piece * LANES
        total = total + ref[:, at : at + LANES].astype(F32)
    return total


def neighbours():
    subdomain = lax.axis_index("sub")
    count = lax.axis_size("sub")
    return lax.rem(subdomain + count - 1, count), subdomain, lax.rem(subdomain + 1, count)


def hot_rows(ids_ref, subdomain, extent):
    ids = ids_ref[pl.ds(subdomain, 1), :]
    names = lax.broadcasted_iota(jnp.int32, (extent, ids.shape[1]), 0)
    return (names == ids).astype(F32)


def hot_names(ids_ref):
    spare = jnp.zeros((LANES, LANES - 3 * ids_ref.shape[1]), F32)
    hots = [hot_rows(ids_ref, each, LANES) for each in neighbours()]
    return jnp.concatenate([*hots, spare], axis=1)


def selected(values, names):
    high, middle, low = thirds(values)
    rows = values.shape[0]
    parts = nt(jnp.concatenate([high, middle, low], axis=0), names)
    return parts[:rows] + parts[rows : 2 * rows] + parts[2 * rows :]


def solved_backs(coarse, solver):
    rows = coarse.shape[0]
    parts = nn(stacked(coarse), solver)
    width = solver.shape[1] // 2
    return parts[:rows, :width] + (parts[:rows, width:] + parts[rows:, :width])


def open_kernel(
    sizes_in,
    loads_in,
    maps_in,
    weights_in,
    ids_in,
    inverse_in,
    right_in,
    left_in,
    pack_ref,
    skew_ref,
    loaded_ref,
    live_ref,
    weights_ref,
    ids_ref,
    inverse_ref,
    right_ref,
    left_ref,
    sizes_ref,
    loads_ref,
    maps_ref,
    sems,
):
    pairs = (
        (sizes_in, sizes_ref),
        (loads_in, loads_ref),
        (weights_in, weights_ref),
        (maps_in, maps_ref),
        (ids_in, ids_ref),
        (inverse_in, inverse_ref),
        (right_in, right_ref),
        (left_in, left_ref),
    )
    copies = [pltpu.make_async_copy(*pair, sems.at[at]) for at, pair in enumerate(pairs)]
    for copy in copies:
        copy.start()
    before, subdomain, _ = neighbours()
    for copy in copies:
        copy.wait()
    slots = lax.broadcasted_iota(jnp.int32, live_ref.shape, 1)
    which = lax.broadcasted_iota(jnp.int32, live_ref.shape, 0)
    bound = jnp.where(which == 0, sizes_ref[before], sizes_ref[subdomain])
    live = (slots < bound).astype(F32)
    live_ref[...] = live
    scale = weights_ref[...]
    loaded = jnp.where(live[0:1] > 0.0, loads_ref[...], 0.0)
    loaded_ref[...] = loaded
    first = loaded * scale
    high = scale.astype(BF16).astype(F32)
    spare = jnp.where(which == 0, high, jnp.where(which == 1, scale - high, 0.0))
    maps = maps_ref[...].astype(F32)
    pack_ref[...] = jnp.concatenate([first, maps, spare], axis=0).astype(BF16)
    short = jnp.concatenate([first, spare], axis=0)
    skew_ref[...] = jnp.where(lax.axis_index("row") == 0, short, maps).astype(BF16)


def side_columns(ref, side, half):
    return ref.at[:, pl.ds(pl.multiple_of(side * half, half), half)]


def turn(source_ref, target_ref):
    for at in range(0, source_ref.shape[1], LANES):
        block = slice(at, at + LANES)
        target_ref[block, :] = jnp.transpose(source_ref[:, block])


def select_kernel(
    right_ref,
    left_ref,
    pack_ref,
    operator_in,
    right_hot_ref,
    order_ref,
    left_hot_ref,
    square_ref,
    cross_ref,
    early_ref,
    local_ref,
    turned_ref,
    sems,
):
    half = right_ref.shape[1]
    columns = local_ref.shape[0]
    side = lax.axis_index("row")
    lower = side == 0
    square = pltpu.make_async_copy(side_columns(operator_in, side, half), square_ref, sems.at[0])
    cross = pltpu.make_async_copy(side_columns(operator_in, 1 - side, half), cross_ref, sems.at[1])

    @pl.when(lower)
    def _():
        square.start()
        cross.start()

    @pl.when(jnp.logical_not(lower))
    def _():
        cross.start()
        square.start()

    short = jnp.int16
    right = right_ref[...]
    tall = jnp.transpose(jnp.broadcast_to(right, (8, half)).astype(F32))[:, 0:1].astype(jnp.int32)
    tall = jnp.broadcast_to(tall, (half, LANES)).astype(short)
    names = lax.broadcasted_iota(jnp.int32, (LANES, LANES), 1)
    full, none = jnp.ones((LANES, half), BF16), jnp.zeros((LANES, half), BF16)
    narrow_full, narrow_none = jnp.ones((LANES, LANES), BF16), jnp.zeros((LANES, LANES), BF16)
    for at in range(half // LANES):
        rows = slice(at * LANES, (at + 1) * LANES)
        for block in range(half // LANES):
            own = (names + block * LANES).astype(short)
            hit = own == tall[rows]
            columns_at = slice(block * LANES, (block + 1) * LANES)
            order_ref[rows, columns_at] = jnp.where(hit, narrow_full, narrow_none)
    wide_right = jnp.broadcast_to(right, (LANES, half)).astype(short)
    wide_left = jnp.broadcast_to(left_ref[...], (LANES, half)).astype(short)

    def one(at, carry):
        start = pl.multiple_of(at * LANES, LANES)
        slots = (lax.broadcasted_iota(jnp.int32, (LANES, half), 0) + start).astype(short)
        rows = pl.ds(start, LANES)
        right_hot_ref[rows, :] = jnp.where(slots == wide_right, full, none)
        left_hot_ref[rows, :] = jnp.where(slots == wide_left, full, none)
        return carry

    lax.fori_loop(0, half // LANES, one, 0)
    left = pack_ref[:columns, :]

    @pl.when(lower)
    def _():
        turned_ref[...] = left
        square.wait()
        local_ref[...] = nn(left, square_ref[...])
        cross.wait()
        turn(cross_ref, early_ref)

    @pl.when(jnp.logical_not(lower))
    def _():
        turned_ref[...] = nt(left, left_hot_ref[...]).astype(BF16)
        cross.wait()
        local_ref[...] = nt(left, cross_ref[...])
        square.wait()


def first_kernel(
    ids_ref,
    square_ref,
    early_ref,
    right_hot_ref,
    order_ref,
    local_ref,
    turned_ref,
    own_pack_ref,
    across_ref,
    along_ref,
    slant_ref,
    send_ref,
    pair_ref,
):
    columns, half = local_ref.shape
    corners = ids_ref.shape[1]
    before, subdomain, after = neighbours()
    lower = lax.axis_index("row") == 0

    def coarse_part(own_side, other_side, other):
        one = nt(own_side, across_ref[...])
        two = nt(other_side, along_ref[columns:, :])[:, :corners]
        hot_own = hot_rows(ids_ref, subdomain, LANES)
        hot_other = hot_rows(ids_ref, other, LANES)
        high, low = halves(selected(one, hot_own) + selected(two, hot_other))
        send_ref[:, half:] = jnp.concatenate([high, low], axis=1)

    @pl.when(lower)
    def _():
        right = along_ref[:columns, :]
        slotted = nn(right, right_hot_ref[...]).astype(BF16)
        coarse_part(slotted, right, after)
        send_ref[:, :half] = (local_ref[...] + nn(slotted, early_ref[...])).astype(BF16)

    @pl.when(jnp.logical_not(lower))
    def _():
        slotted = nn(slant_ref[:columns, :], right_hot_ref[...]).astype(BF16)
        coarse_part(own_pack_ref[:columns, :], turned_ref[...], before)
        local = (local_ref[...] + nn(slotted, square_ref[...])).astype(BF16)
        send_ref[:, :half] = nn(local, order_ref[...]).astype(BF16)

    wide = send_ref.shape[1]
    relayed = own_pack_ref[columns : columns + corners, :].astype(F32)
    tail = relayed[columns:]
    tail = jnp.concatenate([tail[:, : half // 2], tail[:, half // 2 :]], axis=0)
    pair_ref[:, :wide] = send_ref[...]
    pair_ref[:, wide:] = jnp.concatenate([relayed[:columns], tail], axis=1).astype(BF16)


def order_kernel(
    ids_ref,
    inverse_ref,
    order_ref,
    left_hot_ref,
    cross_ref,
    own_pack_ref,
    across_ref,
    along_ref,
    slant_ref,
    maps_ref,
    solver_ref,
    scale_ref,
    names_ref,
    late_ref,
):
    half = order_ref.shape[1]
    corners = ids_ref.shape[1]
    width = inverse_ref.shape[0]
    columns = own_pack_ref.shape[0] - corners - 8
    lower = lax.axis_index("row") == 0
    own, across = own_pack_ref[columns:, :].astype(F32)[:corners], across_ref[...].astype(F32)
    along, slant = along_ref[columns:, :].astype(F32), slant_ref[...].astype(F32)
    behind = jnp.where(lower, slant, along[:corners])
    ahead = jnp.where(lower, along[:corners], 0.0)
    scales = jnp.where(lower, along[corners:], slant[columns:])
    scale_ref[...] = scales[0:1] + scales[1:2]
    raw = jnp.where(lower, across, own).astype(BF16)
    ordered = nn(raw, order_ref[...])
    turned = nn(behind.astype(BF16), left_hot_ref[...])
    spare = jnp.zeros((LANES - 3 * corners, half), F32)
    blank = jnp.zeros((corners, half), F32)
    mine = jnp.where(lower, own, across)
    maps_ref[:, :half] = jnp.concatenate([turned, mine, blank, spare], axis=0).astype(BF16)
    maps_ref[:, half:] = jnp.concatenate([blank, ordered, ahead, spare], axis=0).astype(BF16)
    names = hot_names(ids_ref)
    names_ref[...] = names.astype(BF16)
    backs = nn(inverse_ref[...], names[:width], HIGH)
    low_rows = jnp.zeros((LANES - width, LANES), F32)
    side = jnp.concatenate([inverse_ref[...], jnp.zeros((width, LANES - width), F32)], axis=1)
    pieces = []
    for piece in (backs, side):
        tall = jnp.concatenate([piece, low_rows], axis=0)
        pieces.extend(halves(tall))
    solver_ref[...] = jnp.concatenate(pieces, axis=1)

    @pl.when(jnp.logical_not(lower))
    def _():
        turn(cross_ref, late_ref)


def second_kernel(
    names_ref,
    solver_ref,
    maps_ref,
    right_hot_ref,
    order_ref,
    square_ref,
    early_ref,
    late_ref,
    live_ref,
    loaded_ref,
    weights_ref,
    scale_ref,
    own_ref,
    across_ref,
    along_ref,
    slant_ref,
    image_ref,
    next_ref,
    up_ref,
    small_ref,
):
    lower = lax.axis_index("row") == 0
    columns, half = loaded_ref.shape
    own, across = own_ref[:, :half].astype(F32), across_ref[:, :half].astype(F32)
    along, slant = along_ref[:, :half].astype(F32), slant_ref[:, :half].astype(F32)
    mine = pieces_sum(own_ref, half, 2) + pieces_sum(across_ref, half, 2)
    coarse = mine + (pieces_sum(along_ref, half, 2) + pieces_sum(slant_ref, half, 2))
    backs = solved_backs(coarse, solver_ref[:, : 2 * LANES]).astype(BF16)
    fix = nn(backs, maps_ref[...])
    image = jnp.where(lower, own, across) + jnp.where(lower, slant, along) + fix[:, :half]
    image = jnp.where(live_ref[0:1] > 0.0, image, 0.0)
    wide = own_ref.shape[1]
    half_rows = columns // 2
    tail = slant_ref[:, wide + half :].astype(F32)
    tail = jnp.concatenate([tail[:half_rows], tail[half_rows:]], axis=1)
    relayed = jnp.concatenate([slant_ref[:, wide : wide + half].astype(F32), tail], axis=0)
    count = relayed.shape[0]
    more = nn(backs[:, 2 * count : 3 * count], relayed.astype(BF16))
    fix_right = fix[:, half:] + jnp.where(lower, 0.0, more)
    image_right = jnp.where(lower, across, own) + jnp.where(lower, along, slant) + fix_right
    image_right = jnp.where(live_ref[1:2] > 0.0, image_right, 0.0)
    left = weights_ref[...] * image
    right = scale_ref[...] * image_right
    image_ref[...] = image
    next_ref[...] = left
    left_2, right_2 = left.astype(BF16), right.astype(BF16)

    def totals(block, local, corner):
        loaded = loaded_ref[...]
        first = loaded * weights_ref[...]
        pairs = ((loaded, first), (first, image), (image, left), (block, local))
        lane = lax.broadcasted_iota(jnp.int32, (columns, LANES), 1)
        small = selected(corner, names_ref[...])
        for at, (one, other) in enumerate(pairs):
            value = jnp.sum(one * other, axis=1, keepdims=True)
            small = jnp.where(lane == LANES - len(pairs) + at, value, small)
        small_ref[...] = small
        up_ref[:, half:] = jnp.concatenate(thirds(small), axis=1)

    @pl.when(lower)
    def _():
        local = nn(left_2, square_ref[...])
        slotted_2 = nn(right_2, right_hot_ref[...]).astype(BF16)
        corner = nt(right_2, maps_ref[:, half:])
        local = local + nn(slotted_2, early_ref[...])
        up_ref[:, :half] = local.astype(BF16)
        totals(left_2.astype(F32), local, corner)

    @pl.when(jnp.logical_not(lower))
    def _():
        slotted_2 = nn(right_2, right_hot_ref[...]).astype(BF16)
        local = nn(left_2, late_ref[...])
        corner = nt(left_2, maps_ref[:, :half])
        local = local + nn(slotted_2, square_ref[...])
        up_ref[:, :half] = nn(local.astype(BF16), order_ref[...]).astype(BF16)
        totals(slotted_2.astype(F32), local, corner)


def relay_kernel(up_own_ref, up_ref, down_ref, far_ref, own_ref, out_ref):
    lower = lax.axis_index("row") == 0
    half = up_ref.shape[1] - 3 * LANES
    total = own_ref[...] + pieces_sum(up_ref, half, 3)
    total = total + down_ref[...] + far_ref[...]
    out_ref[:, :half] = jnp.where(lower, up_own_ref[:, :half], up_ref[:, :half])
    out_ref[:, half:] = jnp.concatenate(thirds(total), axis=1)


def close_kernel(
    solver_ref,
    maps_ref,
    live_ref,
    loaded_ref,
    weights_ref,
    image_ref,
    next_ref,
    mine_ref,
    theirs_ref,
    solution_ref,
    residual_ref,
):
    lower = lax.axis_index("row") == 0
    columns, half = loaded_ref.shape
    mine, theirs = pieces_sum(mine_ref, half, 3), pieces_sum(theirs_ref, half, 3)
    total = jnp.where(lower, mine, theirs)
    lane = lax.broadcasted_iota(jnp.int32, (columns, LANES), 1)
    coarse = jnp.where(lane < LANES - 4, total, 0.0)
    backs = solved_backs(coarse, solver_ref[:, : 2 * LANES]).astype(BF16)
    solved = solved_backs(coarse, solver_ref[:, 2 * LANES :])
    fix = nn(backs, maps_ref[:, :half])
    image_next = mine_ref[:, :half].astype(F32) + theirs_ref[:, :half].astype(F32) + fix
    image_next = jnp.where(live_ref[0:1] > 0.0, image_next, 0.0)

    def column(values, at):
        return jnp.sum(jnp.where(lane == LANES - 4 + at, values, 0.0), axis=1, keepdims=True)

    gamma = column(total, 0)
    delta = column(total, 1)
    cross = column(total, 2)
    energy = column(mine + theirs, 3) + jnp.sum(coarse * solved, axis=1, keepdims=True)
    alpha = gamma / delta
    gamma_next = gamma - 2.0 * alpha * delta + alpha * alpha * cross
    ratio = gamma_next / gamma
    grown = 1.0 + ratio
    curvature = grown * grown * delta - 2.0 * grown * alpha * cross + alpha * alpha * energy
    alpha_next = gamma_next / curvature
    loaded = loaded_ref[...]
    first = loaded * weights_ref[...]
    direction = grown * first - alpha * next_ref[...]
    along = grown * image_ref[...] - alpha * image_next
    solution_ref[...] = alpha * first + alpha_next * direction
    residual_ref[...] = loaded - alpha * image_ref[...] - alpha_next * along


def ring(
    loads,
    weights,
    dual_ops,
    corner_maps,
    coarse_inverse,
    corner_ids,
    iface_sizes,
    left_partner,
    right_partner,
):
    count = lax.axis_size("sub")
    sides = lax.axis_size("row")
    columns, half = loads.shape[1:]
    corners = corner_maps.shape[1]
    operator = dual_ops[0]
    own_map = corner_maps[0]
    loaded = loads[0]
    block = operator.shape[0]
    shape = jax.ShapeDtypeStruct
    grid = ("sub", "row")
    big = 2 * columns * block * 2 * half

    def pairs(target):
        listed = []
        for at in range(count):
            for side in range(sides):
                to_at, to_side = target(at, side)
                listed.append((at * sides + side, (to_at % count) * sides + to_side))
        return listed

    across = pairs(lambda at, side: (at, 1 - side))
    along = pairs(lambda at, side: (at - 1, 0) if side == 0 else (at + 1, 1))
    slant = pairs(lambda at, side: (at - 1, 1) if side == 0 else (at + 1, 0))

    def call(kernel, operands, outs, scratch=(), flops=0, moved=0, room=4):
        specs, placed = [], []
        for operand in operands:
            held = isinstance(operand, tuple)
            specs.append(HBM if held else VMEM)
            placed.append(
                pltpu.with_memory_space_constraint(operand[0], pltpu.HBM) if held else operand
            )
        return pl.pallas_call(
            kernel,
            in_specs=specs,
            out_specs=[VMEM] * len(outs),
            out_shape=[shape(*out) for out in outs],
            scratch_shapes=scratch,
            cost_estimate=cost(flops, moved),
            compiler_params=pltpu.CompilerParams(vmem_limit_bytes=room << 20),
        )(*placed)

    rows = columns + corners + 8
    arguments = (weights, corner_ids, coarse_inverse, right_partner, left_partner)
    pack, skew, load, live, scale, ids, inverse, right_map, left_map = call(
        open_kernel,
        [(array,) for array in (iface_sizes, loaded, own_map, *arguments)],
        [((rows, half), BF16), ((columns + 8, half), BF16)]
        + [((columns, half), F32), ((8, half), F32)]
        + [(array.shape, array.dtype) for array in arguments],
        scratch=[
            pltpu.SMEM(iface_sizes.shape, jnp.int32),
            pltpu.VMEM(loaded.shape, F32),
            pltpu.VMEM(own_map.shape, BF16),
            pltpu.SemaphoreType.DMA((8,)),
        ],
        moved=4 * rows * half,
    )
    pack_slant = lax.ppermute(skew, grid, slant)
    pack_along = lax.ppermute(pack, grid, along)
    map_across = lax.ppermute(own_map, grid, across)
    right_hot, order, left_hot, square, cross, early, local_left, turned = call(
        select_kernel,
        [right_map, left_map, pack, (operator,)],
        [((half, half), BF16)] * 3
        + [((block, half), BF16)] * 3
        + [((columns, block), F32), ((columns, half), BF16)],
        scratch=[pltpu.SemaphoreType.DMA((2,))],
        flops=big,
        moved=4 * half * half,
        room=16,
    )
    wide = half + 2 * LANES
    send, pair = call(
        first_kernel,
        [
            ids,
            square,
            early,
            right_hot,
            order,
            local_left,
            turned,
            pack,
            map_across,
            pack_along,
            pack_slant,
        ],
        [((columns, wide), BF16), ((columns, wide + half + half // 2), BF16)],
        flops=2 * big,
        moved=4 * block * half,
        room=16,
    )
    send_slant = lax.ppermute(pair, grid, slant)
    send_along = lax.ppermute(send, grid, along)
    send_across = lax.ppermute(send, grid, across)
    maps, solver, scale_right, names, late = call(
        order_kernel,
        [ids, inverse, order, left_hot, cross, pack, map_across, pack_along, pack_slant],
        [
            ((LANES, 2 * half), BF16),
            ((LANES, 4 * LANES), BF16),
            ((1, half), F32),
            ((LANES, LANES), BF16),
            ((half, block), BF16),
        ],
        flops=4 * corners * half * half,
        moved=4 * half * half,
        room=12,
    )
    image, following, up, small = call(
        second_kernel,
        [
            names,
            solver,
            maps,
            right_hot,
            order,
            square,
            early,
            late,
            live,
            load,
            scale,
            scale_right,
            send,
            send_across,
            send_along,
            send_slant,
        ],
        [
            ((columns, half), F32),
            ((columns, half), F32),
            ((columns, half + 3 * LANES), BF16),
            ((columns, LANES), F32),
        ],
        flops=2 * big,
        moved=4 * block * half,
        room=16,
    )
    far_in = shifted(small, "sub", 2)
    down_in = shifted(small, "sub", -1)
    up_in = shifted(up, "sub", 1)
    (mine,) = call(
        relay_kernel,
        [up, up_in, down_in, far_in, small],
        [((columns, half + 3 * LANES), BF16)],
        moved=8 * columns * half,
    )
    theirs = lax.ppermute(mine, grid, across)
    solution, residual = call(
        close_kernel,
        [solver, maps, live, load, scale, image, following, mine, theirs],
        [((columns, half), F32), ((columns, half), F32)],
        moved=24 * columns * half,
    )
    return solution[None], residual[None]


def per_device(*arrays):
    loads, _, dual_ops, corner_maps, coarse_inverse = arrays[:5]
    half = loads.shape[2]
    neighbourly = lax.axis_size("sub") == 4 and lax.axis_size("row") == 2
    sided = dual_ops.shape[1] == half and half % LANES == 0
    columns, corners = loads.shape[1], corner_maps.shape[1]
    fitting = columns % 16 == 0 and corners == columns + columns // 2 and corners == columns + 8
    narrow = coarse_inverse.shape[0] + 4 <= LANES and 3 * corner_maps.shape[1] <= LANES
    if neighbourly and sided and fitting and narrow and ITERS == 2:
        return ring(*arrays)
    return general(*arrays)


def solution(mesh):
    placed = (
        P(("parts", "sub"), "col", None),
        P(("parts", "sub"), None),
        P(("parts", "sub"), "row", None),
        P(("parts", "sub"), None, "row"),
        P("parts", None),
        P("parts", None),
        P("parts"),
        P(("parts", "sub"), None),
        P(("parts", "sub"), None),
    )
    return jax.shard_map(
        per_device,
        mesh=mesh,
        in_specs=placed,
        out_specs=(P(("parts", "sub"), "col", None), P(("parts", "sub"), "col", None)),
        check_vma=False,
    )
```

```python
import jax
import jax.numpy as jnp
from jax import lax
from jax.experimental import pallas as pl
from jax.experimental.pallas import tpu as pltpu
from jax.sharding import PartitionSpec as P

TILE = 128
LANES = 128
ITERS = 2
F32 = jnp.float32
BF16 = jnp.bfloat16
HIGH = lax.Precision.HIGHEST
VMEM = pl.BlockSpec(memory_space=pltpu.VMEM)
HBM = pl.BlockSpec(memory_space=pltpu.HBM)


def shifted(value, axis, steps):
    count = lax.axis_size(axis)
    pairs = [(source, (source + steps) % count) for source in range(count)]
    return lax.ppermute(value, axis, pairs)


def inner(first, second, half):
    return jnp.sum(first[:, :half] * second[:, :half], axis=1)


def paired_totals(residual, precond, image, half):
    return lax.psum((inner(residual, precond, half), inner(precond, image, half)), "sub")


def tile_products(vector, rows_op, first_tile, last_tile, output):

    def one_tile(tile_at, acc):
        piece = lax.dynamic_slice_in_dim(rows_op, tile_at * TILE, TILE, 0)
        product = lax.dot_general(
            vector, piece, (((1,), (1,)), ((), ())), preferred_element_type=jnp.float32
        )
        return lax.dynamic_update_slice_in_dim(acc, product, tile_at * TILE, 1)

    return lax.fori_loop(first_tile, last_tile, one_tile, output)


def live_tiles(size_before, size_after, block_start, block, half):
    left_live = jnp.clip(size_before - block_start, 0, block)
    right_live = jnp.clip(size_after - (block_start - half), 0, block)
    live_cols = jnp.where(block_start < half, left_live, right_live)
    return (live_cols + TILE - 1) // TILE


def general(
    loads,
    weights,
    dual_ops,
    corner_maps,
    coarse_inverse,
    corner_ids,
    iface_sizes,
    left_partner,
    right_partner,
):
    half = loads.shape[2]
    block = dual_ops.shape[1]
    width = coarse_inverse.shape[0]
    subdomain = lax.axis_index("sub")
    count = lax.axis_size("sub")
    row_index = lax.axis_index("row")
    left_map = left_partner[0]
    right_map = right_partner[0]
    slots = jnp.arange(half, dtype=jnp.int32)
    size_before = iface_sizes[(subdomain + count - 1) % count]
    size_after = iface_sizes[subdomain]
    live_left = (slots < size_before).astype(jnp.float32)
    live_right = (right_map < size_after).astype(jnp.float32)
    columns = jnp.arange(width, dtype=jnp.int32)
    own_hot = (corner_ids[subdomain][:, None] == columns[None, :]).astype(jnp.float32)
    operator = dual_ops[0]
    coupling = corner_maps[0]
    block_start = row_index * block
    own_tiles = live_tiles(size_before, size_after, block_start, block, half)

    def apply_operator(vec):
        halfway = vec.astype(jnp.bfloat16)
        empty = jnp.zeros((halfway.shape[0], block), jnp.float32)
        local = tile_products(halfway, operator, jnp.int32(0), own_tiles, empty)
        own_slots = lax.dynamic_slice_in_dim(halfway, row_index * block, block, 1)
        corner = lax.dot_general(
            own_slots, coupling, (((1,), (1,)), ((), ())), preferred_element_type=jnp.float32
        )
        scattered = jnp.dot(corner, own_hot, precision=lax.Precision.HIGHEST)
        coarse = lax.psum(scattered, ("sub", "row"))
        solved = jnp.dot(coarse, coarse_inverse, precision=lax.Precision.HIGHEST)
        back = lax.dot_general(
            solved, own_hot, (((1,), (1,)), ((), ())), precision=lax.Precision.HIGHEST
        ).astype(jnp.bfloat16)
        united = local + jnp.dot(back, coupling, preferred_element_type=jnp.float32)
        whole = lax.all_gather(united.astype(jnp.bfloat16), "row", axis=1, tiled=True).astype(
            united.dtype
        )
        lower = whole[:, :half]
        upper = whole[:, half:]
        arrived_left = shifted(upper.astype(jnp.bfloat16), "sub", 1).astype(upper.dtype)
        arrived_right = shifted(lower.astype(jnp.bfloat16), "sub", -1).astype(lower.dtype)
        result_left = (lower + jnp.take(arrived_left, left_map, axis=1)) * live_left
        result_right = (upper + jnp.take(arrived_right, right_map, axis=1)) * live_right
        return jnp.concatenate([result_left, result_right], axis=1)

    received = (
        shifted(loads[0].astype(jnp.bfloat16), "sub", -1).astype(jnp.float32),
        shifted(weights.astype(jnp.bfloat16), "sub", -1).astype(weights.dtype),
    )
    right_load = jnp.take(received[0], right_map, axis=1) * live_right
    right_weight = jnp.take(received[1], right_map, axis=1)
    residual = jnp.concatenate([loads[0] * live_left, right_load], axis=1)
    scaling = jnp.concatenate([weights, right_weight], axis=1)
    solution = jnp.zeros_like(residual)
    precond = scaling * residual
    image = apply_operator(precond)
    gamma, delta = paired_totals(residual, precond, image, half)
    alpha = gamma / delta
    direction = precond
    along = image
    for step in range(ITERS):
        solution = solution + alpha[:, None] * direction
        residual = residual - alpha[:, None] * along
        if step + 1 < ITERS:
            precond = scaling * residual
            image = apply_operator(precond)
            gamma_next, delta = paired_totals(residual, precond, image, half)
            ratio = gamma_next / gamma
            alpha = gamma_next / (delta - ratio * gamma_next / alpha)
            direction = precond + ratio[:, None] * direction
            along = image + ratio[:, None] * along
            gamma = gamma_next
    return (solution[:, :half][None], residual[:, :half][None])


def cost(flops, moved):
    return pl.CostEstimate(flops=flops, bytes_accessed=moved, transcendentals=0)


def nt(first, second, precision=None):
    return lax.dot_general(
        first, second, (((1,), (1,)), ((), ())), preferred_element_type=F32, precision=precision
    )


def nn(first, second, precision=None):
    return jnp.dot(first, second, preferred_element_type=F32, precision=precision)


def halves(value):
    high = value.astype(BF16)
    return high, (value - high.astype(F32)).astype(BF16)


def stacked(value):
    return jnp.concatenate(halves(value), axis=0)


def thirds(value):
    high = value.astype(BF16)
    rest = value - high.astype(F32)
    middle = rest.astype(BF16)
    return high, middle, (rest - middle.astype(F32)).astype(BF16)


def pieces_sum(ref, half, count):
    total = ref[:, half : half + LANES].astype(F32)
    for piece in range(1, count):
        at = half + piece * LANES
        total = total + ref[:, at : at + LANES].astype(F32)
    return total


def neighbours():
    subdomain = lax.axis_index("sub")
    count = lax.axis_size("sub")
    return lax.rem(subdomain + count - 1, count), subdomain, lax.rem(subdomain + 1, count)


def hot_rows(ids_ref, subdomain, extent):
    ids = ids_ref[pl.ds(subdomain, 1), :]
    names = lax.broadcasted_iota(jnp.int32, (extent, ids.shape[1]), 0)
    return (names == ids).astype(F32)


def hot_names(ids_ref):
    spare = jnp.zeros((LANES, LANES - 3 * ids_ref.shape[1]), F32)
    hots = [hot_rows(ids_ref, each, LANES) for each in neighbours()]
    return jnp.concatenate([*hots, spare], axis=1)


def selected(values, names):
    high, middle, low = thirds(values)
    rows = values.shape[0]
    parts = nt(jnp.concatenate([high, middle, low], axis=0), names)
    return parts[:rows] + parts[rows : 2 * rows] + parts[2 * rows :]


def solved_backs(coarse, solver):
    rows = coarse.shape[0]
    parts = nn(stacked(coarse), solver)
    width = solver.shape[1] // 2
    return parts[:rows, :width] + (parts[:rows, width:] + parts[rows:, :width])


def open_kernel(
    sizes_in,
    loads_in,
    maps_in,
    weights_in,
    ids_in,
    inverse_in,
    right_in,
    left_in,
    pack_ref,
    skew_ref,
    loaded_ref,
    live_ref,
    weights_ref,
    ids_ref,
    inverse_ref,
    right_ref,
    left_ref,
    sizes_ref,
    loads_ref,
    maps_ref,
    sems,
):
    pairs = (
        (sizes_in, sizes_ref),
        (loads_in, loads_ref),
        (weights_in, weights_ref),
        (maps_in, maps_ref),
        (ids_in, ids_ref),
        (inverse_in, inverse_ref),
        (right_in, right_ref),
        (left_in, left_ref),
    )
    copies = [pltpu.make_async_copy(*pair, sems.at[at]) for at, pair in enumerate(pairs)]
    for copy in copies:
        copy.start()
    before, subdomain, _ = neighbours()
    for copy in copies:
        copy.wait()
    slots = lax.broadcasted_iota(jnp.int32, live_ref.shape, 1)
    which = lax.broadcasted_iota(jnp.int32, live_ref.shape, 0)
    bound = jnp.where(which == 0, sizes_ref[before], sizes_ref[subdomain])
    live = (slots < bound).astype(F32)
    live_ref[...] = live
    scale = weights_ref[...]
    loaded = jnp.where(live[0:1] > 0.0, loads_ref[...], 0.0)
    loaded_ref[...] = loaded
    first = loaded * scale
    high = scale.astype(BF16).astype(F32)
    spare = jnp.where(which == 0, high, jnp.where(which == 1, scale - high, 0.0))
    maps = maps_ref[...].astype(F32)
    pack_ref[...] = jnp.concatenate([first, maps, spare], axis=0).astype(BF16)
    short = jnp.concatenate([first, spare], axis=0)
    skew_ref[...] = jnp.where(lax.axis_index("row") == 0, short, maps).astype(BF16)


def side_columns(ref, side, half):
    return ref.at[:, pl.ds(pl.multiple_of(side * half, half), half)]


def turn(source_ref, target_ref):
    for at in range(0, source_ref.shape[1], LANES):
        block = slice(at, at + LANES)
        target_ref[block, :] = jnp.transpose(source_ref[:, block])


def select_kernel(
    right_ref,
    left_ref,
    pack_ref,
    operator_in,
    right_hot_ref,
    order_ref,
    left_hot_ref,
    square_ref,
    cross_ref,
    early_ref,
    local_ref,
    turned_ref,
    sems,
):
    half = right_ref.shape[1]
    columns = local_ref.shape[0]
    side = lax.axis_index("row")
    lower = side == 0
    square = pltpu.make_async_copy(side_columns(operator_in, side, half), square_ref, sems.at[0])
    cross = pltpu.make_async_copy(side_columns(operator_in, 1 - side, half), cross_ref, sems.at[1])

    @pl.when(lower)
    def _():
        square.start()
        cross.start()

    @pl.when(jnp.logical_not(lower))
    def _():
        cross.start()
        square.start()

    short = jnp.int16
    right = right_ref[...]
    tall = jnp.transpose(jnp.broadcast_to(right, (8, half)).astype(F32))[:, 0:1].astype(jnp.int32)
    tall = jnp.broadcast_to(tall, (half, LANES)).astype(short)
    names = lax.broadcasted_iota(jnp.int32, (LANES, LANES), 1)
    full, none = jnp.ones((LANES, half), BF16), jnp.zeros((LANES, half), BF16)
    narrow_full, narrow_none = jnp.ones((LANES, LANES), BF16), jnp.zeros((LANES, LANES), BF16)
    for at in range(half // LANES):
        rows = slice(at * LANES, (at + 1) * LANES)
        for block in range(half // LANES):
            own = (names + block * LANES).astype(short)
            hit = own == tall[rows]
            columns_at = slice(block * LANES, (block + 1) * LANES)
            order_ref[rows, columns_at] = jnp.where(hit, narrow_full, narrow_none)
    wide_right = jnp.broadcast_to(right, (LANES, half)).astype(short)
    wide_left = jnp.broadcast_to(left_ref[...], (LANES, half)).astype(short)

    def one(at, carry):
        start = pl.multiple_of(at * LANES, LANES)
        slots = (lax.broadcasted_iota(jnp.int32, (LANES, half), 0) + start).astype(short)
        rows = pl.ds(start, LANES)
        right_hot_ref[rows, :] = jnp.where(slots == wide_right, full, none)
        left_hot_ref[rows, :] = jnp.where(slots == wide_left, full, none)
        return carry

    lax.fori_loop(0, half // LANES, one, 0)
    left = pack_ref[:columns, :]

    @pl.when(lower)
    def _():
        turned_ref[...] = left
        square.wait()
        local_ref[...] = nn(left, square_ref[...])
        cross.wait()
        turn(cross_ref, early_ref)

    @pl.when(jnp.logical_not(lower))
    def _():
        turned_ref[...] = nt(left, left_hot_ref[...]).astype(BF16)
        cross.wait()
        local_ref[...] = nt(left, cross_ref[...])
        square.wait()


def first_kernel(
    ids_ref,
    square_ref,
    early_ref,
    right_hot_ref,
    order_ref,
    local_ref,
    turned_ref,
    own_pack_ref,
    across_ref,
    along_ref,
    slant_ref,
    send_ref,
    pair_ref,
):
    columns, half = local_ref.shape
    corners = ids_ref.shape[1]
    before, subdomain, after = neighbours()
    lower = lax.axis_index("row") == 0

    def coarse_part(own_side, other_side, other):
        one = nt(own_side, across_ref[...])
        two = nt(other_side, along_ref[columns:, :])[:, :corners]
        hot_own = hot_rows(ids_ref, subdomain, LANES)
        hot_other = hot_rows(ids_ref, other, LANES)
        high, low = halves(selected(one, hot_own) + selected(two, hot_other))
        send_ref[:, half:] = jnp.concatenate([high, low], axis=1)

    @pl.when(lower)
    def _():
        right = along_ref[:columns, :]
        slotted = nn(right, right_hot_ref[...]).astype(BF16)
        coarse_part(slotted, right, after)
        send_ref[:, :half] = (local_ref[...] + nn(slotted, early_ref[...])).astype(BF16)

    @pl.when(jnp.logical_not(lower))
    def _():
        slotted = nn(slant_ref[:columns, :], right_hot_ref[...]).astype(BF16)
        coarse_part(own_pack_ref[:columns, :], turned_ref[...], before)
        local = (local_ref[...] + nn(slotted, square_ref[...])).astype(BF16)
        send_ref[:, :half] = nn(local, order_ref[...]).astype(BF16)

    wide = send_ref.shape[1]
    relayed = along_ref[columns : columns + corners, :].astype(F32)
    tail = relayed[columns:]
    tail = jnp.concatenate([tail[:, : half // 2], tail[:, half // 2 :]], axis=0)
    pair_ref[:, :wide] = send_ref[...]
    pair_ref[:, wide:] = jnp.concatenate([relayed[:columns], tail], axis=1).astype(BF16)


def order_kernel(
    ids_ref,
    inverse_ref,
    order_ref,
    left_hot_ref,
    cross_ref,
    own_pack_ref,
    across_ref,
    along_ref,
    slant_ref,
    maps_ref,
    solver_ref,
    scale_ref,
    names_ref,
    late_ref,
):
    half = order_ref.shape[1]
    corners = ids_ref.shape[1]
    width = inverse_ref.shape[0]
    columns = own_pack_ref.shape[0] - corners - 8
    lower = lax.axis_index("row") == 0
    own, across = own_pack_ref[columns:, :].astype(F32)[:corners], across_ref[...].astype(F32)
    along, slant = along_ref[columns:, :].astype(F32), slant_ref[...].astype(F32)
    behind = jnp.where(lower, slant, along[:corners])
    ahead = jnp.where(lower, along[:corners], 0.0)
    scales = jnp.where(lower, along[corners:], slant[columns:])
    scale_ref[...] = scales[0:1] + scales[1:2]
    raw = jnp.where(lower, across, own).astype(BF16)
    ordered = nn(raw, order_ref[...])
    turned = nn(behind.astype(BF16), left_hot_ref[...])
    spare = jnp.zeros((LANES - 3 * corners, half), F32)
    blank = jnp.zeros((corners, half), F32)
    mine = jnp.where(lower, own, across)
    maps_ref[:, :half] = jnp.concatenate([turned, mine, blank, spare], axis=0).astype(BF16)
    maps_ref[:, half:] = jnp.concatenate([blank, ordered, ahead, spare], axis=0).astype(BF16)
    names = hot_names(ids_ref)
    names_ref[...] = names.astype(BF16)
    backs = nn(inverse_ref[...], names[:width], HIGH)
    low_rows = jnp.zeros((LANES - width, LANES), F32)
    side = jnp.concatenate([inverse_ref[...], jnp.zeros((width, LANES - width), F32)], axis=1)
    pieces = []
    for piece in (backs, side):
        tall = jnp.concatenate([piece, low_rows], axis=0)
        pieces.extend(halves(tall))
    solver_ref[...] = jnp.concatenate(pieces, axis=1)

    @pl.when(jnp.logical_not(lower))
    def _():
        turn(cross_ref, late_ref)


def second_kernel(
    names_ref,
    solver_ref,
    maps_ref,
    right_hot_ref,
    order_ref,
    square_ref,
    early_ref,
    late_ref,
    live_ref,
    loaded_ref,
    weights_ref,
    scale_ref,
    own_ref,
    across_ref,
    along_ref,
    slant_ref,
    image_ref,
    next_ref,
    up_ref,
    small_ref,
):
    lower = lax.axis_index("row") == 0
    columns, half = loaded_ref.shape
    own, across = own_ref[:, :half].astype(F32), across_ref[:, :half].astype(F32)
    along, slant = along_ref[:, :half].astype(F32), slant_ref[:, :half].astype(F32)
    mine = pieces_sum(own_ref, half, 2) + pieces_sum(across_ref, half, 2)
    coarse = mine + (pieces_sum(along_ref, half, 2) + pieces_sum(slant_ref, half, 2))
    backs = solved_backs(coarse, solver_ref[:, : 2 * LANES]).astype(BF16)
    fix = nn(backs, maps_ref[...])
    image = jnp.where(lower, own, across) + jnp.where(lower, slant, along) + fix[:, :half]
    image = jnp.where(live_ref[0:1] > 0.0, image, 0.0)
    wide = own_ref.shape[1]
    half_rows = columns // 2
    tail = across_ref[:, wide + half :].astype(F32)
    tail = jnp.concatenate([tail[:half_rows], tail[half_rows:]], axis=1)
    relayed = jnp.concatenate([across_ref[:, wide : wide + half].astype(F32), tail], axis=0)
    count = relayed.shape[0]
    more = nn(backs[:, 2 * count : 3 * count], relayed.astype(BF16))
    fix_right = fix[:, half:] + jnp.where(lower, 0.0, more)
    image_right = jnp.where(lower, across, own) + jnp.where(lower, along, slant) + fix_right
    image_right = jnp.where(live_ref[1:2] > 0.0, image_right, 0.0)
    left = weights_ref[...] * image
    right = scale_ref[...] * image_right
    image_ref[...] = image
    next_ref[...] = left
    left_2, right_2 = left.astype(BF16), right.astype(BF16)
    loaded = loaded_ref[...]
    first = loaded * weights_ref[...]
    sums = [
        jnp.sum(loaded * first, axis=1, keepdims=True),
        jnp.sum(first * image, axis=1, keepdims=True),
        jnp.sum(image * left, axis=1, keepdims=True),
    ]
    lane = lax.broadcasted_iota(jnp.int32, (columns, LANES), 1)

    def totals(block, local, corner):
        energy = jnp.sum(block * local, axis=1, keepdims=True)
        small = selected(corner, names_ref[...])
        for at, value in enumerate([*sums, energy]):
            small = jnp.where(lane == LANES - len(sums) - 1 + at, value, small)
        small_ref[...] = small
        up_ref[:, half:] = jnp.concatenate(halves(small), axis=1)

    @pl.when(lower)
    def _():
        local = nn(left_2, square_ref[...])
        slotted_2 = nn(right_2, right_hot_ref[...]).astype(BF16)
        corner = nt(right_2, maps_ref[:, half:])
        local = local + nn(slotted_2, early_ref[...])
        up_ref[:, :half] = local.astype(BF16)
        totals(left_2.astype(F32), local, corner)

    @pl.when(jnp.logical_not(lower))
    def _():
        slotted_2 = nn(right_2, right_hot_ref[...]).astype(BF16)
        local = nn(left_2, late_ref[...])
        corner = nt(left_2, maps_ref[:, :half])
        local = local + nn(slotted_2, square_ref[...])
        up_ref[:, :half] = nn(local.astype(BF16), order_ref[...]).astype(BF16)
        totals(slotted_2.astype(F32), local, corner)


def relay_kernel(up_own_ref, up_ref, down_ref, far_ref, own_ref, out_ref):
    lower = lax.axis_index("row") == 0
    half = up_ref.shape[1] - 2 * LANES
    total = own_ref[...] + pieces_sum(up_ref, half, 2)
    total = total + down_ref[...] + far_ref[...]
    out_ref[:, :half] = jnp.where(lower, up_own_ref[:, :half], up_ref[:, :half])
    out_ref[:, half:] = jnp.concatenate(halves(total), axis=1)


def close_kernel(
    solver_ref,
    maps_ref,
    live_ref,
    loaded_ref,
    weights_ref,
    image_ref,
    next_ref,
    mine_ref,
    theirs_ref,
    solution_ref,
    residual_ref,
):
    lower = lax.axis_index("row") == 0
    columns, half = loaded_ref.shape
    mine, theirs = pieces_sum(mine_ref, half, 2), pieces_sum(theirs_ref, half, 2)
    total = jnp.where(lower, mine, theirs)
    lane = lax.broadcasted_iota(jnp.int32, (columns, LANES), 1)
    coarse = jnp.where(lane < LANES - 4, total, 0.0)
    backs = solved_backs(coarse, solver_ref[:, : 2 * LANES]).astype(BF16)
    solved = solved_backs(coarse, solver_ref[:, 2 * LANES :])
    fix = nn(backs, maps_ref[:, :half])
    image_next = mine_ref[:, :half].astype(F32) + theirs_ref[:, :half].astype(F32) + fix
    image_next = jnp.where(live_ref[0:1] > 0.0, image_next, 0.0)

    def column(values, at):
        return jnp.sum(jnp.where(lane == LANES - 4 + at, values, 0.0), axis=1, keepdims=True)

    gamma = column(total, 0)
    delta = column(total, 1)
    cross = column(total, 2)
    energy = column(mine + theirs, 3) + jnp.sum(coarse * solved, axis=1, keepdims=True)
    alpha = gamma / delta
    gamma_next = gamma - 2.0 * alpha * delta + alpha * alpha * cross
    ratio = gamma_next / gamma
    grown = 1.0 + ratio
    curvature = grown * grown * delta - 2.0 * grown * alpha * cross + alpha * alpha * energy
    alpha_next = gamma_next / curvature
    loaded = loaded_ref[...]
    first = loaded * weights_ref[...]
    direction = grown * first - alpha * next_ref[...]
    along = grown * image_ref[...] - alpha * image_next
    solution_ref[...] = alpha * first + alpha_next * direction
    residual_ref[...] = loaded - alpha * image_ref[...] - alpha_next * along


def ring(
    loads,
    weights,
    dual_ops,
    corner_maps,
    coarse_inverse,
    corner_ids,
    iface_sizes,
    left_partner,
    right_partner,
):
    count = lax.axis_size("sub")
    sides = lax.axis_size("row")
    columns, half = loads.shape[1:]
    corners = corner_maps.shape[1]
    operator = dual_ops[0]
    own_map = corner_maps[0]
    loaded = loads[0]
    block = operator.shape[0]
    shape = jax.ShapeDtypeStruct
    grid = ("sub", "row")
    big = 2 * columns * block * 2 * half

    def pairs(target):
        listed = []
        for at in range(count):
            for side in range(sides):
                to_at, to_side = target(at, side)
                listed.append((at * sides + side, (to_at % count) * sides + to_side))
        return listed

    across = pairs(lambda at, side: (at, 1 - side))
    along = pairs(lambda at, side: (at - 1, 0) if side == 0 else (at + 1, 1))
    slant = pairs(lambda at, side: (at - 1, 1) if side == 0 else (at + 1, 0))

    def call(kernel, operands, outs, scratch=(), flops=0, moved=0, room=4):
        specs, placed = [], []
        for operand in operands:
            held = isinstance(operand, tuple)
            specs.append(HBM if held else VMEM)
            placed.append(
                pltpu.with_memory_space_constraint(operand[0], pltpu.HBM) if held else operand
            )
        return pl.pallas_call(
            kernel,
            in_specs=specs,
            out_specs=[VMEM] * len(outs),
            out_shape=[shape(*out) for out in outs],
            scratch_shapes=scratch,
            cost_estimate=cost(flops, moved),
            compiler_params=pltpu.CompilerParams(vmem_limit_bytes=room << 20),
        )(*placed)

    rows = columns + corners + 8
    arguments = (weights, corner_ids, coarse_inverse, right_partner, left_partner)
    pack, skew, load, live, scale, ids, inverse, right_map, left_map = call(
        open_kernel,
        [(array,) for array in (iface_sizes, loaded, own_map, *arguments)],
        [((rows, half), BF16), ((columns + 8, half), BF16)]
        + [((columns, half), F32), ((8, half), F32)]
        + [(array.shape, array.dtype) for array in arguments],
        scratch=[
            pltpu.SMEM(iface_sizes.shape, jnp.int32),
            pltpu.VMEM(loaded.shape, F32),
            pltpu.VMEM(own_map.shape, BF16),
            pltpu.SemaphoreType.DMA((8,)),
        ],
        moved=4 * rows * half,
    )
    pack_slant = lax.ppermute(skew, grid, slant)
    pack_along = lax.ppermute(pack, grid, along)
    map_across = lax.ppermute(own_map, grid, across)
    right_hot, order, left_hot, square, cross, early, local_left, turned = call(
        select_kernel,
        [right_map, left_map, pack, (operator,)],
        [((half, half), BF16)] * 3
        + [((block, half), BF16)] * 3
        + [((columns, block), F32), ((columns, half), BF16)],
        scratch=[pltpu.SemaphoreType.DMA((2,))],
        flops=big,
        moved=4 * half * half,
        room=16,
    )
    wide = half + 2 * LANES
    send, pair = call(
        first_kernel,
        [
            ids,
            square,
            early,
            right_hot,
            order,
            local_left,
            turned,
            pack,
            map_across,
            pack_along,
            pack_slant,
        ],
        [((columns, wide), BF16), ((columns, wide + half + half // 2), BF16)],
        flops=2 * big,
        moved=4 * block * half,
        room=16,
    )
    send_slant = lax.ppermute(send, grid, slant)
    send_along = lax.ppermute(send, grid, along)
    send_across = lax.ppermute(pair, grid, across)
    maps, solver, scale_right, names, late = call(
        order_kernel,
        [ids, inverse, order, left_hot, cross, pack, map_across, pack_along, pack_slant],
        [
            ((LANES, 2 * half), BF16),
            ((LANES, 4 * LANES), BF16),
            ((1, half), F32),
            ((LANES, LANES), BF16),
            ((half, block), BF16),
        ],
        flops=4 * corners * half * half,
        moved=4 * half * half,
        room=12,
    )
    image, following, up, small = call(
        second_kernel,
        [
            names,
            solver,
            maps,
            right_hot,
            order,
            square,
            early,
            late,
            live,
            load,
            scale,
            scale_right,
            send,
            send_across,
            send_along,
            send_slant,
        ],
        [
            ((columns, half), F32),
            ((columns, half), F32),
            ((columns, half + 2 * LANES), BF16),
            ((columns, LANES), F32),
        ],
        flops=2 * big,
        moved=4 * block * half,
        room=16,
    )
    far_in = shifted(small, "sub", 2)
    down_in = shifted(small, "sub", -1)
    up_in = shifted(up, "sub", 1)
    (mine,) = call(
        relay_kernel,
        [up, up_in, down_in, far_in, small],
        [((columns, half + 2 * LANES), BF16)],
        moved=8 * columns * half,
    )
    theirs = lax.ppermute(mine, grid, across)
    solution, residual = call(
        close_kernel,
        [solver, maps, live, load, scale, image, following, mine, theirs],
        [((columns, half), F32), ((columns, half), F32)],
        moved=24 * columns * half,
    )
    return solution[None], residual[None]


def per_device(*arrays):
    loads, _, dual_ops, corner_maps, coarse_inverse = arrays[:5]
    half = loads.shape[2]
    neighbourly = lax.axis_size("sub") == 4 and lax.axis_size("row") == 2
    sided = dual_ops.shape[1] == half and half % LANES == 0
    columns, corners = loads.shape[1], corner_maps.shape[1]
    fitting = columns % 16 == 0 and corners == columns + columns // 2 and corners == columns + 8
    narrow = coarse_inverse.shape[0] + 4 <= LANES and 3 * corner_maps.shape[1] <= LANES
    if neighbourly and sided and fitting and narrow and ITERS == 2:
        return ring(*arrays)
    return general(*arrays)


def solution(mesh):
    placed = (
        P(("parts", "sub"), "col", None),
        P(("parts", "sub"), None),
        P(("parts", "sub"), "row", None),
        P(("parts", "sub"), None, "row"),
        P("parts", None),
        P("parts", None),
        P("parts"),
        P(("parts", "sub"), None),
        P(("parts", "sub"), None),
    )
    return jax.shard_map(
        per_device,
        mesh=mesh,
        in_specs=placed,
        out_specs=(P(("parts", "sub"), "col", None), P(("parts", "sub"), "col", None)),
        check_vma=False,
    )
```
